256 devices in a mesh: bt: 16 (over y, x), freq: 16 (over z, core).
Axes of the slice: x: 4, y: 4, z: 8, core: 2. Of those that a mesh axis runs over, the one named last changes fastest.
Arguments:
- uv_grid: bfloat16 [16, 8, 1024, 1024], P('freq', None, 'bt'), may hold values from -6 to 6
- screens: bfloat16 [2, 256, 4, 1024], P(None, ('bt', 'freq')), may hold values from -6 to 6
- residual: bfloat16 [16, 1024, 8, 256], P('freq', 'bt'), may hold values from -0.033935547 to 0.033935547
- uv_coords: float32 [16, 1024, 2, 256], P('freq', 'bt'), may hold values from 0 to 32
- owner_tile: int32 [16, 1024, 1], P('freq', 'bt'), may hold values from 0 to 15; in each aligned block of 64 rows (0 to 63, 64 to 127, ..., all dimensions but the last counted through in order) at most 8 rows name the same one
- row_offset: int32 [16, 1024], P('freq', 'bt'), may hold values from 0 to 32
- column: int32 [16, 1024], P('freq', 'bt'), may hold values from 0 to 992
- stations: int32 [16, 1024, 2], P('freq', 'bt'), may hold values from 0 to 255
- time_slot: int32 [16, 1024], P('freq', 'bt'), may hold values from 0 to 1
Outputs:
- grid_grad: float32 [16, 8, 1024, 1024], P('freq', None, 'bt')
- screen_grad: float32 [2, 256, 4, 1024], P(None, ('bt', 'freq'))
The draws below stay inside these ranges and needn't reach their ends.
Inputs may be any that keep to these rules, and one draw needn't show every extreme that they name: Among the 64 subgrids of one device at most 8 have the same owner_tile, and in some device exactly 8 do.
All inputs are finite; a program needn't handle non-finite values.
Results may differ from the reference program's by a relative error of at most 0.0077.
Values may be sent and summed in bfloat16 or wider, within the bound.
No kernel may reach another device: no remote copies, remote signals or barrier semaphores. Data moves between devices by JAX's collectives and lax.ppermute only.
A program may use at most 128 MiB of HBM per device.

```python
import math
import jax
import jax.numpy as jnp
import numpy as np
from jax import lax

PIX = 32
VIS = 256
TR = 64
NCOLS = 1024
TSLOTS = 2
SUB_DEV = 64
FG = 16
SUBS = 1024
NROWS = 1024
STATIONS = 256
CAP = 8
N_BT = 16


def with_ends(drawn, stream_key, least, top_value):
    shape = drawn.shape
    index_at = [jax.random.randint(jax.random.fold_in(stream_key, axis), (), 0, shape[axis]) for axis in range(len(shape))]
    drawn = drawn.at[tuple(index_at)].set(least)
    longest = shape.index(max(shape))
    index_at[longest] = (index_at[longest] + 1) % shape[longest]
    return drawn.at[tuple(index_at)].set(top_value)


def steps_of(key, extent, cuts, smallest, top_value):
    level = 1.0
    for axis_at, shards_of in cuts:
        heights = jax.random.uniform(jax.random.fold_in(jax.random.fold_in(key, 6), axis_at), (shards_of,), jnp.float32, smallest / len(cuts), top_value / len(cuts))
        level = level * jnp.repeat(jnp.exp(heights), extent[axis_at] // shards_of).reshape((-1,) + (1,) * (len(extent) - 1 - axis_at))
    return level


def deal_out(key, own, number, rows, number_of, top, bound, lean):
    ranking = jax.random.permutation(key, number_of)
    heavy_load, ordinary = shares(number_of, rows * top, bound, lean, True), shares(number_of, rows * top, bound, lean, False)
    places = jnp.arange(number_of)

    def named(lengths, offset_by):
        used = int((lengths > 0).sum())
        fixed = max(1, used // 4)
        passed = fixed + (places - fixed + offset_by * (used - fixed)) % max(1, number_of - fixed)
        return jnp.zeros((number_of,), jnp.int32).at[ranking[jnp.where(places < fixed, places, passed)]].set(jnp.asarray(lengths, jnp.int32))

    lengths = jnp.where(number % 4 == 0, named(heavy_load, number // 4), named(ordinary, number - number // 4 - 1))
    mixed = jax.random.permutation(jax.random.fold_in(own, 3), number_of)
    donor, taker = mixed[0:number_of // 2 * 2:2], mixed[1:number_of // 2 * 2:2]
    margin = jnp.minimum(lengths[donor] - 1, bound - lengths[taker]) // 2
    margin = jnp.where((donor == ranking[0]) | (taker == ranking[0]) | (lengths[taker] == 0), 0, jnp.maximum(margin, 0))
    passed = jax.random.randint(jax.random.fold_in(own, 4), (number_of // 2,), 0, 1 << 20) % (margin + 1)
    lengths = lengths.at[donor].add(-passed).at[taker].add(passed)
    labels = jnp.searchsorted(jnp.cumsum(lengths), jnp.arange(rows * top), side="right").astype(jnp.int32)
    listing = labels.reshape(top, rows).T
    listing = listing[jax.random.permutation(jax.random.fold_in(own, 1), rows)]
    offset_by = jax.random.randint(jax.random.fold_in(own, 2), (rows, 1), 0, top)
    return jnp.take_along_axis(listing, (jnp.arange(top)[None, :] + offset_by) % top, axis=1)


def shares(amount, total, most, slope, full):
    loads = [(1 << 20) // math.isqrt(grade ** slope) + 1 for grade in range(1, amount + 1)]
    largest = most if full else min(most, max(-(-total // amount), total * loads[0] // sum(loads)))
    least = 1 if total - largest >= amount - 1 else 0
    counts, spare = [largest] + [least] * (amount - 1), total - largest - least * (amount - 1)
    while spare > 0:
        movable = [i for i in range(1, amount) if counts[i] < largest] or [i for i in range(1, amount) if counts[i] < most]
        mass, budget = sum([loads[i] for i in movable]), spare
        for i in movable:
            extra = min(most - counts[i], max(1, budget * loads[i] // mass), spare)
            counts[i] = counts[i] + extra
            spare = spare - extra
    return np.array(counts)


def noise(key, shape, deviation, bound, shards=(), kind=jnp.bfloat16):
    array = deviation * jax.random.normal(key, shape, jnp.float32)
    if shards:
        array = array * steps_of(key, shape, shards, -0.22, 0.18)
    return jnp.clip(array, -bound, bound).astype(kind)


def setup_inputs(seed: int = 0) -> dict:
    seeds = jax.random.split(jax.random.key(seed), 10)
    uv_grid = noise(seeds[0], (FG, 8, NROWS, NCOLS), 1.0, 6.0, ((0, 16), (2, 16)))
    screens = noise(seeds[1], (TSLOTS, STATIONS, 4, PIX * PIX), 1.0, 6.0, ((1, 256),))
    residual = noise(seeds[2], (FG, SUBS, 8, VIS), 0.0057, 0.033935547, ((0, 16), (1, 16)))
    uv_coords = jnp.clip(32.0 * jax.random.uniform(seeds[3], (FG, SUBS, 2, VIS), jnp.float32) ** steps_of(seeds[3], (FG, SUBS, 2, VIS), ((0, 16), (1, 16)), -0.2, 0.2), 0.0, 32.0)
    owner_tile_keys = jax.random.split(jax.random.fold_in(seeds[4], 1), FG * SUBS // SUB_DEV)
    owner_tile_turns = jax.random.permutation(jax.random.fold_in(seeds[4], 3), FG * SUBS // SUB_DEV)
    owner_tile = jax.vmap(lambda own, number: deal_out(jax.random.fold_in(seeds[4], 2), own, number, SUB_DEV, N_BT, 1, CAP, 2))(owner_tile_keys, owner_tile_turns).reshape((FG, SUBS, 1))
    row_offset = with_ends(jax.random.randint(seeds[5], (FG, SUBS), 0, TR - PIX + 1), jax.random.fold_in(seeds[5], 1), 0, TR - PIX).astype(jnp.int32)
    column = with_ends(jax.random.randint(seeds[6], (FG, SUBS), 0, NCOLS - PIX + 1), jax.random.fold_in(seeds[6], 1), 0, NCOLS - PIX).astype(jnp.int32)
    stations = with_ends(jax.random.randint(seeds[7], (FG, SUBS, 2), 0, STATIONS), jax.random.fold_in(seeds[7], 1), 0, STATIONS - 1).astype(jnp.int32)
    time_slot = with_ends(jax.random.randint(seeds[8], (FG, SUBS), 0, TSLOTS), jax.random.fold_in(seeds[8], 1), 0, TSLOTS - 1).astype(jnp.int32)
    return dict(uv_grid=uv_grid, screens=screens, residual=residual, uv_coords=uv_coords, owner_tile=owner_tile, row_offset=row_offset, column=column, stations=stations, time_slot=time_slot)


highest = lax.Precision.HIGHEST

def dft_tables(side_len):
    ramp = jnp.arange(side_len, dtype=jnp.int32)
    product_index = ramp[:, None] * ramp[None, :] % side_len
    angle = product_index.astype(jnp.float32) * (2.0 * math.pi / side_len)
    norm_factor = 1.0 / math.sqrt(side_len)
    cos_part = (jnp.cos(angle) * norm_factor).astype(jnp.bfloat16).astype(jnp.float32)
    sin_part = (jnp.sin(angle) * norm_factor).astype(jnp.bfloat16).astype(jnp.float32)
    return (cos_part, sin_part)

def subgrid_terms(patches, vis_rows, uv_rows, screen_p, screen_q, cos_table, sin_table):
    batch_size = vis_rows.shape[0]
    side_len = cos_table.shape[0]
    pixels = side_len * side_len
    samples = vis_rows.shape[2]
    positions = jnp.arange(side_len, dtype=jnp.int32).astype(jnp.float32)
    phase_x = 2.0 * math.pi / side_len * positions[None, :, None] * uv_rows[:, 0:1, :]
    phase_y = 2.0 * math.pi / side_len * positions[None, :, None] * uv_rows[:, 1:2, :]
    wave_x = jnp.stack([jnp.cos(phase_x), jnp.sin(phase_x)], 1).astype(jnp.bfloat16)
    wave_y = jnp.stack([jnp.cos(phase_y), jnp.sin(phase_y)], 1).astype(jnp.bfloat16)
    wave_y = lax.optimization_barrier(wave_y)
    vis_f32 = vis_rows.astype(jnp.float32).reshape(batch_size, 2, 4, 1, samples)
    wave_f32 = wave_y.astype(jnp.float32)[:, :, None, :, :]
    weight_re = vis_f32[:, 0] * wave_f32[:, 0] - vis_f32[:, 1] * wave_f32[:, 1]
    weight_im = vis_f32[:, 0] * wave_f32[:, 1] + vis_f32[:, 1] * wave_f32[:, 0]
    weighted = jnp.stack([weight_re, weight_im], 1).astype(jnp.bfloat16)
    products = jnp.einsum('baxk,bpcyk->bapcxy', wave_x.astype(jnp.float32), weighted.astype(jnp.float32), precision=highest)
    adj_re = (products[:, 0, 0] - products[:, 1, 1]).reshape(batch_size, 4, pixels)
    adj_im = (products[:, 0, 1] + products[:, 1, 0]).reshape(batch_size, 4, pixels)
    grid_re = patches[0:4].astype(jnp.float32).reshape(4, batch_size, side_len, side_len)
    grid_im = patches[4:8].astype(jnp.float32).reshape(4, batch_size, side_len, side_len)

    def rounded(values):
        return values.astype(jnp.bfloat16).astype(jnp.float32)

    def first_left(table, values):
        return jnp.einsum('xu,cbuv->bcxv', table, values, precision=highest)

    def first_right(values, table):
        return jnp.einsum('bcxv,yv->bcxy', values, table, precision=highest)

    def back_left(table, values):
        return jnp.einsum('xu,bcxy->bcuy', table, values, precision=highest)

    def back_right(values, table):
        return jnp.einsum('bcuy,yv->cbuv', values, table, precision=highest)
    mid_re = rounded(first_left(cos_table, grid_re) - first_left(sin_table, grid_im))
    mid_im = rounded(first_left(cos_table, grid_im) + first_left(sin_table, grid_re))
    sky_re = (first_right(mid_re, cos_table) - first_right(mid_im, sin_table)).reshape(batch_size, 4, pixels)
    sky_im = (first_right(mid_re, sin_table) + first_right(mid_im, cos_table)).reshape(batch_size, 4, pixels)
    scr_first = screen_p.astype(jnp.float32)
    scr_second = screen_q.astype(jnp.float32)
    first_re = jnp.repeat(scr_first[:, 0:2], 2, axis=1)
    first_im = jnp.repeat(scr_first[:, 2:4], 2, axis=1)
    second_re = jnp.tile(scr_second[:, 0:2], (1, 2, 1))
    second_im = jnp.tile(scr_second[:, 2:4], (1, 2, 1))
    both_re = first_re * second_re + first_im * second_im
    both_im = first_re * second_im - first_im * second_re
    back_re = rounded(both_re * adj_re - both_im * adj_im).reshape(batch_size, 4, side_len, side_len)
    back_im = rounded(both_re * adj_im + both_im * adj_re).reshape(batch_size, 4, side_len, side_len)
    carry_re = second_re * adj_re - second_im * adj_im
    carry_im = second_re * adj_im + second_im * adj_re
    grad_first_re = (sky_re * carry_re + sky_im * carry_im).reshape(batch_size, 2, 2, pixels).sum(2)
    grad_first_im = (sky_re * carry_im - sky_im * carry_re).reshape(batch_size, 2, 2, pixels).sum(2)
    model_re = first_re * sky_re - first_im * sky_im
    model_im = first_re * sky_im + first_im * sky_re
    grad_second_re = (adj_re * model_re + adj_im * model_im).reshape(batch_size, 2, 2, pixels).sum(1)
    grad_second_im = (adj_re * model_im - adj_im * model_re).reshape(batch_size, 2, 2, pixels).sum(1)
    low_re = rounded(back_left(cos_table, back_re) + back_left(sin_table, back_im))
    low_im = rounded(back_left(cos_table, back_im) - back_left(sin_table, back_re))
    out_re = back_right(low_re, cos_table) + back_right(low_im, sin_table)
    out_im = back_right(low_im, cos_table) - back_right(low_re, sin_table)
    patch_grad = jnp.concatenate([out_re, out_im], 0).reshape(8, batch_size, pixels).astype(jnp.bfloat16)
    grad_first = jnp.concatenate([grad_first_re, grad_first_im], 1)
    grad_second = jnp.concatenate([grad_second_re, grad_second_im], 1)
    return (patch_grad, grad_first, grad_second)

def reference(uv_grid, screens, residual, uv_coords, owner_tile, row_offset, column, stations, time_slot):
    ncols_all = uv_grid.shape[3]
    nrows_all = uv_grid.shape[2]
    pixels = PIX * PIX
    cos_table, sin_table = dft_tables(PIX)
    tables = screens.reshape(TSLOTS * STATIONS, 4, pixels)
    positions = jnp.arange(PIX, dtype=jnp.int32)
    blocks = SUBS // 8

    def one_group(inputs):
        group_grid, group_res, group_uv, group_tile, group_off, group_col, group_st, group_slot = inputs
        flat_grid = group_grid.reshape(8, nrows_all * ncols_all)
        row_start = group_tile[:, 0] * TR + group_off
        cell_index = ((row_start[:, None, None] + positions[None, :, None]) * ncols_all + group_col[:, None, None] + positions[None, None, :]).reshape(SUBS, pixels)
        first_row = group_slot * STATIONS + group_st[:, 0]
        second_row = group_slot * STATIONS + group_st[:, 1]

        def scan_step(state, block_in):
            grad_acc, screen_acc = state
            block_cells, block_res, block_uv, block_first, block_second = block_in
            patches = jnp.take(flat_grid, block_cells, axis=1)
            patch_grad, grad_first, grad_second = subgrid_terms(patches, block_res, block_uv, tables[block_first], tables[block_second], cos_table, sin_table)
            grad_acc = grad_acc.at[:, block_cells].add(patch_grad.astype(jnp.float32))
            screen_acc = screen_acc.at[block_first].add(grad_first).at[block_second].add(grad_second)
            return ((grad_acc, screen_acc), None)
        block_inputs = (cell_index.reshape(blocks, 8, pixels), group_res.reshape(blocks, 8, 8, VIS), group_uv.reshape(blocks, 8, 2, VIS), first_row.reshape(blocks, 8), second_row.reshape(blocks, 8))
        start_state = (jnp.zeros((8, nrows_all * ncols_all), jnp.float32), jnp.zeros((TSLOTS * STATIONS, 4, pixels), jnp.float32))
        (grad_acc, screen_acc), _ = lax.scan(scan_step, start_state, block_inputs)
        return (grad_acc.reshape(8, nrows_all, ncols_all), screen_acc)
    grid_grads, screen_parts = lax.map(one_group, (uv_grid, residual, uv_coords, owner_tile, row_offset, column, stations, time_slot))
    screen_grad = lax.optimization_barrier(jnp.sum(screen_parts, axis=0)).reshape(TSLOTS, STATIONS, 4, pixels)
    return (grid_grads, screen_grad)
```

```python
import math

import jax
import jax.numpy as jnp
import numpy as np
from jax import lax
from jax.experimental import pallas as pl
from jax.experimental.pallas import tpu as pltpu
from jax.sharding import PartitionSpec as P

PIX = 32
TSLOTS = 2
COMPS = 8
LANES = 128
CAP = 8
F32 = jnp.float32
BF16 = jnp.bfloat16


def constant_tables():
    ramp = np.arange(PIX)
    angle = (ramp[:, None] * ramp[None, :] % PIX) * (2.0 * math.pi / PIX)
    cos_part = (np.cos(angle) / math.sqrt(PIX)).astype(np.float32)
    sin_part = (np.sin(angle) / math.sqrt(PIX)).astype(np.float32)
    forward = np.block([[cos_part, -sin_part], [sin_part, cos_part]])
    backward = np.block([[cos_part, sin_part], [-sin_part, cos_part]])
    eye = np.eye(4, dtype=np.float32)
    right = np.concatenate([np.kron(eye, cos_part), np.kron(eye, sin_part)], 1)
    block = np.eye(PIX, dtype=np.float32)

    def spread(picks):
        out = np.zeros((LANES, len(picks) * PIX), np.float32)
        for j, i in enumerate(picks):
            out[i * PIX : (i + 1) * PIX, j * PIX : (j + 1) * PIX] = block
        return out

    spread_first = spread([0, 0, 1, 1, 2, 2, 3, 3])
    spread_second = spread([0, 1, 0, 1, 2, 3, 2, 3])
    as_bf16 = [
        jnp.asarray(v, BF16) for v in (forward, backward, right, spread_first, spread_second)
    ]
    return as_bf16


def dot(a, b):
    return jnp.dot(a, b, preferred_element_type=F32)


def route_kernel(owner, row_offset, column, station_a, station_b, slot_time, request, slot, first, second, fill):
    count = owner.shape[0]

    def clear(i, carry):
        request[i] = -1
        return carry

    lax.fori_loop(0, request.shape[0], clear, 0)

    def zero(i, carry):
        fill[i] = 0
        return carry

    lax.fori_loop(0, fill.shape[0], zero, 0)

    def step(s, carry):
        o = owner[s]
        place = o * CAP + fill[o]
        fill[o] = fill[o] + 1
        slot[s] = place
        request[place] = row_offset[s] * 1024 + column[s]
        first[s] = station_a[s] * TSLOTS + slot_time[s]
        second[s] = station_b[s] * TSLOTS + slot_time[s]
        return carry

    lax.fori_loop(0, count, step, 0)


def route(owners, row_offset, column, station_a, station_b, slot_time, n_owners):
    count = owners.shape[0]
    smem = pl.BlockSpec(memory_space=pltpu.SMEM)
    ints = lambda n: jax.ShapeDtypeStruct((n,), jnp.int32)
    return pl.pallas_call(
        route_kernel,
        out_shape=(ints(n_owners * CAP), ints(count), ints(count), ints(count)),
        in_specs=[smem] * 6,
        out_specs=(smem,) * 4,
        scratch_shapes=[pltpu.SMEM((n_owners,), jnp.int32)],
        name="route",
    )(owners, row_offset, column, station_a, station_b, slot_time)


def listed(asked, order):
    def step(i, n):
        order[n] = i
        return n + (asked[i] >= 0).astype(jnp.int32)

    return lax.fori_loop(0, asked.shape[0], step, jnp.int32(0))


def for_listed(n, group, body):
    def whole(g, carry):
        body([g * group + k for k in range(group)])
        return carry

    lax.fori_loop(0, n // group, whole, 0)

    def rest(i, carry):
        body([i])
        return carry

    lax.fori_loop(n // group * group, n, rest, 0)


def cut_kernel(asked, tile, out, wide, order):
    comps, rows, columns = tile.shape
    panels = columns // LANES
    for j in range(panels):
        wide[j] = tile[:, :, j * LANES : (j + 1) * LANES].astype(F32).reshape(comps * rows, LANES)
    n = listed(asked, order)
    line = lax.broadcasted_iota(jnp.int32, (LANES, LANES), 0)
    lane = lax.broadcasted_iota(jnp.int32, (LANES, LANES), 1)
    ahead = line - lane % PIX
    block = lax.broadcasted_iota(jnp.int32, (PIX, LANES), 1) // PIX

    def body(places):
        for place in places:
            i = order[place]
            code = asked[i]
            r, c0 = code // 1024, code % 1024
            j, shift = c0 // LANES, c0 % LANES
            after = jnp.minimum(j + 1, panels - 1)

            def rows_of(panel):
                return jnp.concatenate(
                    [wide[panel, pl.ds(c * rows + r, PIX), :] for c in range(comps)], 0
                ).astype(BF16)

            both = jnp.concatenate([rows_of(j), rows_of(after)], 1)
            pick = jnp.concatenate([ahead == shift, ahead + LANES == shift], 0)
            moved = dot(both, jnp.where(pick, 1.0, 0.0).astype(BF16))
            parts = []
            for ri in range(2):
                part = moved[ri * 128 : ri * 128 + PIX]
                for m in range(1, 4):
                    start = (ri * 4 + m) * PIX
                    part = jnp.where(block == m, moved[start : start + PIX], part)
                parts.append(part)
            out[i] = jnp.concatenate(parts, 0).astype(BF16)

    for_listed(n, 4, body)


def cut_windows(asked, tile):
    comps, rows, columns = tile.shape
    slots = asked.shape[0]
    return pl.pallas_call(
        cut_kernel,
        out_shape=jax.ShapeDtypeStruct((slots, 2 * PIX, LANES), BF16),
        in_specs=[pl.BlockSpec(memory_space=pltpu.SMEM), pl.BlockSpec(memory_space=pltpu.VMEM)],
        out_specs=pl.BlockSpec(memory_space=pltpu.VMEM),
        scratch_shapes=[
            pltpu.VMEM((columns // LANES, comps * rows, LANES), F32),
            pltpu.SMEM((slots + 1,), jnp.int32),
        ],
        name="cut",
    )(asked, tile)


def add_kernel(asked, pieces, out, wide, order):
    comps, rows, columns = out.shape
    panels = columns // LANES
    for j in range(panels):
        wide[j] = jnp.zeros((comps * rows, LANES), F32)
    n = listed(asked, order)
    line = lax.broadcasted_iota(jnp.int32, (LANES, LANES), 0)
    lane = lax.broadcasted_iota(jnp.int32, (LANES, LANES), 1)
    ahead = lane - line % PIX
    block = lax.broadcasted_iota(jnp.int32, (PIX, LANES), 1) // PIX

    def body(places):
        spread = []
        for place in places:
            i = order[place]
            code = asked[i]
            r, c0 = code // 1024, code % 1024
            j, shift = c0 // LANES, c0 % LANES
            piece = pieces[i].astype(F32)
            lines = []
            for ri in range(2):
                for m in range(4):
                    lines.append(jnp.where(block == m, piece[ri * PIX : (ri + 1) * PIX], 0.0))
            lines = jnp.concatenate(lines, 0).astype(BF16)
            moved = dot(lines, jnp.where(ahead == shift, 1.0, 0.0).astype(BF16))
            spread.append((r, j, shift, lines, moved))
        for r, j, shift, lines, moved in spread:
            for c in range(comps):
                at = pl.ds(c * rows + r, PIX)
                wide[j, at, :] = wide[j, at, :] + moved[c * PIX : (c + 1) * PIX]
        for r, j, shift, lines, moved in spread:

            @pl.when(shift > LANES - PIX)
            def _(r=r, j=j, shift=shift, lines=lines):
                over = dot(lines, jnp.where(ahead + LANES == shift, 1.0, 0.0).astype(BF16))
                for c in range(comps):
                    at = pl.ds(c * rows + r, PIX)
                    wide[j + 1, at, :] = wide[j + 1, at, :] + over[c * PIX : (c + 1) * PIX]

    for_listed(n, 4, body)
    for j in range(panels):
        out[:, :, j * LANES : (j + 1) * LANES] = wide[j].reshape(comps, rows, LANES)


def add_windows(asked, pieces, comps, rows, columns):
    slots = asked.shape[0]
    return pl.pallas_call(
        add_kernel,
        out_shape=jax.ShapeDtypeStruct((comps, rows, columns), F32),
        in_specs=[pl.BlockSpec(memory_space=pltpu.SMEM), pl.BlockSpec(memory_space=pltpu.VMEM)],
        out_specs=pl.BlockSpec(memory_space=pltpu.VMEM),
        scratch_shapes=[
            pltpu.VMEM((columns // LANES, comps * rows, LANES), F32),
            pltpu.SMEM((slots + 1,), jnp.int32),
        ],
        name="add",
    )(asked, pieces)


def turn_waves(turns):
    part = turns - jnp.round(turns)
    z = part * part
    coef_sin = [(-1.0) ** k * math.pi ** (2 * k + 1) / math.factorial(2 * k + 1) for k in range(7)]
    coef_cos = [(-1.0) ** k * math.pi ** (2 * k) / math.factorial(2 * k) for k in range(8)]
    s = jnp.full_like(z, coef_sin[-1])
    for v in coef_sin[-2::-1]:
        s = s * z + v
    s = s * part
    c = jnp.full_like(z, coef_cos[-1])
    for v in coef_cos[-2::-1]:
        c = c * z + v
    return 1.0 - 2.0 * s * s, 2.0 * s * c


def image_kernel(group, vis, uv, out):
    samples = vis.shape[2]
    position = lax.broadcasted_iota(jnp.int32, (PIX, samples), 0).astype(F32) * (1.0 / PIX)

    def step(g, carry):
        for k in range(group):
            s = g * group + k
            uv_rows = uv[s]
            x_cos, x_sin = turn_waves(position * uv_rows[0:1])
            y_cos, y_sin = turn_waves(position * uv_rows[1:2])
            wave_x = jnp.concatenate([x_cos, x_sin], 0).astype(BF16)
            y_cos, y_sin = y_cos.astype(BF16).astype(F32), y_sin.astype(BF16).astype(F32)
            rows = vis[s].astype(F32)
            weight_re, weight_im = [], []
            for m in range(4):
                re, im = rows[m : m + 1], rows[m + 4 : m + 5]
                weight_re.append(re * y_cos - im * y_sin)
                weight_im.append(re * y_sin + im * y_cos)
            weighted = jnp.concatenate(weight_re + weight_im, 0).astype(BF16)
            products = lax.dot_general(
                wave_x, weighted, (((1,), (1,)), ((), ())), preferred_element_type=F32
            )
            low, high = products[:PIX], products[PIX:]
            out[s, 0:PIX] = low[:, :LANES] - high[:, LANES:]
            out[s, PIX:] = low[:, LANES:] + high[:, :LANES]
        return carry

    lax.fori_loop(0, vis.shape[0] // group, step, 0)


def adjoint_images(vis, uv):
    count = vis.shape[0]
    group = math.gcd(count, 4)
    vmem = pl.BlockSpec(memory_space=pltpu.VMEM)
    return pl.pallas_call(
        lambda *refs: image_kernel(group, *refs),
        out_shape=jax.ShapeDtypeStruct((count, 2 * PIX, LANES), F32),
        in_specs=[vmem, vmem],
        out_specs=vmem,
        name="image",
    )(vis, uv)


def screens_of(table, row, spread):
    wide = dot(table[row], spread[...])
    return wide[:, :LANES], wide[:, LANES:]


def patch_kernel(group, slot, first, second, image, table, backward, right, spread_a, spread_b, out):
    def step(g, carry):
        for k in range(group):
            s = g * group + k
            a_re, a_im = screens_of(table, first[s], spread_a)
            b_re, b_im = screens_of(table, second[s], spread_b)
            m_re, m_im = image[s, 0:PIX], image[s, PIX:]
            both_re = a_re * b_re + a_im * b_im
            both_im = a_re * b_im - a_im * b_re
            back_re = both_re * m_re - both_im * m_im
            back_im = both_re * m_im + both_im * m_re
            back = jnp.concatenate([back_re, back_im], 0).astype(BF16)
            low = dot(backward[...], back).astype(BF16)
            grad = dot(low, right[...])
            re, im = grad[:PIX], grad[PIX:]
            grad_re = re[:, :LANES] + im[:, LANES:]
            grad_im = im[:, :LANES] - re[:, LANES:]
            out[slot[s]] = jnp.concatenate([grad_re, grad_im], 0).astype(BF16)
        return carry

    lax.fori_loop(0, image.shape[0] // group, step, 0)


def patch_gradients(slot, first, second, image, table, consts, slots):
    forward, backward, right, spread_a, spread_b = consts
    group = math.gcd(image.shape[0], 4)
    vmem, smem = pl.BlockSpec(memory_space=pltpu.VMEM), pl.BlockSpec(memory_space=pltpu.SMEM)
    return pl.pallas_call(
        lambda *refs: patch_kernel(group, *refs),
        out_shape=jax.ShapeDtypeStruct((slots, 2 * PIX, LANES), BF16),
        in_specs=[smem] * 3 + [vmem] * 6,
        out_specs=vmem,
        name="patch",
    )(slot, first, second, image, table, backward, right, spread_a, spread_b)


def screen_kernel(group, slot, first, second, image, patches, table, forward, right, spread_a, spread_b, out, acc):
    chunk = 32

    def clear(i, carry):
        acc[pl.ds(i * chunk, chunk)] = jnp.zeros((chunk, PIX, LANES), F32)
        return carry

    lax.fori_loop(0, acc.shape[0] // chunk, clear, 0)
    block = lax.broadcasted_iota(jnp.int32, (PIX, LANES), 1) // PIX

    def step(g, carry):
        terms = []
        for k in range(group):
            s = g * group + k
            a_re, a_im = screens_of(table, first[s], spread_a)
            b_re, b_im = screens_of(table, second[s], spread_b)
            m_re, m_im = image[s, 0:PIX], image[s, PIX:]
            mid = dot(forward[...], patches[slot[s]]).astype(BF16)
            wide = dot(mid, right[...])
            re, im = wide[:PIX], wide[PIX:]
            sky_re = re[:, :LANES] - im[:, LANES:]
            sky_im = re[:, LANES:] + im[:, :LANES]
            carry_re = b_re * m_re - b_im * m_im
            carry_im = b_re * m_im + b_im * m_re
            ga_re = sky_re * carry_re + sky_im * carry_im
            ga_im = sky_re * carry_im - sky_im * carry_re
            model_re = a_re * sky_re - a_im * sky_im
            model_im = a_re * sky_im + a_im * sky_re
            gb_re = m_re * model_re + m_im * model_im
            gb_im = m_re * model_im - m_im * model_re
            ta = jnp.where(
                block % 2 == 0,
                ga_re + pltpu.roll(ga_re, LANES - PIX, 1),
                ga_im + pltpu.roll(ga_im, PIX, 1),
            )
            ta = jnp.where(
                block == 1,
                pltpu.roll(ta, LANES - PIX, 1),
                jnp.where(block == 2, pltpu.roll(ta, PIX, 1), ta),
            )
            tb = jnp.where(
                block < 2,
                gb_re + pltpu.roll(gb_re, 2 * PIX, 1),
                gb_im + pltpu.roll(gb_im, 2 * PIX, 1),
            )
            terms.append((s, ta, tb))
        for s, ta, tb in terms:
            acc[first[s]] = acc[first[s]] + ta
            acc[second[s]] = acc[second[s]] + tb
        return carry

    lax.fori_loop(0, image.shape[0] // group, step, 0)

    def give(i, carry):
        at = pl.ds(i * chunk, chunk)
        out[at] = acc[at].astype(BF16)
        return carry

    lax.fori_loop(0, acc.shape[0] // chunk, give, 0)


def screen_gradients(slot, first, second, image, patches, table, consts):
    forward, backward, right, spread_a, spread_b = consts
    group = math.gcd(image.shape[0], 4)
    vmem, smem = pl.BlockSpec(memory_space=pltpu.VMEM), pl.BlockSpec(memory_space=pltpu.SMEM)
    return pl.pallas_call(
        lambda *refs: screen_kernel(group, *refs),
        out_shape=jax.ShapeDtypeStruct(table.shape, BF16),
        in_specs=[smem] * 3 + [vmem] * 7,
        out_specs=vmem,
        scratch_shapes=[pltpu.VMEM(table.shape, F32)],
        name="screen",
    )(slot, first, second, image, patches, table, forward, right, spread_a, spread_b)


def exchange(x, axis):
    return lax.all_to_all(x, axis, split_axis=0, concat_axis=0, tiled=True)


def per_device(
    uv_grid, screens, residual, uv_coords, owner_tile, row_offset, column, stations, time_slot
):
    n_bt, n_freq = lax.axis_size("bt"), lax.axis_size("freq")
    slots = n_bt * CAP
    consts = constant_tables()
    held = screens.shape[1]
    own = screens.reshape(TSLOTS, held, 4, PIX, PIX).transpose(1, 0, 3, 2, 4)
    own = own.reshape(held, TSLOTS, PIX, LANES)
    table = lax.all_gather(own, "freq", axis=0, tiled=True)
    table = lax.all_gather(table, "bt", axis=0, tiled=True)
    table = table.reshape(-1, PIX, LANES)
    request, slot, first, second = route(
        owner_tile[0, :, 0],
        row_offset[0],
        column[0],
        stations[0, :, 0],
        stations[0, :, 1],
        time_slot[0],
        n_bt,
    )
    asked = exchange(request.reshape(n_bt, CAP), "bt").reshape(slots)
    image = adjoint_images(residual[0], uv_coords[0])
    cut = cut_windows(asked, uv_grid[0])
    fetched = exchange(cut.reshape(n_bt, CAP, 2 * PIX, LANES), "bt").reshape(slots, 2 * PIX, LANES)
    grads = patch_gradients(slot, first, second, image, table, consts, slots)
    returned = exchange(grads.reshape(n_bt, CAP, 2 * PIX, LANES), "bt").reshape(slots, 2 * PIX, LANES)
    terms = screen_gradients(slot, first, second, image, fetched, table, consts)
    grid_grad = add_windows(asked, returned, *uv_grid.shape[1:])
    part = exchange(terms.reshape(n_bt, -1, TSLOTS, PIX, LANES), "bt")
    part = jnp.sum(part.astype(F32), 0).astype(BF16)
    part = exchange(part.reshape(n_freq, held, TSLOTS, PIX, LANES), "freq")
    part = jnp.sum(part.astype(F32), 0).reshape(held, TSLOTS, PIX, 4, PIX)
    screen_grad = part.transpose(1, 0, 3, 2, 4).reshape(TSLOTS, held, 4, PIX * PIX)
    return grid_grad[None], screen_grad


def solution(mesh):
    in_specs = (
        P("freq", None, "bt", None),
        P(None, ("bt", "freq"), None, None),
        P("freq", "bt", None, None),
        P("freq", "bt", None, None),
        P("freq", "bt", None),
        P("freq", "bt"),
        P("freq", "bt"),
        P("freq", "bt", None),
        P("freq", "bt"),
    )
    out_specs = (P("freq", None, "bt", None), P(None, ("bt", "freq"), None, None))
    return jax.shard_map(
        per_device, mesh=mesh, in_specs=in_specs, out_specs=out_specs, check_vma=False
    )
```

```python
import math

import jax
import jax.numpy as jnp
import numpy as np
from jax import lax
from jax.experimental import pallas as pl
from jax.experimental.pallas import tpu as pltpu
from jax.sharding import PartitionSpec as P


PIX = 32
TSLOTS = 2
LANES = 128
CAP = 8
F32 = jnp.float32
BF16 = jnp.bfloat16


def constant_tables():
    ramp = np.arange(PIX)
    angle = (ramp[:, None] * ramp[None, :] % PIX) * (2.0 * math.pi / PIX)
    cos_part = (np.cos(angle) / math.sqrt(PIX)).astype(np.float32)
    sin_part = (np.sin(angle) / math.sqrt(PIX)).astype(np.float32)
    forward = np.block([[cos_part, -sin_part], [sin_part, cos_part]])
    backward = np.block([[cos_part, sin_part], [-sin_part, cos_part]])
    eye = np.eye(4, dtype=np.float32)
    right = np.concatenate([np.kron(eye, cos_part), np.kron(eye, sin_part)], 1)
    block = np.eye(PIX, dtype=np.float32)

    def spread(picks):
        out = np.zeros((LANES, len(picks) * PIX), np.float32)
        for j, i in enumerate(picks):
            out[i * PIX : (i + 1) * PIX, j * PIX : (j + 1) * PIX] = block
        return out

    spread_first = spread([0, 0, 1, 1, 2, 2, 3, 3])
    spread_second = spread([0, 1, 0, 1, 2, 3, 2, 3])
    as_bf16 = [
        jnp.asarray(v, BF16) for v in (forward, backward, right, spread_first, spread_second)
    ]
    return as_bf16


def dot(a, b):
    return jnp.dot(a, b, preferred_element_type=F32)


def swap_blocks(x):
    rolled = [x] + [pltpu.roll(x, d * PIX, 1) for d in (1, 2, 3)]
    line = lax.broadcasted_iota(jnp.int32, x.shape, 0)
    block = lax.broadcasted_iota(jnp.int32, x.shape, 1) // PIX
    rows = []
    for a in range(4):
        d = (block - a + 4) % 4
        moved = rolled[0]
        for k in (1, 2, 3):
            moved = jnp.where(d == k, rolled[k], moved)
        rows.append(jnp.sum(jnp.where(block == line, moved, 0.0), 0, keepdims=True))
    return rows


def mail_kernel(
    n_bt, n_freq, me, owner, row_offset, column, stations, slot_time, screens,
    mail, slot, first, second, first_sum, second_sum, fill, request, own,
):
    count = owner.shape[0]
    n_z = n_freq // 2
    my_z, my_core = me[0] // 2, me[0] % 2

    def clear(i, carry):
        request[i] = -1
        return carry

    lax.fori_loop(0, n_bt * CAP, clear, 0)

    def zero(i, carry):
        fill[i] = 0
        return carry

    lax.fori_loop(0, n_bt, zero, 0)

    def rows(station, t):
        bt, freq = station // n_freq, station % n_freq
        z, core = freq // 2, freq % 2
        half = jnp.where(core == my_core, 0, n_bt * n_z)
        ahead = (z - my_z + n_z) % n_z
        return (half + ahead * n_bt + bt) * TSLOTS + t, (half + bt * n_z + z) * TSLOTS + t

    def step(s, carry):
        o = owner[s]
        place = o * CAP + fill[o]
        fill[o] = fill[o] + 1
        slot[s] = place
        request[place] = row_offset[s] * 1024 + column[s]
        first[s], first_sum[s] = rows(stations[s * 2], slot_time[s])
        second[s], second_sum[s] = rows(stations[s * 2 + 1], slot_time[s])
        return carry

    lax.fori_loop(0, count, step, 0)
    for t in range(TSLOTS):
        table = screens[t].astype(F32)
        for high in range(PIX // 4):
            for a, line in enumerate(swap_blocks(table[:, high * LANES : (high + 1) * LANES])):
                x = t * PIX + high * 4 + a
                own[x : x + 1] = line
    every = own[...].astype(BF16)
    lane = lax.broadcasted_iota(jnp.int32, (16, LANES), 1)

    def address(j, carry):
        line = jnp.full((16, LANES), -1, jnp.int32)
        for k in range(CAP):
            code = request[j * CAP + k]
            for part, value in enumerate((code >> 10, (code >> 5) & 31, code & 31)):
                line = jnp.where(lane == part * CAP + k, value, line)
        mail[j] = jnp.concatenate([every, line.astype(F32).astype(BF16)], 0)
        return carry

    lax.fori_loop(0, n_bt, address, 0)


def make_mail(me, owners, row_offset, column, stations, slot_time, screens, n_bt, n_freq):
    count = owners.shape[0]
    smem, vmem = pl.BlockSpec(memory_space=pltpu.SMEM), pl.BlockSpec(memory_space=pltpu.VMEM)
    ints = jax.ShapeDtypeStruct((count,), jnp.int32)
    rows = TSLOTS * PIX
    return pl.pallas_call(
        lambda *refs: mail_kernel(n_bt, n_freq, *refs),
        out_shape=(jax.ShapeDtypeStruct((n_bt, rows + 16, LANES), BF16),) + (ints,) * 5,
        in_specs=[smem] * 6 + [vmem],
        out_specs=(vmem,) + (smem,) * 5,
        scratch_shapes=[
            pltpu.SMEM((n_bt,), jnp.int32),
            pltpu.SMEM((n_bt * CAP,), jnp.int32),
            pltpu.VMEM((rows, LANES), F32),
        ],
        name="mail",
    )(me, owners, row_offset, column, stations, slot_time, screens)


def finish_kernel(parts, out):
    total = jnp.sum(parts[...].astype(F32), 0)
    line = lax.broadcasted_iota(jnp.int32, (4, LANES), 0)
    for t in range(TSLOTS):
        for high in range(PIX // 4):
            rows = swap_blocks(total[t, high * 4 : high * 4 + 4])
            tile = jnp.broadcast_to(rows[0], (4, LANES))
            for a in (1, 2, 3):
                tile = jnp.where(line == a, jnp.broadcast_to(rows[a], (4, LANES)), tile)
            out[t, :, high * LANES : (high + 1) * LANES] = tile


def finish(parts):
    vmem = pl.BlockSpec(memory_space=pltpu.VMEM)
    return pl.pallas_call(
        finish_kernel,
        out_shape=jax.ShapeDtypeStruct((TSLOTS, 4, PIX * PIX), F32),
        in_specs=[vmem],
        out_specs=vmem,
        name="finish",
    )(parts)


def listed(asked, order):
    def step(i, n):
        order[n] = i
        return n + (asked[i // CAP, i % CAP] >= 0).astype(jnp.int32)

    return lax.fori_loop(0, asked.shape[0] * CAP, step, jnp.int32(0))


def corner(asked, i):
    j, k = i // CAP, i % CAP
    return asked[j, k], asked[j, CAP + k] * PIX + asked[j, 2 * CAP + k]


def for_listed(n, group, body):
    def whole(g, carry):
        body([g * group + k for k in range(group)])
        return carry

    lax.fori_loop(0, n // group, whole, 0)

    def rest(i, carry):
        body([i])
        return carry

    lax.fori_loop(n // group * group, n, rest, 0)


def cut_kernel(asked, tile, out, wide, order):
    comps, rows, columns = tile.shape
    panels = columns // LANES
    for j in range(panels):
        wide[j] = tile[:, :, j * LANES : (j + 1) * LANES].astype(F32).reshape(comps * rows, LANES)
    n = listed(asked, order)
    line = lax.broadcasted_iota(jnp.int32, (LANES, LANES), 0)
    lane = lax.broadcasted_iota(jnp.int32, (LANES, LANES), 1)
    ahead = line - lane % PIX
    block = lax.broadcasted_iota(jnp.int32, (PIX, LANES), 1) // PIX

    def body(places):
        for place in places:
            i = order[place]
            r, c0 = corner(asked, i)
            j, shift = c0 // LANES, c0 % LANES
            after = jnp.minimum(j + 1, panels - 1)

            def rows_of(panel):
                return jnp.concatenate(
                    [wide[panel, pl.ds(c * rows + r, PIX), :] for c in range(comps)], 0
                ).astype(BF16)

            both = jnp.concatenate([rows_of(j), rows_of(after)], 1)
            pick = jnp.concatenate([ahead == shift, ahead + LANES == shift], 0)
            moved = dot(both, jnp.where(pick, 1.0, 0.0).astype(BF16))
            parts = []
            for ri in range(2):
                part = moved[ri * 128 : ri * 128 + PIX]
                for m in range(1, 4):
                    start = (ri * 4 + m) * PIX
                    part = jnp.where(block == m, moved[start : start + PIX], part)
                parts.append(part)
            out[i] = jnp.concatenate(parts, 0).astype(BF16)

    for_listed(n, 4, body)


def cut_windows(asked, tile):
    comps, rows, columns = tile.shape
    slots = asked.shape[0] * CAP
    return pl.pallas_call(
        cut_kernel,
        out_shape=jax.ShapeDtypeStruct((slots, 2 * PIX, LANES), BF16),
        in_specs=[pl.BlockSpec(memory_space=pltpu.SMEM), pl.BlockSpec(memory_space=pltpu.VMEM)],
        out_specs=pl.BlockSpec(memory_space=pltpu.VMEM),
        scratch_shapes=[
            pltpu.VMEM((columns // LANES, comps * rows, LANES), F32),
            pltpu.SMEM((slots + 1,), jnp.int32),
        ],
        name="cut",
    )(asked, tile)


def add_kernel(asked, pieces, out, wide, order):
    comps, rows, columns = out.shape
    panels = columns // LANES
    for j in range(panels):
        wide[j] = jnp.zeros((comps * rows, LANES), F32)
    n = listed(asked, order)
    line = lax.broadcasted_iota(jnp.int32, (LANES, LANES), 0)
    lane = lax.broadcasted_iota(jnp.int32, (LANES, LANES), 1)
    ahead = lane - line % PIX
    block = lax.broadcasted_iota(jnp.int32, (PIX, LANES), 1) // PIX

    def body(places):
        spread = []
        for place in places:
            i = order[place]
            r, c0 = corner(asked, i)
            j, shift = c0 // LANES, c0 % LANES
            piece = pieces[i].astype(F32)
            lines = []
            for ri in range(2):
                for m in range(4):
                    lines.append(jnp.where(block == m, piece[ri * PIX : (ri + 1) * PIX], 0.0))
            lines = jnp.concatenate(lines, 0).astype(BF16)
            moved = dot(lines, jnp.where(ahead == shift, 1.0, 0.0).astype(BF16))
            spread.append((r, j, shift, lines, moved))
        for r, j, shift, lines, moved in spread:
            for c in range(comps):
                at = pl.ds(c * rows + r, PIX)
                wide[j, at, :] = wide[j, at, :] + moved[c * PIX : (c + 1) * PIX]
        for r, j, shift, lines, moved in spread:

            @pl.when(shift > LANES - PIX)
            def _(r=r, j=j, shift=shift, lines=lines):
                over = dot(lines, jnp.where(ahead + LANES == shift, 1.0, 0.0).astype(BF16))
                for c in range(comps):
                    at = pl.ds(c * rows + r, PIX)
                    wide[j + 1, at, :] = wide[j + 1, at, :] + over[c * PIX : (c + 1) * PIX]

    for_listed(n, 4, body)
    for j in range(panels):
        out[:, :, j * LANES : (j + 1) * LANES] = wide[j].reshape(comps, rows, LANES)


def add_windows(asked, pieces, comps, rows, columns):
    slots = asked.shape[0] * CAP
    return pl.pallas_call(
        add_kernel,
        out_shape=jax.ShapeDtypeStruct((comps, rows, columns), F32),
        in_specs=[pl.BlockSpec(memory_space=pltpu.SMEM), pl.BlockSpec(memory_space=pltpu.VMEM)],
        out_specs=pl.BlockSpec(memory_space=pltpu.VMEM),
        scratch_shapes=[
            pltpu.VMEM((columns // LANES, comps * rows, LANES), F32),
            pltpu.SMEM((slots + 1,), jnp.int32),
        ],
        name="add",
    )(asked, pieces)


def turn_waves(turns):
    part = turns - jnp.round(turns)
    z = part * part
    coef_sin = [(-1.0) ** k * math.pi ** (2 * k + 1) / math.factorial(2 * k + 1) for k in range(7)]
    coef_cos = [(-1.0) ** k * math.pi ** (2 * k) / math.factorial(2 * k) for k in range(8)]
    s = jnp.full_like(z, coef_sin[-1])
    for v in coef_sin[-2::-1]:
        s = s * z + v
    s = s * part
    c = jnp.full_like(z, coef_cos[-1])
    for v in coef_cos[-2::-1]:
        c = c * z + v
    return 1.0 - 2.0 * s * s, 2.0 * s * c


def image_kernel(group, vis, uv, out):
    samples = vis.shape[2]
    position = lax.broadcasted_iota(jnp.int32, (PIX, samples), 0).astype(F32) * (1.0 / PIX)

    def step(g, carry):
        for k in range(group):
            s = g * group + k
            uv_rows = uv[s]
            x_cos, x_sin = turn_waves(position * uv_rows[0:1])
            y_cos, y_sin = turn_waves(position * uv_rows[1:2])
            wave_x = jnp.concatenate([x_cos, x_sin], 0).astype(BF16)
            y_cos, y_sin = y_cos.astype(BF16).astype(F32), y_sin.astype(BF16).astype(F32)
            rows = vis[s].astype(F32)
            weight_re, weight_im = [], []
            for m in range(4):
                re, im = rows[m : m + 1], rows[m + 4 : m + 5]
                weight_re.append(re * y_cos - im * y_sin)
                weight_im.append(re * y_sin + im * y_cos)
            weighted = jnp.concatenate(weight_re + weight_im, 0).astype(BF16)
            products = lax.dot_general(
                wave_x, weighted, (((1,), (1,)), ((), ())), preferred_element_type=F32
            )
            low, high = products[:PIX], products[PIX:]
            out[s, 0:PIX] = low[:, :LANES] - high[:, LANES:]
            out[s, PIX:] = low[:, LANES:] + high[:, :LANES]
        return carry

    lax.fori_loop(0, vis.shape[0] // group, step, 0)


def adjoint_images(vis, uv):
    count = vis.shape[0]
    group = math.gcd(count, 4)
    vmem = pl.BlockSpec(memory_space=pltpu.VMEM)
    return pl.pallas_call(
        lambda *refs: image_kernel(group, *refs),
        out_shape=jax.ShapeDtypeStruct((count, 2 * PIX, LANES), F32),
        in_specs=[vmem, vmem],
        out_specs=vmem,
        name="image",
    )(vis, uv)


def join_halves(near, far, table, sems):
    half = near.shape[0]
    copies = [
        pltpu.make_async_copy(ref, table.at[pl.ds(i * half, half)], sems.at[i])
        for i, ref in enumerate((near, far))
    ]
    for copy in copies:
        copy.start()
    return copies


def screens_of(table, row, spread):
    wide = dot(table[row], spread[...])
    return wide[:, :LANES], wide[:, LANES:]


def patch_kernel(
    group, slot, first, second, image, near, far, backward, right, spread_a, spread_b,
    out, table, sems,
):
    for copy in join_halves(near, far, table, sems):
        copy.wait()

    def step(g, carry):
        for k in range(group):
            s = g * group + k
            a_re, a_im = screens_of(table, first[s], spread_a)
            b_re, b_im = screens_of(table, second[s], spread_b)
            m_re, m_im = image[s, 0:PIX], image[s, PIX:]
            both_re = a_re * b_re + a_im * b_im
            both_im = a_re * b_im - a_im * b_re
            back_re = both_re * m_re - both_im * m_im
            back_im = both_re * m_im + both_im * m_re
            back = jnp.concatenate([back_re, back_im], 0).astype(BF16)
            low = dot(backward[...], back).astype(BF16)
            grad = dot(low, right[...])
            re, im = grad[:PIX], grad[PIX:]
            grad_re = re[:, :LANES] + im[:, LANES:]
            grad_im = im[:, :LANES] - re[:, LANES:]
            out[slot[s]] = jnp.concatenate([grad_re, grad_im], 0).astype(BF16)
        return carry

    lax.fori_loop(0, image.shape[0] // group, step, 0)


def table_scratch(near):
    whole = (2 * near.shape[0],) + near.shape[1:]
    return [pltpu.VMEM(whole, BF16), pltpu.SemaphoreType.DMA((2,))]


def patch_gradients(slot, first, second, image, near, far, consts, slots):
    _, backward, right, spread_a, spread_b = consts
    group = math.gcd(image.shape[0], 4)
    vmem, smem = pl.BlockSpec(memory_space=pltpu.VMEM), pl.BlockSpec(memory_space=pltpu.SMEM)
    return pl.pallas_call(
        lambda *refs: patch_kernel(group, *refs),
        out_shape=jax.ShapeDtypeStruct((slots, 2 * PIX, LANES), BF16),
        in_specs=[smem] * 3 + [vmem] + [pl.BlockSpec(memory_space=pl.ANY)] * 2 + [vmem] * 4,
        out_specs=vmem,
        scratch_shapes=table_scratch(near),
        name="patch",
    )(slot, first, second, image, near, far, backward, right, spread_a, spread_b)


def screen_kernel(
    group, slot, first, second, first_sum, second_sum, image, patches, near, far,
    forward, right, spread_a, spread_b, out_near, out_far, table, sems, acc,
):
    chunk = 32
    copies = join_halves(near, far, table, sems)

    def clear(i, carry):
        acc[pl.ds(i * chunk, chunk)] = jnp.zeros((chunk, PIX, LANES), F32)
        return carry

    lax.fori_loop(0, acc.shape[0] // chunk, clear, 0)
    for copy in copies:
        copy.wait()
    block = lax.broadcasted_iota(jnp.int32, (PIX, LANES), 1) // PIX

    def step(g, carry):
        terms = []
        for k in range(group):
            s = g * group + k
            a_re, a_im = screens_of(table, first[s], spread_a)
            b_re, b_im = screens_of(table, second[s], spread_b)
            m_re, m_im = image[s, 0:PIX], image[s, PIX:]
            mid = dot(forward[...], patches[slot[s]]).astype(BF16)
            wide = dot(mid, right[...])
            re, im = wide[:PIX], wide[PIX:]
            sky_re = re[:, :LANES] - im[:, LANES:]
            sky_im = re[:, LANES:] + im[:, :LANES]
            carry_re = b_re * m_re - b_im * m_im
            carry_im = b_re * m_im + b_im * m_re
            ga_re = sky_re * carry_re + sky_im * carry_im
            ga_im = sky_re * carry_im - sky_im * carry_re
            model_re = a_re * sky_re - a_im * sky_im
            model_im = a_re * sky_im + a_im * sky_re
            gb_re = m_re * model_re + m_im * model_im
            gb_im = m_re * model_im - m_im * model_re
            ta = jnp.where(
                block % 2 == 0,
                ga_re + pltpu.roll(ga_re, LANES - PIX, 1),
                ga_im + pltpu.roll(ga_im, PIX, 1),
            )
            ta = jnp.where(
                block == 1,
                pltpu.roll(ta, LANES - PIX, 1),
                jnp.where(block == 2, pltpu.roll(ta, PIX, 1), ta),
            )
            tb = jnp.where(
                block < 2,
                gb_re + pltpu.roll(gb_re, 2 * PIX, 1),
                gb_im + pltpu.roll(gb_im, 2 * PIX, 1),
            )
            terms.append((s, ta, tb))
        for s, ta, tb in terms:
            acc[first_sum[s]] = acc[first_sum[s]] + ta
            acc[second_sum[s]] = acc[second_sum[s]] + tb
        return carry

    lax.fori_loop(0, image.shape[0] // group, step, 0)

    for start, out in ((0, out_near), (out_near.shape[0], out_far)):

        def give(i, carry, start=start, out=out):
            out[pl.ds(i * chunk, chunk)] = acc[pl.ds(start + i * chunk, chunk)].astype(BF16)
            return carry

        lax.fori_loop(0, out.shape[0] // chunk, give, 0)


def screen_gradients(slot, rows, image, patches, near, far, consts):
    forward, _, right, spread_a, spread_b = consts
    group = math.gcd(image.shape[0], 4)
    vmem, smem = pl.BlockSpec(memory_space=pltpu.VMEM), pl.BlockSpec(memory_space=pltpu.SMEM)
    scratch = table_scratch(near)
    return pl.pallas_call(
        lambda *refs: screen_kernel(group, *refs),
        out_shape=(jax.ShapeDtypeStruct(near.shape, BF16),) * 2,
        in_specs=[smem] * 5 + [vmem] * 2 + [pl.BlockSpec(memory_space=pl.ANY)] * 2 + [vmem] * 4,
        out_specs=(vmem,) * 2,
        scratch_shapes=scratch + [pltpu.VMEM(scratch[0].shape, F32)],
        name="screen",
    )(slot, *rows, image, patches, near, far, forward, right, spread_a, spread_b)


def exchange(x, axis, groups=None):
    return lax.all_to_all(
        x, axis, split_axis=0, concat_axis=0, tiled=True, axis_index_groups=groups
    )


def ring_gather(x, n_z):
    def by(step):
        return [(2 * z + c, 2 * ((z + step) % n_z) + c) for z in range(n_z) for c in range(2)]

    blocks = [None] * n_z
    blocks[0] = up = down = x
    for k in range(1, n_z // 2 + 1):
        up = lax.ppermute(up, "freq", by(1))
        blocks[n_z - k] = up
        if k < n_z - k:
            down = lax.ppermute(down, "freq", by(-1))
            blocks[k] = down
    return jnp.stack(blocks)


def per_device(
    uv_grid, screens, residual, uv_coords, owner_tile, row_offset, column, stations, time_slot
):
    n_bt, n_freq = lax.axis_size("bt"), lax.axis_size("freq")
    n_z = n_freq // 2
    slots = n_bt * CAP
    consts = constant_tables()
    swap = [(f, f ^ 1) for f in range(n_freq)]
    same_core = [[2 * z + c for z in range(n_z)] for c in range(2)]
    row = TSLOTS * PIX
    mail, slot, first, second, first_sum, second_sum = make_mail(
        lax.axis_index("freq").astype(jnp.int32).reshape(1),
        owner_tile[0, :, 0],
        row_offset[0],
        column[0],
        stations[0].reshape(-1),
        time_slot[0],
        screens[:, 0],
        n_bt,
        n_freq,
    )
    image = adjoint_images(residual[0], uv_coords[0])
    mail, image = lax.optimization_barrier((exchange(mail, "bt"), image))
    asked = mail[:, row].astype(jnp.int32)
    cut = cut_windows(asked, uv_grid[0])
    cut, screens_here = lax.optimization_barrier((cut, mail[:, :row]))
    fetched = exchange(cut.reshape(n_bt, CAP, 2 * PIX, LANES), "bt")
    fetched = fetched.reshape(slots, 2 * PIX, LANES)
    near = ring_gather(screens_here, n_z).reshape(n_z * n_bt * TSLOTS, PIX, LANES)
    far = lax.ppermute(near, "freq", swap)
    terms, sent = screen_gradients(
        slot, (first, second, first_sum, second_sum), image, fetched, near, far, consts
    )
    grads = patch_gradients(slot, first, second, image, near, far, consts, slots)
    returned = exchange(grads.reshape(n_bt, CAP, 2 * PIX, LANES), "bt").reshape(slots, 2 * PIX, LANES)
    grid_grad = add_windows(asked, returned, *uv_grid.shape[1:])
    came = lax.ppermute(sent, "freq", swap)
    part = (terms.astype(F32) + came.astype(F32)).astype(BF16)
    part = exchange(part.reshape(n_bt, n_z, TSLOTS, PIX, LANES), "bt")
    part = jnp.sum(part.astype(F32), 0).astype(BF16)
    screen_grad = finish(exchange(part, "freq", same_core))
    return grid_grad[None], screen_grad[:, None]


def solution(mesh):
    in_specs = (
        P("freq", None, "bt", None),
        P(None, ("bt", "freq"), None, None),
        P("freq", "bt", None, None),
        P("freq", "bt", None, None),
        P("freq", "bt", None),
        P("freq", "bt"),
        P("freq", "bt"),
        P("freq", "bt", None),
        P("freq", "bt"),
    )
    out_specs = (P("freq", None, "bt", None), P(None, ("bt", "freq"), None, None))

    return jax.shard_map(
        per_device, mesh=mesh, in_specs=in_specs, out_specs=out_specs, check_vma=False
    )
```

```python
import math

import jax
import jax.numpy as jnp
import numpy as np
from jax import lax
from jax.experimental import pallas as pl
from jax.experimental.pallas import tpu as pltpu
from jax.sharding import PartitionSpec as P


PIX = 32
TSLOTS = 2
LANES = 128
CAP = 8
F32 = jnp.float32
BF16 = jnp.bfloat16


def constant_tables():
    ramp = np.arange(PIX)
    angle = (ramp[:, None] * ramp[None, :] % PIX) * (2.0 * math.pi / PIX)
    cos_part = (np.cos(angle) / math.sqrt(PIX)).astype(np.float32)
    sin_part = (np.sin(angle) / math.sqrt(PIX)).astype(np.float32)
    forward = np.block([[cos_part, -sin_part], [sin_part, cos_part]])
    backward = np.block([[cos_part, sin_part], [-sin_part, cos_part]])
    eye = np.eye(4, dtype=np.float32)
    right = np.concatenate([np.kron(eye, cos_part), np.kron(eye, sin_part)], 1)
    block = np.eye(PIX, dtype=np.float32)

    def spread(picks):
        out = np.zeros((LANES, len(picks) * PIX), np.float32)
        for j, i in enumerate(picks):
            out[i * PIX : (i + 1) * PIX, j * PIX : (j + 1) * PIX] = block
        return out

    spread_first = spread([0, 0, 1, 1, 2, 2, 3, 3])
    spread_second = spread([0, 1, 0, 1, 2, 3, 2, 3])
    as_bf16 = [
        jnp.asarray(v, BF16) for v in (forward, backward, right, spread_first, spread_second)
    ]
    return as_bf16


def dot(a, b):
    return jnp.dot(a, b, preferred_element_type=F32)


def swap_blocks(x):
    rolled = [x] + [pltpu.roll(x, d * PIX, 1) for d in (1, 2, 3)]
    line = lax.broadcasted_iota(jnp.int32, x.shape, 0)
    block = lax.broadcasted_iota(jnp.int32, x.shape, 1) // PIX
    rows = []
    for a in range(4):
        d = (block - a + 4) % 4
        moved = rolled[0]
        for k in (1, 2, 3):
            moved = jnp.where(d == k, rolled[k], moved)
        rows.append(jnp.sum(jnp.where(block == line, moved, 0.0), 0, keepdims=True))
    return rows


def mail_kernel(
    n_bt, n_freq, me, owner, row_offset, column, stations, slot_time, screens,
    mail, slot, first, second, first_sum, second_sum, fill, request, own,
):
    count = owner.shape[0]
    n_z = n_freq // 2
    my_z, my_core = me[0] // 2, me[0] % 2

    def clear(i, carry):
        request[i] = -1
        return carry

    lax.fori_loop(0, n_bt * CAP, clear, 0)

    def zero(i, carry):
        fill[i] = 0
        return carry

    lax.fori_loop(0, n_bt, zero, 0)

    def rows(station, t):
        bt, freq = station // n_freq, station % n_freq
        z, core = freq // 2, freq % 2
        half = jnp.where(core == my_core, 0, n_bt * n_z)
        ahead = (z - my_z + n_z) % n_z
        return (half + ahead * n_bt + bt) * TSLOTS + t, (half + bt * n_z + z) * TSLOTS + t

    def step(s, carry):
        o = owner[s]
        place = o * CAP + fill[o]
        fill[o] = fill[o] + 1
        slot[s] = place
        request[place] = row_offset[s] * 1024 + column[s]
        first[s], first_sum[s] = rows(stations[0, s], slot_time[s])
        second[s], second_sum[s] = rows(stations[1, s], slot_time[s])
        return carry

    lax.fori_loop(0, count, step, 0)
    for t in range(TSLOTS):
        table = screens[t].astype(F32)
        for high in range(PIX // 4):
            for a, line in enumerate(swap_blocks(table[:, high * LANES : (high + 1) * LANES])):
                x = t * PIX + high * 4 + a
                own[x : x + 1] = line
    every = own[...].astype(BF16)
    lane = lax.broadcasted_iota(jnp.int32, (16, LANES), 1)

    def address(j, carry):
        line = jnp.full((16, LANES), -1, jnp.int32)
        for k in range(CAP):
            code = request[j * CAP + k]
            for part, value in enumerate((code >> 10, (code >> 5) & 31, code & 31)):
                line = jnp.where(lane == part * CAP + k, value, line)
        mail[j] = jnp.concatenate([every, line.astype(F32).astype(BF16)], 0)
        return carry

    lax.fori_loop(0, n_bt, address, 0)


def make_mail(me, owners, row_offset, column, stations, slot_time, screens, n_bt, n_freq):
    count = owners.shape[0]
    smem, vmem = pl.BlockSpec(memory_space=pltpu.SMEM), pl.BlockSpec(memory_space=pltpu.VMEM)
    ints = jax.ShapeDtypeStruct((count,), jnp.int32)
    rows = TSLOTS * PIX
    return pl.pallas_call(
        lambda *refs: mail_kernel(n_bt, n_freq, *refs),
        out_shape=(jax.ShapeDtypeStruct((n_bt, rows + 16, LANES), BF16),) + (ints,) * 5,
        in_specs=[smem] * 6 + [vmem],
        out_specs=(vmem,) + (smem,) * 5,
        scratch_shapes=[
            pltpu.SMEM((n_bt,), jnp.int32),
            pltpu.SMEM((n_bt * CAP,), jnp.int32),
            pltpu.VMEM((rows, LANES), F32),
        ],
        name="mail",
    )(me, owners, row_offset, column, stations, slot_time, screens)


def finish_kernel(parts, out):
    total = jnp.sum(parts[...].astype(F32), 0)
    line = lax.broadcasted_iota(jnp.int32, (4, LANES), 0)
    for t in range(TSLOTS):
        for high in range(PIX // 4):
            rows = swap_blocks(total[t, high * 4 : high * 4 + 4])
            tile = jnp.broadcast_to(rows[0], (4, LANES))
            for a in (1, 2, 3):
                tile = jnp.where(line == a, jnp.broadcast_to(rows[a], (4, LANES)), tile)
            out[t, :, high * LANES : (high + 1) * LANES] = tile


def finish(parts):
    vmem = pl.BlockSpec(memory_space=pltpu.VMEM)
    return pl.pallas_call(
        finish_kernel,
        out_shape=jax.ShapeDtypeStruct((TSLOTS, 4, PIX * PIX), F32),
        in_specs=[vmem],
        out_specs=vmem,
        name="finish",
    )(parts)


def listed(asked, order):
    def step(i, n):
        order[n] = i
        return n + (asked[i // CAP, i % CAP] >= 0).astype(jnp.int32)

    return lax.fori_loop(0, asked.shape[0] * CAP, step, jnp.int32(0))


def corner(asked, i):
    j, k = i // CAP, i % CAP
    return asked[j, k], asked[j, CAP + k] * PIX + asked[j, 2 * CAP + k]


def for_listed(n, group, body):
    def whole(g, carry):
        body([g * group + k for k in range(group)])
        return carry

    lax.fori_loop(0, n // group, whole, 0)

    def rest(i, carry):
        body([i])
        return carry

    lax.fori_loop(n // group * group, n, rest, 0)


def cut_kernel(asked, tile, out, wide, order):
    comps, rows, columns = tile.shape
    panels = columns // LANES
    for j in range(panels):
        wide[j] = tile[:, :, j * LANES : (j + 1) * LANES].astype(F32).reshape(comps * rows, LANES)
    n = listed(asked, order)
    line = lax.broadcasted_iota(jnp.int32, (LANES, LANES), 0)
    lane = lax.broadcasted_iota(jnp.int32, (LANES, LANES), 1)
    ahead = line - lane % PIX
    block = lax.broadcasted_iota(jnp.int32, (PIX, LANES), 1) // PIX

    def body(places):
        done = []
        for place in places:
            i = order[place]
            r, c0 = corner(asked, i)
            j, shift = c0 // LANES, c0 % LANES
            after = jnp.minimum(j + 1, panels - 1)

            def rows_of(panel):
                return jnp.concatenate(
                    [wide[panel, pl.ds(c * rows + r, PIX), :] for c in range(comps)], 0
                ).astype(BF16)

            both = jnp.concatenate([rows_of(j), rows_of(after)], 1)
            pick = jnp.concatenate([ahead == shift, ahead + LANES == shift], 0)
            moved = dot(both, jnp.where(pick, 1.0, 0.0).astype(BF16))
            parts = []
            for ri in range(2):
                part = moved[ri * 128 : ri * 128 + PIX]
                for m in range(1, 4):
                    start = (ri * 4 + m) * PIX
                    part = jnp.where(block == m, moved[start : start + PIX], part)
                parts.append(part)
            done.append((i, jnp.concatenate(parts, 0).astype(BF16)))
        for i, piece in done:
            out[i] = piece

    for_listed(n, 4, body)


def cut_windows(asked, tile):
    comps, rows, columns = tile.shape
    slots = asked.shape[0] * CAP
    return pl.pallas_call(
        cut_kernel,
        out_shape=jax.ShapeDtypeStruct((slots, 2 * PIX, LANES), BF16),
        in_specs=[pl.BlockSpec(memory_space=pltpu.SMEM), pl.BlockSpec(memory_space=pltpu.VMEM)],
        out_specs=pl.BlockSpec(memory_space=pltpu.VMEM),
        scratch_shapes=[
            pltpu.VMEM((columns // LANES, comps * rows, LANES), F32),
            pltpu.SMEM((slots + 1,), jnp.int32),
        ],
        name="cut",
    )(asked, tile)


def add_kernel(asked, pieces, out, wide, order):
    comps, rows, columns = out.shape
    panels = columns // LANES
    for j in range(panels):
        wide[j] = jnp.zeros((comps * rows, LANES), F32)
    n = listed(asked, order)
    line = lax.broadcasted_iota(jnp.int32, (LANES, LANES), 0)
    lane = lax.broadcasted_iota(jnp.int32, (LANES, LANES), 1)
    ahead = lane - line % PIX
    block = lax.broadcasted_iota(jnp.int32, (PIX, LANES), 1) // PIX

    def body(places):
        spread = []
        for place in places:
            i = order[place]
            r, c0 = corner(asked, i)
            j, shift = c0 // LANES, c0 % LANES
            piece = pieces[i].astype(F32)
            lines = []
            for ri in range(2):
                for m in range(4):
                    lines.append(jnp.where(block == m, piece[ri * PIX : (ri + 1) * PIX], 0.0))
            lines = jnp.concatenate(lines, 0).astype(BF16)
            pick = jnp.concatenate([ahead == shift, ahead + LANES == shift], 1)
            spread.append((r, j, shift, dot(lines, jnp.where(pick, 1.0, 0.0).astype(BF16))))
        for r, j, shift, moved in spread:
            for c in range(comps):
                at = pl.ds(c * rows + r, PIX)
                wide[j, at, :] = wide[j, at, :] + moved[c * PIX : (c + 1) * PIX, :LANES]
        for r, j, shift, moved in spread:

            @pl.when(shift > LANES - PIX)
            def _(r=r, j=j, moved=moved):
                for c in range(comps):
                    at = pl.ds(c * rows + r, PIX)
                    wide[j + 1, at, :] = wide[j + 1, at, :] + moved[c * PIX : (c + 1) * PIX, LANES:]

    for_listed(n, 4, body)
    for j in range(panels):
        out[:, :, j * LANES : (j + 1) * LANES] = wide[j].reshape(comps, rows, LANES)


def add_windows(asked, pieces, comps, rows, columns):
    slots = asked.shape[0] * CAP
    return pl.pallas_call(
        add_kernel,
        out_shape=jax.ShapeDtypeStruct((comps, rows, columns), F32),
        in_specs=[pl.BlockSpec(memory_space=pltpu.SMEM), pl.BlockSpec(memory_space=pltpu.VMEM)],
        out_specs=pl.BlockSpec(memory_space=pltpu.VMEM),
        scratch_shapes=[
            pltpu.VMEM((columns // LANES, comps * rows, LANES), F32),
            pltpu.SMEM((slots + 1,), jnp.int32),
        ],
        name="add",
    )(asked, pieces)


def turn_waves(turns):
    part = turns - jnp.round(turns)
    z = part * part
    coef_sin = [(-1.0) ** k * math.pi ** (2 * k + 1) / math.factorial(2 * k + 1) for k in range(7)]
    coef_cos = [(-1.0) ** k * math.pi ** (2 * k) / math.factorial(2 * k) for k in range(8)]
    s = jnp.full_like(z, coef_sin[-1])
    for v in coef_sin[-2::-1]:
        s = s * z + v
    s = s * part
    c = jnp.full_like(z, coef_cos[-1])
    for v in coef_cos[-2::-1]:
        c = c * z + v
    return 1.0 - 2.0 * s * s, 2.0 * s * c


def image_kernel(group, vis, uv, out):
    samples = vis.shape[2]
    position = lax.broadcasted_iota(jnp.int32, (PIX, samples), 0).astype(F32) * (1.0 / PIX)

    def step(g, carry):
        done = []
        for k in range(group):
            s = g * group + k
            uv_rows = uv[s]
            x_cos, x_sin = turn_waves(position * uv_rows[0:1])
            y_cos, y_sin = turn_waves(position * uv_rows[1:2])
            wave_x = jnp.concatenate([x_cos, x_sin], 0).astype(BF16)
            y_cos, y_sin = y_cos.astype(BF16).astype(F32), y_sin.astype(BF16).astype(F32)
            rows = vis[s].astype(F32)
            weight_re, weight_im = [], []
            for m in range(4):
                re, im = rows[m : m + 1], rows[m + 4 : m + 5]
                weight_re.append(re * y_cos - im * y_sin)
                weight_im.append(re * y_sin + im * y_cos)
            weighted = jnp.concatenate(weight_re + weight_im, 0).astype(BF16)
            products = lax.dot_general(
                wave_x, weighted, (((1,), (1,)), ((), ())), preferred_element_type=F32
            )
            low, high = products[:PIX], products[PIX:]
            done.append((s, low[:, :LANES] - high[:, LANES:], low[:, LANES:] + high[:, :LANES]))
        for s, re, im in done:
            out[s, 0:PIX] = re
            out[s, PIX:] = im
        return carry

    lax.fori_loop(0, vis.shape[0] // group, step, 0)


def adjoint_images(vis, uv):
    count = vis.shape[0]
    group = math.gcd(count, 4)
    vmem = pl.BlockSpec(memory_space=pltpu.VMEM)
    return pl.pallas_call(
        lambda *refs: image_kernel(group, *refs),
        out_shape=jax.ShapeDtypeStruct((count, 2 * PIX, LANES), F32),
        in_specs=[vmem, vmem],
        out_specs=vmem,
        name="image",
    )(vis, uv)


def join_halves(near, far, table, sems):
    half = near.shape[0]
    copies = [
        pltpu.make_async_copy(ref, table.at[pl.ds(i * half, half)], sems.at[i])
        for i, ref in enumerate((near, far))
    ]
    for copy in copies:
        copy.start()
    return copies


def screens_of(table, rows, spread):
    wide = dot(jnp.concatenate([table[row] for row in rows], 0), spread[...])
    at = [slice(k * PIX, (k + 1) * PIX) for k in range(len(rows))]
    return [(wide[k, :LANES], wide[k, LANES:]) for k in at]


def transforms(left, pieces, right):
    inner = dot(left[...], jnp.concatenate(pieces, 1)).astype(BF16)
    lines = [inner[:, k * LANES : (k + 1) * LANES] for k in range(len(pieces))]
    outer = dot(jnp.concatenate(lines, 0), right[...])
    return [outer[k * 2 * PIX : (k + 1) * 2 * PIX] for k in range(len(pieces))]


def patch_kernel(
    group, slot, first, second, image, near, far, backward, right, spread_a, spread_b,
    out, table, sems,
):
    for copy in join_halves(near, far, table, sems):
        copy.wait()

    def step(g, carry):
        subs = [g * group + k for k in range(group)]
        first_screens = screens_of(table, [first[s] for s in subs], spread_a)
        second_screens = screens_of(table, [second[s] for s in subs], spread_b)
        backs = []
        for s, (a_re, a_im), (b_re, b_im) in zip(subs, first_screens, second_screens):
            m_re, m_im = image[s, 0:PIX], image[s, PIX:]
            both_re = a_re * b_re + a_im * b_im
            both_im = a_re * b_im - a_im * b_re
            back_re = both_re * m_re - both_im * m_im
            back_im = both_re * m_im + both_im * m_re
            backs.append(jnp.concatenate([back_re, back_im], 0).astype(BF16))
        grads = []
        for grad in transforms(backward, backs, right):
            re, im = grad[:PIX], grad[PIX:]
            grad_re = re[:, :LANES] + im[:, LANES:]
            grad_im = im[:, :LANES] - re[:, LANES:]
            grads.append(jnp.concatenate([grad_re, grad_im], 0).astype(BF16))
        for s, grad in zip(subs, grads):
            out[slot[s]] = grad
        return carry

    lax.fori_loop(0, image.shape[0] // group, step, 0)


def table_scratch(near):
    whole = (2 * near.shape[0],) + near.shape[1:]
    return [pltpu.VMEM(whole, BF16), pltpu.SemaphoreType.DMA((2,))]


def patch_gradients(slot, first, second, image, near, far, consts, slots):
    _, backward, right, spread_a, spread_b = consts
    group = math.gcd(image.shape[0], 4)
    vmem, smem = pl.BlockSpec(memory_space=pltpu.VMEM), pl.BlockSpec(memory_space=pltpu.SMEM)
    return pl.pallas_call(
        lambda *refs: patch_kernel(group, *refs),
        out_shape=jax.ShapeDtypeStruct((slots, 2 * PIX, LANES), BF16),
        in_specs=[smem] * 3 + [vmem] + [pl.BlockSpec(memory_space=pl.ANY)] * 2 + [vmem] * 4,
        out_specs=vmem,
        scratch_shapes=table_scratch(near),
        name="patch",
    )(slot, first, second, image, near, far, backward, right, spread_a, spread_b)


def screen_kernel(
    group, slot, first, second, first_sum, second_sum, image, patches, near, far,
    forward, right, spread_a, spread_b, out_near, out_far, table, sems, acc,
):
    chunk = 32
    copies = join_halves(near, far, table, sems)

    def clear(i, carry):
        acc[pl.ds(i * chunk, chunk)] = jnp.zeros((chunk, PIX, LANES), F32)
        return carry

    lax.fori_loop(0, acc.shape[0] // chunk, clear, 0)
    for copy in copies:
        copy.wait()
    block = lax.broadcasted_iota(jnp.int32, (PIX, LANES), 1) // PIX

    def step(g, carry):
        terms = []
        subs = [g * group + k for k in range(group)]
        first_screens = screens_of(table, [first[s] for s in subs], spread_a)
        second_screens = screens_of(table, [second[s] for s in subs], spread_b)
        skies = transforms(forward, [patches[slot[s]] for s in subs], right)
        for s, (a_re, a_im), (b_re, b_im), sky in zip(subs, first_screens, second_screens, skies):
            m_re, m_im = image[s, 0:PIX], image[s, PIX:]
            re, im = sky[:PIX], sky[PIX:]
            sky_re = re[:, :LANES] - im[:, LANES:]
            sky_im = re[:, LANES:] + im[:, :LANES]
            carry_re = b_re * m_re - b_im * m_im
            carry_im = b_re * m_im + b_im * m_re
            ga_re = sky_re * carry_re + sky_im * carry_im
            ga_im = sky_re * carry_im - sky_im * carry_re
            model_re = a_re * sky_re - a_im * sky_im
            model_im = a_re * sky_im + a_im * sky_re
            gb_re = m_re * model_re + m_im * model_im
            gb_im = m_re * model_im - m_im * model_re
            ta = jnp.where(
                block % 2 == 0,
                ga_re + pltpu.roll(ga_re, LANES - PIX, 1),
                ga_im + pltpu.roll(ga_im, PIX, 1),
            )
            ta = jnp.where(
                block == 1,
                pltpu.roll(ta, LANES - PIX, 1),
                jnp.where(block == 2, pltpu.roll(ta, PIX, 1), ta),
            )
            tb = jnp.where(
                block < 2,
                gb_re + pltpu.roll(gb_re, 2 * PIX, 1),
                gb_im + pltpu.roll(gb_im, 2 * PIX, 1),
            )
            terms.append((s, ta, tb))
        for s, ta, tb in terms:
            acc[first_sum[s]] = acc[first_sum[s]] + ta
            acc[second_sum[s]] = acc[second_sum[s]] + tb
        return carry

    lax.fori_loop(0, image.shape[0] // group, step, 0)

    for start, out in ((0, out_near), (out_near.shape[0], out_far)):

        def give(i, carry, start=start, out=out):
            out[pl.ds(i * chunk, chunk)] = acc[pl.ds(start + i * chunk, chunk)].astype(BF16)
            return carry

        lax.fori_loop(0, out.shape[0] // chunk, give, 0)


def screen_gradients(slot, rows, image, patches, near, far, consts):
    forward, _, right, spread_a, spread_b = consts
    group = math.gcd(image.shape[0], 4)
    vmem, smem = pl.BlockSpec(memory_space=pltpu.VMEM), pl.BlockSpec(memory_space=pltpu.SMEM)
    scratch = table_scratch(near)
    return pl.pallas_call(
        lambda *refs: screen_kernel(group, *refs),
        out_shape=(jax.ShapeDtypeStruct(near.shape, BF16),) * 2,
        in_specs=[smem] * 5 + [vmem] * 2 + [pl.BlockSpec(memory_space=pl.ANY)] * 2 + [vmem] * 4,
        out_specs=(vmem,) * 2,
        scratch_shapes=scratch + [pltpu.VMEM(scratch[0].shape, F32)],
        name="screen",
    )(slot, *rows, image, patches, near, far, forward, right, spread_a, spread_b)


def exchange(x, axis, groups=None):
    return lax.all_to_all(
        x, axis, split_axis=0, concat_axis=0, tiled=True, axis_index_groups=groups
    )


def ring_gather(x, n_z):
    def by(step):
        return [(2 * z + c, 2 * ((z + step) % n_z) + c) for z in range(n_z) for c in range(2)]

    blocks = [None] * n_z
    blocks[0] = up = down = x
    for k in range(1, n_z // 2 + 1):
        up = lax.ppermute(up, "freq", by(1))
        blocks[n_z - k] = up
        if k < n_z - k:
            down = lax.ppermute(down, "freq", by(-1))
            blocks[k] = down
    return jnp.stack(blocks)


def per_device(
    uv_grid, screens, residual, uv_coords, owner_tile, row_offset, column, stations, time_slot
):
    n_bt, n_freq = lax.axis_size("bt"), lax.axis_size("freq")
    n_z = n_freq // 2
    slots = n_bt * CAP
    consts = constant_tables()
    swap = [(f, f ^ 1) for f in range(n_freq)]
    same_core = [[2 * z + c for z in range(n_z)] for c in range(2)]
    row = TSLOTS * PIX
    mail, slot, first, second, first_sum, second_sum = make_mail(
        lax.axis_index("freq").astype(jnp.int32).reshape(1),
        owner_tile[0, :, 0],
        row_offset[0],
        column[0],
        stations[0].T,
        time_slot[0],
        screens[:, 0],
        n_bt,
        n_freq,
    )
    image = adjoint_images(residual[0], uv_coords[0])
    mail, image = lax.optimization_barrier((exchange(mail, "bt"), image))
    asked = mail[:, row].astype(jnp.int32)
    near = ring_gather(mail[:, :row], n_z).reshape(n_z * n_bt * TSLOTS, PIX, LANES)
    far = lax.ppermute(near, "freq", swap)
    cut = cut_windows(asked, uv_grid[0])
    fetched = exchange(cut.reshape(n_bt, CAP, 2 * PIX, LANES), "bt")
    fetched = fetched.reshape(slots, 2 * PIX, LANES)
    grads = patch_gradients(slot, first, second, image, near, far, consts, slots)
    returned = exchange(grads.reshape(n_bt, CAP, 2 * PIX, LANES), "bt")
    returned = returned.reshape(slots, 2 * PIX, LANES)
    terms, sent = screen_gradients(
        slot, (first, second, first_sum, second_sum), image, fetched, near, far, consts
    )
    came = lax.ppermute(sent, "freq", swap)
    part = (terms.astype(F32) + came.astype(F32)).astype(BF16)
    part = exchange(part.reshape(n_bt, n_z, TSLOTS, PIX, LANES), "bt")
    grid_grad = add_windows(asked, returned, *uv_grid.shape[1:])
    part = jnp.sum(part.astype(F32), 0).astype(BF16)
    screen_grad = finish(exchange(part, "freq", same_core))
    return grid_grad[None], screen_grad[:, None]


def solution(mesh):
    in_specs = (
        P("freq", None, "bt", None),
        P(None, ("bt", "freq"), None, None),
        P("freq", "bt", None, None),
        P("freq", "bt", None, None),
        P("freq", "bt", None),
        P("freq", "bt"),
        P("freq", "bt"),
        P("freq", "bt", None),
        P("freq", "bt"),
    )
    out_specs = (P("freq", None, "bt", None), P(None, ("bt", "freq"), None, None))

    return jax.shard_map(
        per_device, mesh=mesh, in_specs=in_specs, out_specs=out_specs, check_vma=False
    )
```

```python
import math

import jax
import jax.numpy as jnp
import numpy as np
from jax import lax
from jax.experimental import pallas as pl
from jax.experimental.pallas import tpu as pltpu
from jax.sharding import PartitionSpec as P


PIX = 32
TSLOTS = 2
LANES = 128
CAP = 8
F32 = jnp.float32
BF16 = jnp.bfloat16


def constant_tables():
    ramp = np.arange(PIX)
    angle = (ramp[:, None] * ramp[None, :] % PIX) * (2.0 * math.pi / PIX)
    cos_part = (np.cos(angle) / math.sqrt(PIX)).astype(np.float32)
    sin_part = (np.sin(angle) / math.sqrt(PIX)).astype(np.float32)
    forward = np.block([[cos_part, -sin_part], [sin_part, cos_part]])
    backward = np.block([[cos_part, sin_part], [-sin_part, cos_part]])
    eye = np.eye(4, dtype=np.float32)
    right = np.concatenate([np.kron(eye, cos_part), np.kron(eye, sin_part)], 1)
    block = np.eye(PIX, dtype=np.float32)

    def spread(picks):
        out = np.zeros((LANES, len(picks) * PIX), np.float32)
        for j, i in enumerate(picks):
            out[i * PIX : (i + 1) * PIX, j * PIX : (j + 1) * PIX] = block
        return out

    spread_first = spread([0, 0, 1, 1, 2, 2, 3, 3])
    spread_second = spread([0, 1, 0, 1, 2, 3, 2, 3])
    as_bf16 = [
        jnp.asarray(v, BF16) for v in (forward, backward, right, spread_first, spread_second)
    ]
    return as_bf16


def dot(a, b):
    return jnp.dot(a, b, preferred_element_type=F32)


def swap_blocks(x):
    rolled = [x] + [pltpu.roll(x, d * PIX, 1) for d in (1, 2, 3)]
    line = lax.broadcasted_iota(jnp.int32, x.shape, 0)
    block = lax.broadcasted_iota(jnp.int32, x.shape, 1) // PIX
    rows = []
    for a in range(4):
        d = (block - a + 4) % 4
        moved = rolled[0]
        for k in (1, 2, 3):
            moved = jnp.where(d == k, rolled[k], moved)
        rows.append(jnp.sum(jnp.where(block == line, moved, 0.0), 0, keepdims=True))
    return rows


def mail_kernel(
    n_bt, owner, row_offset, column, screens, mail, slot, fill, request, own,
):
    count = owner.shape[0]
    for i in range(n_bt):
        fill[i] = 0

    def step(s, carry):
        o = owner[s]
        n = fill[o]
        fill[o] = n + 1
        place = o * CAP + n
        slot[s] = place
        request[place] = row_offset[s] * 1024 + column[s]
        return carry

    lax.fori_loop(0, count, step, 0, unroll=4)
    for t in range(TSLOTS):
        table = screens[t].astype(F32)
        for high in range(PIX // 4):
            for a, line in enumerate(swap_blocks(table[:, high * LANES : (high + 1) * LANES])):
                x = t * PIX + high * 4 + a
                own[x : x + 1] = line
    every = own[...].astype(BF16)
    lane = lax.broadcasted_iota(jnp.int32, (16, LANES), 1)

    def address(j, carry):
        n = fill[j]
        line = jnp.where(lane == 3 * CAP, n, 0)
        for k in range(CAP):
            code = jnp.where(k < n, request[j * CAP + k], 0)
            for part, value in enumerate((code >> 10, (code >> 5) & 31, code & 31)):
                line = jnp.where(lane == part * CAP + k, value, line)
        mail[j] = jnp.concatenate([every, line.astype(F32).astype(BF16)], 0)
        return carry

    lax.fori_loop(0, n_bt, address, 0)


def make_mail(owners, row_offset, column, screens, n_bt):
    count = owners.shape[0]
    smem, vmem = pl.BlockSpec(memory_space=pltpu.SMEM), pl.BlockSpec(memory_space=pltpu.VMEM)
    rows = TSLOTS * PIX
    return pl.pallas_call(
        lambda *refs: mail_kernel(n_bt, *refs),
        out_shape=(
            jax.ShapeDtypeStruct((n_bt, rows + 16, LANES), BF16),
            jax.ShapeDtypeStruct((count,), jnp.int32),
        ),
        in_specs=[smem] * 3 + [vmem],
        out_specs=(vmem, smem),
        scratch_shapes=[
            pltpu.SMEM((n_bt,), jnp.int32),
            pltpu.SMEM((n_bt * CAP,), jnp.int32),
            pltpu.VMEM((rows, LANES), F32),
        ],
        name="mail",
    )(owners, row_offset, column, screens)


def finish_kernel(parts, out):
    total = jnp.sum(parts[...].astype(F32), 0)
    line = lax.broadcasted_iota(jnp.int32, (4, LANES), 0)
    for t in range(TSLOTS):
        for high in range(PIX // 4):
            rows = swap_blocks(total[t, high * 4 : high * 4 + 4])
            tile = jnp.broadcast_to(rows[0], (4, LANES))
            for a in (1, 2, 3):
                tile = jnp.where(line == a, jnp.broadcast_to(rows[a], (4, LANES)), tile)
            out[t, :, high * LANES : (high + 1) * LANES] = tile


def finish(parts):
    vmem = pl.BlockSpec(memory_space=pltpu.VMEM)
    return pl.pallas_call(
        finish_kernel,
        out_shape=jax.ShapeDtypeStruct((TSLOTS, 4, PIX * PIX), F32),
        in_specs=[vmem],
        out_specs=vmem,
        name="finish",
    )(parts)


def listed(asked, order):
    def step(j, n):
        for k in range(CAP):
            order[n + k] = j * CAP + k
        return n + asked[j, 3 * CAP]

    return lax.fori_loop(0, asked.shape[0], step, jnp.int32(0))


def corner(asked, i):
    j, k = i >> 3, i & 7
    return asked[j, k], asked[j, CAP + k] * PIX + asked[j, 2 * CAP + k]


def for_listed(n, group, body):
    def whole(g, carry):
        body([g * group + k for k in range(group)])
        return carry

    lax.fori_loop(0, n // group, whole, 0)

    def rest(i, carry):
        body([i])
        return carry

    lax.fori_loop(n // group * group, n, rest, 0)


def cut_kernel(asked, tile, out, wide, order, stage, sems):
    comps, rows, columns = tile.shape
    panels = columns // LANES
    for j in range(panels):
        wide[j] = tile[:, :, j * LANES : (j + 1) * LANES].astype(F32).reshape(comps * rows, LANES)
    n = listed(asked, order)
    line = lax.broadcasted_iota(jnp.int32, (LANES, LANES), 0)
    lane = lax.broadcasted_iota(jnp.int32, (LANES, LANES), 1)
    ahead = line - lane % PIX
    block = lax.broadcasted_iota(jnp.int32, (PIX, LANES), 1) // PIX

    def body(places):
        done = []
        for place in places:
            i = order[place]
            r, c0 = corner(asked, i)
            j, shift = c0 >> 7, c0 & (LANES - 1)
            after = jnp.minimum(j + 1, panels - 1)

            def rows_of(panel):
                return jnp.concatenate(
                    [wide[panel, pl.ds(c * rows + r, PIX), :] for c in range(comps)], 0
                ).astype(BF16)

            both = jnp.concatenate([rows_of(j), rows_of(after)], 1)
            pick = jnp.concatenate([ahead == shift, ahead + LANES == shift], 0)
            moved = dot(both, jnp.where(pick, 1.0, 0.0).astype(BF16))
            parts = []
            for ri in range(2):
                part = moved[ri * 128 : ri * 128 + PIX]
                for m in range(1, 4):
                    start = (ri * 4 + m) * PIX
                    part = jnp.where(block == m, moved[start : start + PIX], part)
                parts.append(part)
            done.append((i, jnp.concatenate(parts, 0).astype(BF16)))
        for i, piece in done:
            stage[i] = piece
        for i, piece in done:
            pltpu.make_async_copy(stage.at[i], out.at[i], sems.at[i]).start()

    for_listed(n, 4, body)

    def finished(g, carry):
        i = order[g]
        pltpu.make_async_copy(stage.at[i], out.at[i], sems.at[i]).wait()
        return carry

    lax.fori_loop(0, n, finished, 0)


def cut_windows(asked, tile):
    comps, rows, columns = tile.shape
    slots = asked.shape[0] * CAP
    return pl.pallas_call(
        cut_kernel,
        out_shape=jax.ShapeDtypeStruct((slots, 2 * PIX, LANES), BF16),
        in_specs=[pl.BlockSpec(memory_space=pltpu.SMEM), pl.BlockSpec(memory_space=pltpu.VMEM)],
        out_specs=pl.BlockSpec(memory_space=pl.ANY),
        scratch_shapes=[
            pltpu.VMEM((columns // LANES, comps * rows, LANES), F32),
            pltpu.SMEM((slots + CAP,), jnp.int32),
            pltpu.VMEM((slots, 2 * PIX, LANES), BF16),
            pltpu.SemaphoreType.DMA((slots,)),
        ],
        name="cut",
    )(asked, tile)


def add_kernel(asked, pieces, out, wide, order):
    comps, rows, columns = out.shape
    panels = columns // LANES
    for j in range(panels):
        wide[j] = jnp.zeros((comps * rows, LANES), F32)
    n = listed(asked, order)
    line = lax.broadcasted_iota(jnp.int32, (LANES, LANES), 0)
    lane = lax.broadcasted_iota(jnp.int32, (LANES, LANES), 1)
    ahead = lane - line % PIX
    block = lax.broadcasted_iota(jnp.int32, (PIX, LANES), 1) // PIX

    def body(places):
        spread = []
        for place in places:
            i = order[place]
            r, c0 = corner(asked, i)
            j, shift = c0 >> 7, c0 & (LANES - 1)
            piece = pieces[i].astype(F32)
            lines = []
            for ri in range(2):
                for m in range(4):
                    lines.append(jnp.where(block == m, piece[ri * PIX : (ri + 1) * PIX], 0.0))
            lines = jnp.concatenate(lines, 0).astype(BF16)
            pick = jnp.concatenate([ahead == shift, ahead + LANES == shift], 1)
            spread.append((r, j, shift, dot(lines, jnp.where(pick, 1.0, 0.0).astype(BF16))))
        for r, j, shift, moved in spread:
            for c in range(comps):
                at = pl.ds(c * rows + r, PIX)
                wide[j, at, :] = wide[j, at, :] + moved[c * PIX : (c + 1) * PIX, :LANES]
        for r, j, shift, moved in spread:

            @pl.when(shift > LANES - PIX)
            def _(r=r, j=j, moved=moved):
                for c in range(comps):
                    at = pl.ds(c * rows + r, PIX)
                    wide[j + 1, at, :] = wide[j + 1, at, :] + moved[c * PIX : (c + 1) * PIX, LANES:]

    for_listed(n, 4, body)
    for j in range(panels):
        out[:, :, j * LANES : (j + 1) * LANES] = wide[j].reshape(comps, rows, LANES)


def add_windows(asked, pieces, comps, rows, columns):
    slots = asked.shape[0] * CAP
    return pl.pallas_call(
        add_kernel,
        out_shape=jax.ShapeDtypeStruct((comps, rows, columns), F32),
        in_specs=[pl.BlockSpec(memory_space=pltpu.SMEM), pl.BlockSpec(memory_space=pltpu.VMEM)],
        out_specs=pl.BlockSpec(memory_space=pltpu.VMEM),
        scratch_shapes=[
            pltpu.VMEM((columns // LANES, comps * rows, LANES), F32),
            pltpu.SMEM((slots + CAP,), jnp.int32),
        ],
        name="add",
    )(asked, pieces)


def turn_waves(turns):
    part = turns - jnp.round(turns)
    z = part * part
    coef_sin = [(-1.0) ** k * math.pi ** (2 * k + 1) / math.factorial(2 * k + 1) for k in range(7)]
    coef_cos = [(-1.0) ** k * math.pi ** (2 * k) / math.factorial(2 * k) for k in range(8)]
    s = jnp.full_like(z, coef_sin[-1])
    for v in coef_sin[-2::-1]:
        s = s * z + v
    s = s * part
    c = jnp.full_like(z, coef_cos[-1])
    for v in coef_cos[-2::-1]:
        c = c * z + v
    return 1.0 - 2.0 * s * s, 2.0 * s * c


def image_kernel(group, vis, uv, out):
    samples = vis.shape[2]
    position = lax.broadcasted_iota(jnp.int32, (PIX, samples), 0).astype(F32) * (1.0 / PIX)

    def step(g, carry):
        done = []
        for k in range(group):
            s = g * group + k
            uv_rows = uv[s]
            x_cos, x_sin = turn_waves(position * uv_rows[0:1])
            y_cos, y_sin = turn_waves(position * uv_rows[1:2])
            wave_x = jnp.concatenate([x_cos, x_sin], 0).astype(BF16)
            y_cos, y_sin = y_cos.astype(BF16).astype(F32), y_sin.astype(BF16).astype(F32)
            rows = vis[s].astype(F32)
            weight_re, weight_im = [], []
            for m in range(4):
                re, im = rows[m : m + 1], rows[m + 4 : m + 5]
                weight_re.append(re * y_cos - im * y_sin)
                weight_im.append(re * y_sin + im * y_cos)
            weighted = jnp.concatenate(weight_re + weight_im, 0).astype(BF16)
            products = lax.dot_general(
                wave_x, weighted, (((1,), (1,)), ((), ())), preferred_element_type=F32
            )
            low, high = products[:PIX], products[PIX:]
            done.append((s, low[:, :LANES] - high[:, LANES:], low[:, LANES:] + high[:, :LANES]))
        for s, re, im in done:
            out[s, 0:PIX] = re
            out[s, PIX:] = im
        return carry

    lax.fori_loop(0, vis.shape[0] // group, step, 0)


def adjoint_images(vis, uv, part, parts):
    count = vis.shape[0] // parts
    group = math.gcd(count, 4)
    blocks = [
        pl.BlockSpec((count,) + x.shape[1:], lambda i: (part, 0, 0)) for x in (vis, uv)
    ]
    return pl.pallas_call(
        lambda *refs: image_kernel(group, *refs),
        out_shape=jax.ShapeDtypeStruct((count, 2 * PIX, LANES), F32),
        grid=(1,),
        in_specs=blocks,
        out_specs=pl.BlockSpec((count, 2 * PIX, LANES), lambda i: (0, 0, 0)),
        name="image",
    )(vis, uv)


def table_rows(n_bt, n_freq, me, stations, slot_time):
    n_z = n_freq // 2
    my_z, my_core = me[0] >> 1, me[0] & 1

    def rows(which, s):
        station, t = stations[which, s], slot_time[s]
        bt, freq = lax.div(station, n_freq), lax.rem(station, n_freq)
        z, core = freq >> 1, freq & 1
        half = jnp.where(core == my_core, 0, n_bt * n_z)
        ahead = lax.rem(z - my_z + n_z, n_z)
        return (half + ahead * n_bt + bt) * TSLOTS + t, (half + bt * n_z + z) * TSLOTS + t

    return rows


def join_parts(parts, whole, sems, chunk):
    copies = []
    for p, part in enumerate(parts):
        for c in range(0, part.shape[0], chunk):
            at = pl.ds(p * part.shape[0] + c, chunk)
            k = len(copies)
            copy = pltpu.make_async_copy(part.at[pl.ds(c, chunk)], whole.at[at], sems.at[k])
            copy.start()
            copies.append(copy)
    return copies


def screens_of(table, rows, spread):
    wide = dot(jnp.concatenate([table[row] for row in rows], 0), spread[...])
    at = [slice(k * PIX, (k + 1) * PIX) for k in range(len(rows))]
    return [(wide[k, :LANES], wide[k, LANES:]) for k in at]


def transforms(left, pieces, right):
    inner = dot(left[...], jnp.concatenate(pieces, 1)).astype(BF16)
    lines = [inner[:, k * LANES : (k + 1) * LANES] for k in range(len(pieces))]
    outer = dot(jnp.concatenate(lines, 0), right[...])
    return [outer[k * 2 * PIX : (k + 1) * 2 * PIX] for k in range(len(pieces))]


def patch_kernel(
    group, n_bt, n_freq, me, slot, stations, slot_time, image_a, image_b, near, far,
    backward, right, spread_a, spread_b, out, table, sems, image, image_sems, stage, out_sems,
):
    copies = join_parts((near, far), table, sems, near.shape[0])
    images = join_parts((image_a, image_b), image, image_sems, image_a.shape[0] // 2)
    rows = table_rows(n_bt, n_freq, me, stations, slot_time)
    for copy in copies:
        copy.wait()

    def step(g, carry):
        subs = [g * group + k for k in range(group)]
        first_screens = screens_of(table, [rows(0, s)[0] for s in subs], spread_a)
        second_screens = screens_of(table, [rows(1, s)[0] for s in subs], spread_b)
        backs = []
        for s, (a_re, a_im), (b_re, b_im) in zip(subs, first_screens, second_screens):
            m_re, m_im = image[s, 0:PIX], image[s, PIX:]
            both_re = a_re * b_re + a_im * b_im
            both_im = a_re * b_im - a_im * b_re
            back_re = both_re * m_re - both_im * m_im
            back_im = both_re * m_im + both_im * m_re
            backs.append(jnp.concatenate([back_re, back_im], 0).astype(BF16))
        grads = []
        for grad in transforms(backward, backs, right):
            re, im = grad[:PIX], grad[PIX:]
            grad_re = re[:, :LANES] + im[:, LANES:]
            grad_im = im[:, :LANES] - re[:, LANES:]
            grads.append(jnp.concatenate([grad_re, grad_im], 0).astype(BF16))
        for s, grad in zip(subs, grads):
            stage[s] = grad
        for s in subs:
            pltpu.make_async_copy(stage.at[s], out.at[slot[s]], out_sems.at[s]).start()
        return carry

    count, ready = image.shape[0], image.shape[0] // len(images)
    for p, copy in enumerate(images):
        copy.wait()
        lax.fori_loop(p * ready // group, (p + 1) * ready // group, step, 0)

    def finished(s, carry):
        pltpu.make_async_copy(stage.at[s], out.at[slot[s]], out_sems.at[s]).wait()
        return carry

    lax.fori_loop(0, count, finished, 0)


def table_scratch(near, image):
    whole = (2 * near.shape[0],) + near.shape[1:]
    images = (2 * image.shape[0],) + image.shape[1:]
    return [
        pltpu.VMEM(whole, BF16),
        pltpu.SemaphoreType.DMA((2,)),
        pltpu.VMEM(images, F32),
        pltpu.SemaphoreType.DMA((4,)),
    ]


def patch_gradients(where, images, near, far, consts, slots, n_bt, n_freq):
    _, backward, right, spread_a, spread_b = consts
    count = 2 * images[0].shape[0]
    group = math.gcd(count // 4, 4)
    vmem, smem = pl.BlockSpec(memory_space=pltpu.VMEM), pl.BlockSpec(memory_space=pltpu.SMEM)
    return pl.pallas_call(
        lambda *refs: patch_kernel(group, n_bt, n_freq, *refs),
        out_shape=jax.ShapeDtypeStruct((slots, 2 * PIX, LANES), BF16),
        in_specs=[smem] * 4 + [pl.BlockSpec(memory_space=pl.ANY)] * 4 + [vmem] * 4,
        out_specs=pl.BlockSpec(memory_space=pl.ANY),
        scratch_shapes=table_scratch(near, images[0])
        + [pltpu.VMEM((count, 2 * PIX, LANES), BF16), pltpu.SemaphoreType.DMA((count,))],
        name="patch",
    )(*where, *images, near, far, backward, right, spread_a, spread_b)


def screen_kernel(
    group, n_bt, n_freq, me, slot, stations, slot_time, image_a, image_b, near, far,
    patches, forward, right, spread_a, spread_b, out_near, out_far,
    table, sems, image, image_sems, acc,
):
    chunk = 32
    copies = join_parts((near, far), table, sems, near.shape[0])
    copies += join_parts((image_a, image_b), image, image_sems, image_a.shape[0] // 2)
    rows = table_rows(n_bt, n_freq, me, stations, slot_time)

    def clear(i, carry):
        acc[pl.ds(i * chunk, chunk)] = jnp.zeros((chunk, PIX, LANES), F32)
        return carry

    lax.fori_loop(0, acc.shape[0] // chunk, clear, 0)
    for copy in copies:
        copy.wait()
    block = lax.broadcasted_iota(jnp.int32, (PIX, LANES), 1) // PIX

    def step(g, carry):
        terms = []
        subs = [g * group + k for k in range(group)]
        first_rows, second_rows = [[rows(w, s) for s in subs] for w in (0, 1)]
        first_screens = screens_of(table, [row for row, _ in first_rows], spread_a)
        second_screens = screens_of(table, [row for row, _ in second_rows], spread_b)
        skies = transforms(forward, [patches[slot[s]] for s in subs], right)
        for s, (a_re, a_im), (b_re, b_im), sky in zip(subs, first_screens, second_screens, skies):
            m_re, m_im = image[s, 0:PIX], image[s, PIX:]
            re, im = sky[:PIX], sky[PIX:]
            sky_re = re[:, :LANES] - im[:, LANES:]
            sky_im = re[:, LANES:] + im[:, :LANES]
            carry_re = b_re * m_re - b_im * m_im
            carry_im = b_re * m_im + b_im * m_re
            ga_re = sky_re * carry_re + sky_im * carry_im
            ga_im = sky_re * carry_im - sky_im * carry_re
            model_re = a_re * sky_re - a_im * sky_im
            model_im = a_re * sky_im + a_im * sky_re
            gb_re = m_re * model_re + m_im * model_im
            gb_im = m_re * model_im - m_im * model_re
            ta = jnp.where(
                block % 2 == 0,
                ga_re + pltpu.roll(ga_re, LANES - PIX, 1),
                ga_im + pltpu.roll(ga_im, PIX, 1),
            )
            ta = jnp.where(
                block == 1,
                pltpu.roll(ta, LANES - PIX, 1),
                jnp.where(block == 2, pltpu.roll(ta, PIX, 1), ta),
            )
            tb = jnp.where(
                block < 2,
                gb_re + pltpu.roll(gb_re, 2 * PIX, 1),
                gb_im + pltpu.roll(gb_im, 2 * PIX, 1),
            )
            terms.append((ta, tb))
        for (ta, tb), (_, first), (_, second) in zip(terms, first_rows, second_rows):
            acc[first] = acc[first] + ta
            acc[second] = acc[second] + tb
        return carry

    lax.fori_loop(0, image.shape[0] // group, step, 0)

    for start, out in ((0, out_near), (out_near.shape[0], out_far)):

        def give(i, carry, start=start, out=out):
            out[pl.ds(i * chunk, chunk)] = acc[pl.ds(start + i * chunk, chunk)].astype(BF16)
            return carry

        lax.fori_loop(0, out.shape[0] // chunk, give, 0)


def screen_gradients(where, images, patches, near, far, consts, n_bt, n_freq):
    forward, _, right, spread_a, spread_b = consts
    group = math.gcd(images[0].shape[0], 4)
    vmem, smem = pl.BlockSpec(memory_space=pltpu.VMEM), pl.BlockSpec(memory_space=pltpu.SMEM)
    scratch = table_scratch(near, images[0])
    return pl.pallas_call(
        lambda *refs: screen_kernel(group, n_bt, n_freq, *refs),
        out_shape=(jax.ShapeDtypeStruct(near.shape, BF16),) * 2,
        in_specs=[smem] * 4 + [pl.BlockSpec(memory_space=pl.ANY)] * 4 + [vmem] * 5,
        out_specs=(vmem,) * 2,
        scratch_shapes=scratch + [pltpu.VMEM(scratch[0].shape, F32)],
        name="screen",
    )(*where, *images, near, far, patches, forward, right, spread_a, spread_b)


def exchange(x, axis, groups=None):
    return lax.all_to_all(
        x, axis, split_axis=0, concat_axis=0, tiled=True, axis_index_groups=groups
    )


def ring_gather(x, n_z):
    def by(step):
        return [(2 * z + c, 2 * ((z + step) % n_z) + c) for z in range(n_z) for c in range(2)]

    blocks = [None] * n_z
    blocks[0] = up = down = x
    for k in range(1, n_z // 2 + 1):
        up = lax.ppermute(up, "freq", by(1))
        blocks[n_z - k] = up
        if k < n_z - k:
            down = lax.ppermute(down, "freq", by(-1))
            blocks[k] = down
    return jnp.stack(blocks)


def per_device(
    uv_grid, screens, residual, uv_coords, owner_tile, row_offset, column, stations, time_slot
):
    n_bt, n_freq = lax.axis_size("bt"), lax.axis_size("freq")
    n_z = n_freq // 2
    slots = n_bt * CAP
    consts = constant_tables()
    swap = [(f, f ^ 1) for f in range(n_freq)]
    same_core = [[2 * z + c for z in range(n_z)] for c in range(2)]
    row = TSLOTS * PIX
    mail, slot = make_mail(
        owner_tile[0, :, 0], row_offset[0], column[0], screens[:, 0], n_bt
    )
    me = lax.axis_index("freq").astype(jnp.int32).reshape(1)
    where = (me, slot, stations[0].T, time_slot[0])
    image_a = adjoint_images(residual[0], uv_coords[0], 0, 2)
    image_b = adjoint_images(residual[0], uv_coords[0], 1, 2)
    images = (image_a, image_b)
    mail = exchange(mail, "bt")
    asked = mail[:, row].astype(jnp.int32)
    near = ring_gather(mail[:, :row], n_z).reshape(n_z * n_bt * TSLOTS, PIX, LANES)
    far = lax.ppermute(near, "freq", swap)
    cut = cut_windows(asked, uv_grid[0])
    fetched = exchange(cut.reshape(n_bt, CAP, 2 * PIX, LANES), "bt")
    fetched = fetched.reshape(slots, 2 * PIX, LANES)
    grads = patch_gradients(where, images, near, far, consts, slots, n_bt, n_freq)
    returned = exchange(grads.reshape(n_bt, CAP, 2 * PIX, LANES), "bt")
    returned = returned.reshape(slots, 2 * PIX, LANES)
    terms, sent = screen_gradients(
        where, images, fetched, near, far, consts, n_bt, n_freq
    )
    came = lax.ppermute(sent, "freq", swap)
    part = (terms.astype(F32) + came.astype(F32)).astype(BF16)
    part = exchange(part.reshape(n_bt, n_z, TSLOTS, PIX, LANES), "bt")
    grid_grad = add_windows(asked, returned, *uv_grid.shape[1:])
    part = jnp.sum(part.astype(F32), 0).astype(BF16)
    screen_grad = finish(exchange(part, "freq", same_core))
    return grid_grad[None], screen_grad[:, None]


def solution(mesh):
    in_specs = (
        P("freq", None, "bt", None),
        P(None, ("bt", "freq"), None, None),
        P("freq", "bt", None, None),
        P("freq", "bt", None, None),
        P("freq", "bt", None),
        P("freq", "bt"),
        P("freq", "bt"),
        P("freq", "bt", None),
        P("freq", "bt"),
    )
    out_specs = (P("freq", None, "bt", None), P(None, ("bt", "freq"), None, None))

    return jax.shard_map(
        per_device, mesh=mesh, in_specs=in_specs, out_specs=out_specs, check_vma=False
    )
```

```python
import math

import jax
import jax.numpy as jnp
import numpy as np
from jax import lax
from jax.experimental import pallas as pl
from jax.experimental.pallas import tpu as pltpu
from jax.sharding import PartitionSpec as P


PIX = 32
TSLOTS = 2
LANES = 128
CAP = 8
F32 = jnp.float32
BF16 = jnp.bfloat16


def constant_tables():
    ramp = np.arange(PIX)
    angle = (ramp[:, None] * ramp[None, :] % PIX) * (2.0 * math.pi / PIX)
    cos_part = (np.cos(angle) / math.sqrt(PIX)).astype(np.float32)
    sin_part = (np.sin(angle) / math.sqrt(PIX)).astype(np.float32)
    forward = np.block([[cos_part, -sin_part], [sin_part, cos_part]])
    backward = np.block([[cos_part, sin_part], [-sin_part, cos_part]])
    eye = np.eye(4, dtype=np.float32)
    right = np.concatenate([np.kron(eye, cos_part), np.kron(eye, sin_part)], 1)
    block = np.eye(PIX, dtype=np.float32)

    def spread(picks):
        out = np.zeros((LANES, len(picks) * PIX), np.float32)
        for j, i in enumerate(picks):
            out[i * PIX : (i + 1) * PIX, j * PIX : (j + 1) * PIX] = block
        return out

    spread_first = spread([0, 0, 1, 1, 2, 2, 3, 3])
    spread_second = spread([0, 1, 0, 1, 2, 3, 2, 3])
    as_bf16 = [
        jnp.asarray(v, BF16) for v in (forward, backward, right, spread_first, spread_second)
    ]
    return as_bf16


def dot(a, b):
    return jnp.dot(a, b, preferred_element_type=F32)


def swap_blocks(x):
    rolled = [x] + [pltpu.roll(x, d * PIX, 1) for d in (1, 2, 3)]
    line = lax.broadcasted_iota(jnp.int32, x.shape, 0)
    block = lax.broadcasted_iota(jnp.int32, x.shape, 1) // PIX
    rows = []
    for a in range(4):
        d = (block - a + 4) % 4
        moved = rolled[0]
        for k in (1, 2, 3):
            moved = jnp.where(d == k, rolled[k], moved)
        rows.append(jnp.sum(jnp.where(block == line, moved, 0.0), 0, keepdims=True))
    return rows


def mail_kernel(
    n_bt, owner, row_offset, column, screens, mail, slot, fill, request, own,
):
    count = owner.shape[0]
    for i in range(n_bt):
        fill[i] = 0

    def step(s, carry):
        o = owner[s]
        n = fill[o]
        fill[o] = n + 1
        place = o * CAP + n
        slot[s] = place
        request[place] = row_offset[s] * 1024 + column[s]
        return carry

    lax.fori_loop(0, count, step, 0, unroll=4)
    for t in range(TSLOTS):
        table = screens[t].astype(F32)
        for high in range(PIX // 4):
            for a, line in enumerate(swap_blocks(table[:, high * LANES : (high + 1) * LANES])):
                x = t * PIX + high * 4 + a
                own[x : x + 1] = line
    every = own[...].astype(BF16)
    lane = lax.broadcasted_iota(jnp.int32, (16, LANES), 1)

    def address(j, carry):
        n = fill[j]
        line = jnp.where(lane == 3 * CAP, n, 0)
        for k in range(CAP):
            code = jnp.where(k < n, request[j * CAP + k], 0)
            for part, value in enumerate((code >> 10, (code >> 5) & 31, code & 31)):
                line = jnp.where(lane == part * CAP + k, value, line)
        mail[j] = jnp.concatenate([every, line.astype(F32).astype(BF16)], 0)
        return carry

    lax.fori_loop(0, n_bt, address, 0)


def make_mail(owners, row_offset, column, screens, n_bt):
    count = owners.shape[0]
    smem, vmem = pl.BlockSpec(memory_space=pltpu.SMEM), pl.BlockSpec(memory_space=pltpu.VMEM)
    rows = TSLOTS * PIX
    return pl.pallas_call(
        lambda *refs: mail_kernel(n_bt, *refs),
        out_shape=(
            jax.ShapeDtypeStruct((n_bt, rows + 16, LANES), BF16),
            jax.ShapeDtypeStruct((count,), jnp.int32),
        ),
        in_specs=[smem] * 3 + [vmem],
        out_specs=(vmem, smem),
        scratch_shapes=[
            pltpu.SMEM((n_bt,), jnp.int32),
            pltpu.SMEM((n_bt * CAP,), jnp.int32),
            pltpu.VMEM((rows, LANES), F32),
        ],
        name="mail",
    )(owners, row_offset, column, screens)


def finish_kernel(parts, out):
    total = jnp.sum(parts[...].astype(F32), 0)
    line = lax.broadcasted_iota(jnp.int32, (4, LANES), 0)
    for t in range(TSLOTS):
        for high in range(PIX // 4):
            rows = swap_blocks(total[t, high * 4 : high * 4 + 4])
            tile = jnp.broadcast_to(rows[0], (4, LANES))
            for a in (1, 2, 3):
                tile = jnp.where(line == a, jnp.broadcast_to(rows[a], (4, LANES)), tile)
            out[t, :, high * LANES : (high + 1) * LANES] = tile


def finish(parts):
    vmem = pl.BlockSpec(memory_space=pltpu.VMEM)
    return pl.pallas_call(
        finish_kernel,
        out_shape=jax.ShapeDtypeStruct((TSLOTS, 4, PIX * PIX), F32),
        in_specs=[vmem],
        out_specs=vmem,
        name="finish",
    )(parts)


def listed(asked, order):
    def step(j, n):
        for k in range(CAP):
            order[n + k] = j * CAP + k
        return n + asked[j, 3 * CAP]

    return lax.fori_loop(0, asked.shape[0], step, jnp.int32(0))


def corner(asked, i):
    j, k = i >> 3, i & 7
    return asked[j, k], asked[j, CAP + k] * PIX + asked[j, 2 * CAP + k]


def for_listed(n, group, body):
    def whole(g, carry):
        body([g * group + k for k in range(group)])
        return carry

    lax.fori_loop(0, n // group, whole, 0)

    def rest(i, carry):
        body([i])
        return carry

    lax.fori_loop(n // group * group, n, rest, 0)


def cut_kernel(asked, tile, out, wide, order, stage, sems):
    comps, rows, columns = tile.shape
    panels = columns // LANES
    for j in range(panels):
        wide[j] = tile[:, :, j * LANES : (j + 1) * LANES].astype(F32).reshape(comps * rows, LANES)
    n = listed(asked, order)
    line = lax.broadcasted_iota(jnp.int32, (LANES, LANES), 0)
    lane = lax.broadcasted_iota(jnp.int32, (LANES, LANES), 1)
    ahead = line - lane % PIX
    block = lax.broadcasted_iota(jnp.int32, (PIX, LANES), 1) // PIX

    def body(places):
        done = []
        for place in places:
            i = order[place]
            r, c0 = corner(asked, i)
            j, shift = c0 >> 7, c0 & (LANES - 1)
            after = jnp.minimum(j + 1, panels - 1)

            def rows_of(panel):
                return jnp.concatenate(
                    [wide[panel, pl.ds(c * rows + r, PIX), :] for c in range(comps)], 0
                ).astype(BF16)

            both = jnp.concatenate([rows_of(j), rows_of(after)], 1)
            pick = jnp.concatenate([ahead == shift, ahead + LANES == shift], 0)
            moved = dot(both, jnp.where(pick, 1.0, 0.0).astype(BF16))
            parts = []
            for ri in range(2):
                part = moved[ri * 128 : ri * 128 + PIX]
                for m in range(1, 4):
                    start = (ri * 4 + m) * PIX
                    part = jnp.where(block == m, moved[start : start + PIX], part)
                parts.append(part)
            done.append((i, jnp.concatenate(parts, 0).astype(BF16)))
        for i, piece in done:
            stage[i] = piece
        for i, piece in done:
            pltpu.make_async_copy(stage.at[i], out.at[i], sems.at[i]).start()

    for_listed(n, 4, body)

    def finished(g, carry):
        i = order[g]
        pltpu.make_async_copy(stage.at[i], out.at[i], sems.at[i]).wait()
        return carry

    lax.fori_loop(0, n, finished, 0)


def cut_windows(asked, tile):
    comps, rows, columns = tile.shape
    slots = asked.shape[0] * CAP
    return pl.pallas_call(
        cut_kernel,
        out_shape=jax.ShapeDtypeStruct((slots, 2 * PIX, LANES), BF16),
        in_specs=[pl.BlockSpec(memory_space=pltpu.SMEM), pl.BlockSpec(memory_space=pltpu.VMEM)],
        out_specs=pl.BlockSpec(memory_space=pl.ANY),
        scratch_shapes=[
            pltpu.VMEM((columns // LANES, comps * rows, LANES), F32),
            pltpu.SMEM((slots + CAP,), jnp.int32),
            pltpu.VMEM((slots, 2 * PIX, LANES), BF16),
            pltpu.SemaphoreType.DMA((slots,)),
        ],
        name="cut",
    )(asked, tile)


def add_kernel(asked, pieces, out, wide, order):
    comps, rows, columns = out.shape
    panels = columns // LANES
    for j in range(panels):
        wide[j] = jnp.zeros((comps * rows, LANES), F32)
    n = listed(asked, order)
    line = lax.broadcasted_iota(jnp.int32, (LANES, LANES), 0)
    lane = lax.broadcasted_iota(jnp.int32, (LANES, LANES), 1)
    ahead = lane - line % PIX
    block = lax.broadcasted_iota(jnp.int32, (PIX, LANES), 1) // PIX

    def body(places):
        spread = []
        for place in places:
            i = order[place]
            r, c0 = corner(asked, i)
            j, shift = c0 >> 7, c0 & (LANES - 1)
            piece = pieces[i].astype(F32)
            lines = []
            for ri in range(2):
                for m in range(4):
                    lines.append(jnp.where(block == m, piece[ri * PIX : (ri + 1) * PIX], 0.0))
            lines = jnp.concatenate(lines, 0).astype(BF16)
            pick = jnp.concatenate([ahead == shift, ahead + LANES == shift], 1)
            spread.append((r, j, shift, dot(lines, jnp.where(pick, 1.0, 0.0).astype(BF16))))
        for r, j, shift, moved in spread:
            for c in range(comps):
                at = pl.ds(c * rows + r, PIX)
                wide[j, at, :] = wide[j, at, :] + moved[c * PIX : (c + 1) * PIX, :LANES]
        for r, j, shift, moved in spread:

            @pl.when(shift > LANES - PIX)
            def _(r=r, j=j, moved=moved):
                for c in range(comps):
                    at = pl.ds(c * rows + r, PIX)
                    wide[j + 1, at, :] = wide[j + 1, at, :] + moved[c * PIX : (c + 1) * PIX, LANES:]

    for_listed(n, 4, body)
    for j in range(panels):
        out[:, :, j * LANES : (j + 1) * LANES] = wide[j].reshape(comps, rows, LANES)


def add_windows(asked, pieces, comps, rows, columns):
    slots = asked.shape[0] * CAP
    return pl.pallas_call(
        add_kernel,
        out_shape=jax.ShapeDtypeStruct((comps, rows, columns), F32),
        in_specs=[pl.BlockSpec(memory_space=pltpu.SMEM), pl.BlockSpec(memory_space=pltpu.VMEM)],
        out_specs=pl.BlockSpec(memory_space=pltpu.VMEM),
        scratch_shapes=[
            pltpu.VMEM((columns // LANES, comps * rows, LANES), F32),
            pltpu.SMEM((slots + CAP,), jnp.int32),
        ],
        name="add",
    )(asked, pieces)


def turn_waves(turns):
    part = turns - jnp.round(turns)
    z = part * part
    coef_sin = [(-1.0) ** k * math.pi ** (2 * k + 1) / math.factorial(2 * k + 1) for k in range(7)]
    coef_cos = [(-1.0) ** k * math.pi ** (2 * k) / math.factorial(2 * k) for k in range(8)]
    s = jnp.full_like(z, coef_sin[-1])
    for v in coef_sin[-2::-1]:
        s = s * z + v
    s = s * part
    c = jnp.full_like(z, coef_cos[-1])
    for v in coef_cos[-2::-1]:
        c = c * z + v
    return 1.0 - 2.0 * s * s, 2.0 * s * c


def image_kernel(group, vis, uv, out):
    samples = vis.shape[2]
    position = lax.broadcasted_iota(jnp.int32, (PIX, samples), 0).astype(F32) * (1.0 / PIX)

    def step(g, carry):
        done = []
        for k in range(group):
            s = g * group + k
            uv_rows = uv[s]
            x_cos, x_sin = turn_waves(position * uv_rows[0:1])
            y_cos, y_sin = turn_waves(position * uv_rows[1:2])
            wave_x = jnp.concatenate([x_cos, x_sin], 0).astype(BF16)
            y_cos, y_sin = y_cos.astype(BF16).astype(F32), y_sin.astype(BF16).astype(F32)
            rows = vis[s].astype(F32)
            weight_re, weight_im = [], []
            for m in range(4):
                re, im = rows[m : m + 1], rows[m + 4 : m + 5]
                weight_re.append(re * y_cos - im * y_sin)
                weight_im.append(re * y_sin + im * y_cos)
            weighted = jnp.concatenate(weight_re + weight_im, 0).astype(BF16)
            products = lax.dot_general(
                wave_x, weighted, (((1,), (1,)), ((), ())), preferred_element_type=F32
            )
            low, high = products[:PIX], products[PIX:]
            done.append((s, low[:, :LANES] - high[:, LANES:], low[:, LANES:] + high[:, :LANES]))
        for s, re, im in done:
            out[s, 0:PIX] = re
            out[s, PIX:] = im
        return carry

    lax.fori_loop(0, vis.shape[0] // group, step, 0)


def adjoint_images(vis, uv, part, parts):
    count = vis.shape[0] // parts
    group = math.gcd(count, 4)
    blocks = [
        pl.BlockSpec((count,) + x.shape[1:], lambda i: (part, 0, 0)) for x in (vis, uv)
    ]
    return pl.pallas_call(
        lambda *refs: image_kernel(group, *refs),
        out_shape=jax.ShapeDtypeStruct((count, 2 * PIX, LANES), F32),
        grid=(1,),
        in_specs=blocks,
        out_specs=pl.BlockSpec((count, 2 * PIX, LANES), lambda i: (0, 0, 0)),
        name="image",
    )(vis, uv)


def table_rows(n_bt, n_freq, me, stations, slot_time):
    n_z = n_freq // 2
    my_z, my_core = me[0] >> 1, me[0] & 1

    def row(which, s):
        station = stations[which, s]
        bt, freq = lax.div(station, n_freq), lax.rem(station, n_freq)
        half = jnp.where((freq & 1) == my_core, 0, n_bt * n_z)
        ahead = lax.rem((freq >> 1) - my_z + n_z, n_z)
        return (half + ahead * n_bt + bt) * TSLOTS + slot_time[s]

    return row


def join_parts(parts, whole, sems, chunk):
    copies = []
    for p, part in enumerate(parts):
        for c in range(0, part.shape[0], chunk):
            at = pl.ds(p * part.shape[0] + c, chunk)
            k = len(copies)
            copy = pltpu.make_async_copy(part.at[pl.ds(c, chunk)], whole.at[at], sems.at[k])
            copy.start()
            copies.append(copy)
    return copies


def screens_of(table, rows, spread):
    wide = dot(jnp.concatenate([table[row] for row in rows], 0), spread[...])
    at = [slice(k * PIX, (k + 1) * PIX) for k in range(len(rows))]
    return [(wide[k, :LANES], wide[k, LANES:]) for k in at]


def left_side(left, pieces):
    count = pieces.shape[1] // LANES
    inner = dot(left[...], pieces).astype(BF16)
    return jnp.concatenate([inner[:, k * LANES : (k + 1) * LANES] for k in range(count)], 0)


def right_side(lines, right):
    outer = dot(lines, right[...])
    return [outer[k : k + 2 * PIX] for k in range(0, lines.shape[0], 2 * PIX)]


def patch_kernel(
    group, n_bt, n_freq, me, slot, stations, slot_time, image_a, image_b, near, far,
    backward, right, spread_a, spread_b, out, table, sems, image, image_sems, stage, out_sems,
    backs, lows,
):
    copies = join_parts((near, far), table, sems, near.shape[0])
    images = join_parts((image_a, image_b), image, image_sems, image_a.shape[0] // 2)
    row = table_rows(n_bt, n_freq, me, stations, slot_time)
    for copy in copies + images[:1]:
        copy.wait()
    groups = image.shape[0] // group

    def back_side(g):
        subs = [g * group + k for k in range(group)]
        first_screens = screens_of(table, [row(0, s) for s in subs], spread_a)
        second_screens = screens_of(table, [row(1, s) for s in subs], spread_b)
        pieces = []
        for s, (a_re, a_im), (b_re, b_im) in zip(subs, first_screens, second_screens):
            m_re, m_im = image[s, 0:PIX], image[s, PIX:]
            both_re = a_re * b_re + a_im * b_im
            both_im = a_re * b_im - a_im * b_re
            back_re = both_re * m_re - both_im * m_im
            back_im = both_re * m_im + both_im * m_re
            pieces.append(jnp.concatenate([back_re, back_im], 0).astype(BF16))
        return jnp.concatenate(pieces, 1)

    lows[...] = left_side(backward, back_side(0))
    backs[...] = back_side(1)

    def step(g, carry):
        grads = []
        for grad in right_side(lows[...], right):
            re, im = grad[:PIX], grad[PIX:]
            grad_re = re[:, :LANES] + im[:, LANES:]
            grad_im = im[:, :LANES] - re[:, LANES:]
            grads.append(jnp.concatenate([grad_re, grad_im], 0).astype(BF16))
        low = left_side(backward, backs[...])
        back = back_side(jnp.minimum(g + 2, groups - 1))
        lows[...] = low
        backs[...] = back
        subs = [g * group + k for k in range(group)]
        for s, grad in zip(subs, grads):
            stage[s] = grad
        for s in subs:
            pltpu.make_async_copy(stage.at[s], out.at[slot[s]], out_sems.at[s]).start()
        return carry

    count, ready = image.shape[0], groups // len(images)
    for p in range(len(images)):
        if p + 1 < len(images):
            images[p + 1].wait()
        lax.fori_loop(p * ready, (p + 1) * ready, step, 0)

    def finished(s, carry):
        pltpu.make_async_copy(stage.at[s], out.at[slot[s]], out_sems.at[s]).wait()
        return carry

    lax.fori_loop(0, count, finished, 0)


def table_scratch(near, image):
    whole = (2 * near.shape[0],) + near.shape[1:]
    images = (2 * image.shape[0],) + image.shape[1:]
    return [
        pltpu.VMEM(whole, BF16),
        pltpu.SemaphoreType.DMA((2,)),
        pltpu.VMEM(images, F32),
        pltpu.SemaphoreType.DMA((4,)),
    ]


def patch_gradients(where, images, near, far, consts, slots, n_bt, n_freq):
    _, backward, right, spread_a, spread_b = consts
    count = 2 * images[0].shape[0]
    group = math.gcd(count // 4, 4)
    vmem, smem = pl.BlockSpec(memory_space=pltpu.VMEM), pl.BlockSpec(memory_space=pltpu.SMEM)
    return pl.pallas_call(
        lambda *refs: patch_kernel(group, n_bt, n_freq, *refs),
        out_shape=jax.ShapeDtypeStruct((slots, 2 * PIX, LANES), BF16),
        in_specs=[smem] * 4 + [pl.BlockSpec(memory_space=pl.ANY)] * 4 + [vmem] * 4,
        out_specs=pl.BlockSpec(memory_space=pl.ANY),
        scratch_shapes=table_scratch(near, images[0])
        + [
            pltpu.VMEM((count, 2 * PIX, LANES), BF16),
            pltpu.SemaphoreType.DMA((count,)),
            pltpu.VMEM((2 * PIX, group * LANES), BF16),
            pltpu.VMEM((group * 2 * PIX, LANES), BF16),
        ],
        name="patch",
    )(*where, *images, near, far, backward, right, spread_a, spread_b)


def screen_kernel(
    group, n_bt, n_freq, me, slot, stations, slot_time, image_a, image_b, near, far,
    patches, forward, right, spread_a, spread_b, out_near, out_far,
    table, sems, image, image_sems, acc, mids,
):
    chunk = 32
    copies = join_parts((near, far), table, sems, near.shape[0])
    copies += join_parts((image_a, image_b), image, image_sems, image_a.shape[0] // 2)
    row = table_rows(n_bt, n_freq, me, stations, slot_time)
    groups = image.shape[0] // group

    def clear(i, carry):
        acc[pl.ds(i * chunk, chunk)] = jnp.zeros((chunk, PIX, LANES), F32)
        return carry

    lax.fori_loop(0, acc.shape[0] // chunk, clear, 0)
    for copy in copies:
        copy.wait()
    block = lax.broadcasted_iota(jnp.int32, (PIX, LANES), 1) // PIX

    def begin(g):
        return left_side(
            forward, jnp.concatenate([patches[slot[g * group + k]] for k in range(group)], 1)
        )

    mids[...] = begin(0)

    def step(g, carry):
        terms = []
        subs = [g * group + k for k in range(group)]
        first_rows, second_rows = [[row(w, s) for s in subs] for w in (0, 1)]
        skies = right_side(mids[...], right)
        first_screens = screens_of(table, first_rows, spread_a)
        second_screens = screens_of(table, second_rows, spread_b)
        mid = begin(jnp.minimum(g + 1, groups - 1))
        for s, (a_re, a_im), (b_re, b_im), sky in zip(subs, first_screens, second_screens, skies):
            m_re, m_im = image[s, 0:PIX], image[s, PIX:]
            re, im = sky[:PIX], sky[PIX:]
            sky_re = re[:, :LANES] - im[:, LANES:]
            sky_im = re[:, LANES:] + im[:, :LANES]
            carry_re = b_re * m_re - b_im * m_im
            carry_im = b_re * m_im + b_im * m_re
            ga_re = sky_re * carry_re + sky_im * carry_im
            ga_im = sky_re * carry_im - sky_im * carry_re
            model_re = a_re * sky_re - a_im * sky_im
            model_im = a_re * sky_im + a_im * sky_re
            gb_re = m_re * model_re + m_im * model_im
            gb_im = m_re * model_im - m_im * model_re
            ta = jnp.where(
                block % 2 == 0,
                ga_re + pltpu.roll(ga_re, LANES - PIX, 1),
                ga_im + pltpu.roll(ga_im, PIX, 1),
            )
            ta = jnp.where(
                block == 1,
                pltpu.roll(ta, LANES - PIX, 1),
                jnp.where(block == 2, pltpu.roll(ta, PIX, 1), ta),
            )
            tb = jnp.where(
                block < 2,
                gb_re + pltpu.roll(gb_re, 2 * PIX, 1),
                gb_im + pltpu.roll(gb_im, 2 * PIX, 1),
            )
            terms.append((ta, tb))
        mids[...] = mid
        for (ta, tb), first, second in zip(terms, first_rows, second_rows):
            acc[first] = acc[first] + ta
            acc[second] = acc[second] + tb
        return carry

    lax.fori_loop(0, image.shape[0] // group, step, 0)

    for start, out in ((0, out_near), (out_near.shape[0], out_far)):

        def give(i, carry, start=start, out=out):
            out[pl.ds(i * chunk, chunk)] = acc[pl.ds(start + i * chunk, chunk)].astype(BF16)
            return carry

        lax.fori_loop(0, out.shape[0] // chunk, give, 0)


def screen_gradients(where, images, patches, near, far, consts, n_bt, n_freq):
    forward, _, right, spread_a, spread_b = consts
    group = math.gcd(images[0].shape[0], 4)
    vmem, smem = pl.BlockSpec(memory_space=pltpu.VMEM), pl.BlockSpec(memory_space=pltpu.SMEM)
    scratch = table_scratch(near, images[0])
    return pl.pallas_call(
        lambda *refs: screen_kernel(group, n_bt, n_freq, *refs),
        out_shape=(jax.ShapeDtypeStruct(near.shape, BF16),) * 2,
        in_specs=[smem] * 4 + [pl.BlockSpec(memory_space=pl.ANY)] * 4 + [vmem] * 5,
        out_specs=(vmem,) * 2,
        scratch_shapes=scratch
        + [pltpu.VMEM(scratch[0].shape, F32), pltpu.VMEM((group * 2 * PIX, LANES), BF16)],
        name="screen",
    )(*where, *images, near, far, patches, forward, right, spread_a, spread_b)


def exchange(x, axis):
    return lax.all_to_all(x, axis, split_axis=0, concat_axis=0, tiled=True)


def z_shift(n_z, step):
    return [(2 * z + c, 2 * ((z + step) % n_z) + c) for z in range(n_z) for c in range(2)]


def ring_gather(x, n_z):
    half = n_z // 2
    blocks = [None] * n_z
    blocks[0] = up = down = x
    for k in range(1, half):
        up = lax.ppermute(up, "freq", z_shift(n_z, 1))
        down = lax.ppermute(down, "freq", z_shift(n_z, -1))
        blocks[n_z - k], blocks[k] = up, down
    cut = x.shape[0] // 2
    up = lax.ppermute(up[:cut], "freq", z_shift(n_z, 1))
    down = lax.ppermute(down[cut:], "freq", z_shift(n_z, -1))
    blocks[half] = jnp.concatenate([up, down])
    return jnp.stack(blocks)


def ring_sum(mine, came, n_z):
    half, cut = n_z // 2, mine.shape[1] // 2

    def block(k, at=slice(None)):
        return mine[k, at].astype(F32) + came[k, at].astype(F32)

    up, down = block(half, slice(0, cut)).astype(BF16), block(half, slice(cut, None)).astype(BF16)
    up = lax.ppermute(up, "freq", z_shift(n_z, 1))
    down = lax.ppermute(down, "freq", z_shift(n_z, -1))
    for k in range(half - 1, 0, -1):
        next_up, next_down = block(k), block(n_z - k)
        if k == half - 1:
            zeros = jnp.zeros_like(up)
            up, down = jnp.concatenate([up, zeros]), jnp.concatenate([zeros, down])
        next_up = (next_up + up.astype(F32)).astype(BF16)
        next_down = (next_down + down.astype(F32)).astype(BF16)
        up = lax.ppermute(next_up, "freq", z_shift(n_z, 1))
        down = lax.ppermute(next_down, "freq", z_shift(n_z, -1))
    return (block(0) + up.astype(F32) + down.astype(F32)).astype(BF16)


def per_device(
    uv_grid, screens, residual, uv_coords, owner_tile, row_offset, column, stations, time_slot
):
    n_bt, n_freq = lax.axis_size("bt"), lax.axis_size("freq")
    n_z = n_freq // 2
    slots = n_bt * CAP
    consts = constant_tables()
    swap = [(f, f ^ 1) for f in range(n_freq)]
    row = TSLOTS * PIX
    mail, slot = make_mail(
        owner_tile[0, :, 0], row_offset[0], column[0], screens[:, 0], n_bt
    )
    me = lax.axis_index("freq").astype(jnp.int32).reshape(1)
    where = (me, slot, stations[0].T, time_slot[0])
    image_a = adjoint_images(residual[0], uv_coords[0], 0, 2)
    image_b = adjoint_images(residual[0], uv_coords[0], 1, 2)
    images = (image_a, image_b)
    mail = exchange(mail, "bt")
    asked = mail[:, row].astype(jnp.int32)
    near = ring_gather(mail[:, :row], n_z).reshape(n_z * n_bt * TSLOTS, PIX, LANES)
    far = lax.ppermute(near, "freq", swap)
    cut = cut_windows(asked, uv_grid[0])
    fetched = exchange(cut.reshape(n_bt, CAP, 2 * PIX, LANES), "bt")
    fetched = fetched.reshape(slots, 2 * PIX, LANES)
    grads = patch_gradients(where, images, near, far, consts, slots, n_bt, n_freq)
    returned = exchange(grads.reshape(n_bt, CAP, 2 * PIX, LANES), "bt")
    returned = returned.reshape(slots, 2 * PIX, LANES)
    terms, sent = screen_gradients(
        where, images, fetched, near, far, consts, n_bt, n_freq
    )
    came = lax.ppermute(sent, "freq", swap)
    blocks = (n_z, n_bt, TSLOTS * PIX, LANES)
    part = ring_sum(terms.reshape(blocks), came.reshape(blocks), n_z)
    part = exchange(part, "bt")
    grid_grad = add_windows(asked, returned, *uv_grid.shape[1:])
    screen_grad = finish(part.reshape(n_bt, TSLOTS, PIX, LANES))
    return grid_grad[None], screen_grad[:, None]


def solution(mesh):
    in_specs = (
        P("freq", None, "bt", None),
        P(None, ("bt", "freq"), None, None),
        P("freq", "bt", None, None),
        P("freq", "bt", None, None),
        P("freq", "bt", None),
        P("freq", "bt"),
        P("freq", "bt"),
        P("freq", "bt", None),
        P("freq", "bt"),
    )
    out_specs = (P("freq", None, "bt", None), P(None, ("bt", "freq"), None, None))

    return jax.shard_map(
        per_device, mesh=mesh, in_specs=in_specs, out_specs=out_specs, check_vma=False
    )
```

```python
import math

import jax
import jax.numpy as jnp
import numpy as np
from jax import lax
from jax.experimental import pallas as pl
from jax.experimental.pallas import tpu as pltpu
from jax.sharding import PartitionSpec as P


PIX = 32
TSLOTS = 2
LANES = 128
CAP = 8
F32 = jnp.float32
BF16 = jnp.bfloat16


def constant_tables():
    ramp = np.arange(PIX)
    angle = (ramp[:, None] * ramp[None, :] % PIX) * (2.0 * math.pi / PIX)
    cos_part = (np.cos(angle) / math.sqrt(PIX)).astype(np.float32)
    sin_part = (np.sin(angle) / math.sqrt(PIX)).astype(np.float32)
    forward = np.block([[cos_part, -sin_part], [sin_part, cos_part]])
    backward = np.block([[cos_part, sin_part], [-sin_part, cos_part]])
    eye = np.eye(4, dtype=np.float32)
    right = np.concatenate([np.kron(eye, cos_part), np.kron(eye, sin_part)], 1)
    block = np.eye(PIX, dtype=np.float32)

    def spread(picks):
        out = np.zeros((LANES, len(picks) * PIX), np.float32)
        for j, i in enumerate(picks):
            out[i * PIX : (i + 1) * PIX, j * PIX : (j + 1) * PIX] = block
        return out

    spread_first = spread([0, 0, 1, 1, 2, 2, 3, 3])
    spread_second = spread([0, 1, 0, 1, 2, 3, 2, 3])
    as_bf16 = [
        jnp.asarray(v, BF16) for v in (forward, backward, right, spread_first, spread_second)
    ]
    return as_bf16


def dot(a, b):
    return jnp.dot(a, b, preferred_element_type=F32)


def swap_blocks(x):
    rolled = [x] + [pltpu.roll(x, d * PIX, 1) for d in (1, 2, 3)]
    line = lax.broadcasted_iota(jnp.int32, x.shape, 0)
    block = lax.broadcasted_iota(jnp.int32, x.shape, 1) // PIX
    rows = []
    for a in range(4):
        d = (block - a + 4) % 4
        moved = rolled[0]
        for k in (1, 2, 3):
            moved = jnp.where(d == k, rolled[k], moved)
        rows.append(jnp.sum(jnp.where(block == line, moved, 0.0), 0, keepdims=True))
    return rows


def mail_kernel(
    n_bt, owner, row_offset, column, screens, mail, slot, fill, request, own,
):
    count = owner.shape[0]
    for i in range(n_bt):
        fill[i] = 0

    def step(s, carry):
        o = owner[s]
        n = fill[o]
        fill[o] = n + 1
        place = o * CAP + n
        slot[s] = place
        request[place] = row_offset[s] * 1024 + column[s]
        return carry

    lax.fori_loop(0, count, step, 0, unroll=4)
    for t in range(TSLOTS):
        table = screens[t].astype(F32)
        for high in range(PIX // 4):
            for a, line in enumerate(swap_blocks(table[:, high * LANES : (high + 1) * LANES])):
                x = t * PIX + high * 4 + a
                own[x : x + 1] = line
    every = own[...].astype(BF16)
    lane = lax.broadcasted_iota(jnp.int32, (16, LANES), 1)

    def address(j, carry):
        n = fill[j]
        line = jnp.where(lane == 3 * CAP, n, 0)
        for k in range(CAP):
            code = jnp.where(k < n, request[j * CAP + k], 0)
            for part, value in enumerate((code >> 10, (code >> 5) & 31, code & 31)):
                line = jnp.where(lane == part * CAP + k, value, line)
        mail[j] = jnp.concatenate([every, line.astype(F32).astype(BF16)], 0)
        return carry

    lax.fori_loop(0, n_bt, address, 0)


def make_mail(owners, row_offset, column, screens, n_bt):
    count = owners.shape[0]
    smem, vmem = pl.BlockSpec(memory_space=pltpu.SMEM), pl.BlockSpec(memory_space=pltpu.VMEM)
    rows = TSLOTS * PIX
    return pl.pallas_call(
        lambda *refs: mail_kernel(n_bt, *refs),
        out_shape=(
            jax.ShapeDtypeStruct((n_bt, rows + 16, LANES), BF16),
            jax.ShapeDtypeStruct((count,), jnp.int32),
        ),
        in_specs=[smem] * 3 + [vmem],
        out_specs=(vmem, smem),
        scratch_shapes=[
            pltpu.SMEM((n_bt,), jnp.int32),
            pltpu.SMEM((n_bt * CAP,), jnp.int32),
            pltpu.VMEM((rows, LANES), F32),
        ],
        name="mail",
    )(owners, row_offset, column, screens)


def finish_kernel(parts, out):
    total = jnp.sum(parts[...].astype(F32), 0)
    line = lax.broadcasted_iota(jnp.int32, (4, LANES), 0)
    for t in range(TSLOTS):
        for high in range(PIX // 4):
            rows = swap_blocks(total[t, high * 4 : high * 4 + 4])
            tile = jnp.broadcast_to(rows[0], (4, LANES))
            for a in (1, 2, 3):
                tile = jnp.where(line == a, jnp.broadcast_to(rows[a], (4, LANES)), tile)
            out[t, :, high * LANES : (high + 1) * LANES] = tile


def finish(parts):
    vmem = pl.BlockSpec(memory_space=pltpu.VMEM)
    return pl.pallas_call(
        finish_kernel,
        out_shape=jax.ShapeDtypeStruct((TSLOTS, 4, PIX * PIX), F32),
        in_specs=[vmem],
        out_specs=vmem,
        name="finish",
    )(parts)


def listed(asked, order):
    def step(j, n):
        for k in range(CAP):
            order[n + k] = j * CAP + k
        return n + asked[j, 3 * CAP]

    return lax.fori_loop(0, asked.shape[0], step, jnp.int32(0))


def corner(asked, i):
    j, k = i >> 3, i & 7
    return asked[j, k], asked[j, CAP + k] * PIX + asked[j, 2 * CAP + k]


def for_listed(n, body):
    done = 0
    for group in (8, 4, 1):

        def some(g, carry, group=group, done=done):
            body([done + g * group + k for k in range(group)])
            return carry

        count = (n - done) // group
        lax.fori_loop(0, count, some, 0)
        done = done + count * group


HALF = LANES // 2


def panel_of(c0, panels):
    p = jnp.minimum(c0 >> 6, panels - 1)
    return p, c0 - p * HALF


def cut_kernel(asked, tile, out, wide, order, stage, sems):
    comps, rows, columns = tile.shape
    panels = wide.shape[0]
    low = lax.broadcasted_iota(jnp.int32, (comps * rows, LANES), 1) < HALF
    before = None
    for j in range(columns // LANES):
        whole = tile[:, :, j * LANES : (j + 1) * LANES].astype(F32).reshape(comps * rows, LANES)
        wide[2 * j] = whole
        turned = pltpu.roll(whole, HALF, 1)
        if before is not None:
            wide[2 * j - 1] = jnp.where(low, before, turned)
        before = turned
    n = listed(asked, order)
    line = lax.broadcasted_iota(jnp.int32, (LANES, LANES), 0)
    lane = lax.broadcasted_iota(jnp.int32, (LANES, LANES), 1)
    ahead = line - lane % PIX
    block = lax.broadcasted_iota(jnp.int32, (PIX, LANES), 1) // PIX

    def body(places):
        done = []
        for place in places:
            i = order[place]
            r, c0 = corner(asked, i)
            p, shift = panel_of(c0, panels)
            lines = jnp.concatenate(
                [wide[p, pl.ds(c * rows + r, PIX), :] for c in range(comps)], 0
            ).astype(BF16)
            moved = dot(lines, jnp.where(ahead == shift, 1.0, 0.0).astype(BF16))
            parts = []
            for ri in range(2):
                part = moved[ri * 128 : ri * 128 + PIX]
                for m in range(1, 4):
                    start = (ri * 4 + m) * PIX
                    part = jnp.where(block == m, moved[start : start + PIX], part)
                parts.append(part)
            done.append((i, jnp.concatenate(parts, 0).astype(BF16)))
        for i, piece in done:
            stage[i] = piece
        for i, piece in done:
            pltpu.make_async_copy(stage.at[i], out.at[i], sems.at[i]).start()

    for_listed(n, body)

    def finished(g, carry):
        i = order[g]
        pltpu.make_async_copy(stage.at[i], out.at[i], sems.at[i]).wait()
        return carry

    lax.fori_loop(0, n, finished, 0)


def cut_windows(asked, tile):
    comps, rows, columns = tile.shape
    slots = asked.shape[0] * CAP
    return pl.pallas_call(
        cut_kernel,
        out_shape=jax.ShapeDtypeStruct((slots, 2 * PIX, LANES), BF16),
        in_specs=[pl.BlockSpec(memory_space=pltpu.SMEM), pl.BlockSpec(memory_space=pltpu.VMEM)],
        out_specs=pl.BlockSpec(memory_space=pl.ANY),
        scratch_shapes=[
            pltpu.VMEM((columns // HALF - 1, comps * rows, LANES), F32),
            pltpu.SMEM((slots + CAP,), jnp.int32),
            pltpu.VMEM((slots, 2 * PIX, LANES), BF16),
            pltpu.SemaphoreType.DMA((slots,)),
        ],
        name="cut",
    )(asked, tile)


def add_kernel(asked, pieces, out, wide, order):
    comps, rows, columns = out.shape
    panels = wide.shape[0]
    for p in range(panels):
        wide[p] = jnp.zeros((comps * rows, LANES), F32)
    n = listed(asked, order)
    line = lax.broadcasted_iota(jnp.int32, (LANES, LANES), 0)
    lane = lax.broadcasted_iota(jnp.int32, (LANES, LANES), 1)
    ahead = lane - line % PIX
    block = lax.broadcasted_iota(jnp.int32, (PIX, LANES), 1) // PIX

    def body(places):
        spread = []
        for place in places:
            i = order[place]
            r, c0 = corner(asked, i)
            p, shift = panel_of(c0, panels)
            piece = pieces[i].astype(F32)
            lines = []
            for ri in range(2):
                for m in range(4):
                    lines.append(jnp.where(block == m, piece[ri * PIX : (ri + 1) * PIX], 0.0))
            lines = jnp.concatenate(lines, 0).astype(BF16)
            spread.append((r, p, dot(lines, jnp.where(ahead == shift, 1.0, 0.0).astype(BF16))))
        for r, p, moved in spread:
            sums = []
            for c in range(comps):
                at = pl.ds(c * rows + r, PIX)
                sums.append((at, wide[p, at, :] + moved[c * PIX : (c + 1) * PIX]))
            for at, total in sums:
                wide[p, at, :] = total

    for_listed(n, body)
    low = lax.broadcasted_iota(jnp.int32, (comps * rows, LANES), 1) < HALF
    before = jnp.zeros((comps * rows, LANES), F32)
    for j in range(columns // LANES):
        if 2 * j + 1 < panels:
            turned = pltpu.roll(wide[2 * j + 1], HALF, 1)
        else:
            turned = jnp.zeros((comps * rows, LANES), F32)
        total = wide[2 * j] + jnp.where(low, before, turned)
        out[:, :, j * LANES : (j + 1) * LANES] = total.reshape(comps, rows, LANES)
        before = turned


def add_windows(asked, pieces, comps, rows, columns):
    slots = asked.shape[0] * CAP
    return pl.pallas_call(
        add_kernel,
        out_shape=jax.ShapeDtypeStruct((comps, rows, columns), F32),
        in_specs=[pl.BlockSpec(memory_space=pltpu.SMEM), pl.BlockSpec(memory_space=pltpu.VMEM)],
        out_specs=pl.BlockSpec(memory_space=pltpu.VMEM),
        scratch_shapes=[
            pltpu.VMEM((columns // HALF - 1, comps * rows, LANES), F32),
            pltpu.SMEM((slots + CAP,), jnp.int32),
        ],
        name="add",
    )(asked, pieces)


def turn_waves(turns):
    part = turns - jnp.round(turns)
    z = part * part
    coef_sin = [(-1.0) ** k * math.pi ** (2 * k + 1) / math.factorial(2 * k + 1) for k in range(7)]
    coef_cos = [(-1.0) ** k * math.pi ** (2 * k) / math.factorial(2 * k) for k in range(8)]
    s = jnp.full_like(z, coef_sin[-1])
    for v in coef_sin[-2::-1]:
        s = s * z + v
    s = s * part
    c = jnp.full_like(z, coef_cos[-1])
    for v in coef_cos[-2::-1]:
        c = c * z + v
    return 1.0 - 2.0 * s * s, 2.0 * s * c


def image_kernel(group, vis, uv, out):
    samples = vis.shape[2]
    position = lax.broadcasted_iota(jnp.int32, (PIX, samples), 0).astype(F32) * (1.0 / PIX)

    def step(g, carry):
        done = []
        for k in range(group):
            s = g * group + k
            uv_rows = uv[s]
            x_cos, x_sin = turn_waves(position * uv_rows[0:1])
            y_cos, y_sin = turn_waves(position * uv_rows[1:2])
            wave_x = jnp.concatenate([x_cos, x_sin], 0).astype(BF16)
            y_cos, y_sin = y_cos.astype(BF16).astype(F32), y_sin.astype(BF16).astype(F32)
            rows = vis[s].astype(F32)
            weight_re, weight_im = [], []
            for m in range(4):
                re, im = rows[m : m + 1], rows[m + 4 : m + 5]
                weight_re.append(re * y_cos - im * y_sin)
                weight_im.append(re * y_sin + im * y_cos)
            weighted = jnp.concatenate(weight_re + weight_im, 0).astype(BF16)
            products = lax.dot_general(
                wave_x, weighted, (((1,), (1,)), ((), ())), preferred_element_type=F32
            )
            low, high = products[:PIX], products[PIX:]
            done.append((s, low[:, :LANES] - high[:, LANES:], low[:, LANES:] + high[:, :LANES]))
        for s, re, im in done:
            out[s, 0:PIX] = re
            out[s, PIX:] = im
        return carry

    lax.fori_loop(0, vis.shape[0] // group, step, 0)


def adjoint_images(vis, uv, part, parts):
    count = vis.shape[0] // parts
    group = math.gcd(count, 4)
    blocks = [
        pl.BlockSpec((count,) + x.shape[1:], lambda i: (part, 0, 0)) for x in (vis, uv)
    ]
    return pl.pallas_call(
        lambda *refs: image_kernel(group, *refs),
        out_shape=jax.ShapeDtypeStruct((count, 2 * PIX, LANES), F32),
        grid=(1,),
        in_specs=blocks,
        out_specs=pl.BlockSpec((count, 2 * PIX, LANES), lambda i: (0, 0, 0)),
        name="image",
    )(vis, uv)


def table_rows(n_bt, n_freq, me, stations, slot_time):
    n_z = n_freq // 2
    my_z, my_core = me[0] >> 1, me[0] & 1

    def row(which, s):
        station = stations[which, s]
        bt, freq = lax.div(station, n_freq), lax.rem(station, n_freq)
        half = jnp.where((freq & 1) == my_core, 0, n_bt * n_z)
        ahead = lax.rem((freq >> 1) - my_z + n_z, n_z)
        return (half + ahead * n_bt + bt) * TSLOTS + slot_time[s]

    return row


def join_parts(parts, whole, sems, chunk):
    copies = []
    for p, part in enumerate(parts):
        for c in range(0, part.shape[0], chunk):
            at = pl.ds(p * part.shape[0] + c, chunk)
            k = len(copies)
            copy = pltpu.make_async_copy(part.at[pl.ds(c, chunk)], whole.at[at], sems.at[k])
            copy.start()
            copies.append(copy)
    return copies


def screens_of(lines, spread):
    wide = dot(jnp.concatenate(lines, 0), spread[...])
    at = [slice(k * PIX, (k + 1) * PIX) for k in range(len(lines))]
    return [(wide[k, :LANES], wide[k, LANES:]) for k in at]


def left_side(left, pieces):
    count = pieces.shape[1] // LANES
    inner = dot(left[...], pieces).astype(BF16)
    return jnp.concatenate([inner[:, k * LANES : (k + 1) * LANES] for k in range(count)], 0)


def right_side(lines, right):
    outer = dot(lines, right[...])
    return [outer[k : k + 2 * PIX] for k in range(0, lines.shape[0], 2 * PIX)]


def patch_kernel(
    group, n_bt, n_freq, me, slot, stations, slot_time, image_a, image_b, near, far,
    backward, right, spread_a, spread_b, out, used, table, sems, image, image_sems,
    stage, out_sems, backs, lows, lines, line_sems,
):
    copies = join_parts((near, far), table, sems, near.shape[0])
    images = join_parts((image_a, image_b), image, image_sems, image_a.shape[0] // 2)
    row = table_rows(n_bt, n_freq, me, stations, slot_time)
    for copy in copies + images[:1]:
        copy.wait()
    groups = image.shape[0] // group

    def back_side(g):
        subs = [g * group + k for k in range(group)]
        first_lines = [table[row(0, s)] for s in subs]
        second_lines = [table[row(1, s)] for s in subs]
        first_screens = screens_of(first_lines, spread_a)
        second_screens = screens_of(second_lines, spread_b)
        pieces = []
        for s, (a_re, a_im), (b_re, b_im) in zip(subs, first_screens, second_screens):
            m_re, m_im = image[s, 0:PIX], image[s, PIX:]
            both_re = a_re * b_re + a_im * b_im
            both_im = a_re * b_im - a_im * b_re
            back_re = both_re * m_re - both_im * m_im
            back_im = both_re * m_im + both_im * m_re
            pieces.append(jnp.concatenate([back_re, back_im], 0).astype(BF16))
        for s, a, b in zip(subs, first_lines, second_lines):
            lines[s] = jnp.concatenate([a, b], 0)
        return jnp.concatenate(pieces, 1)

    def hand_on(g):
        at = pl.ds(g * group, group)
        return pltpu.make_async_copy(lines.at[at], used.at[at], line_sems.at[g])

    lows[...] = left_side(backward, back_side(0))
    backs[...] = back_side(1)

    def step(g, carry):
        grads = []
        for grad in right_side(lows[...], right):
            re, im = grad[:PIX], grad[PIX:]
            grad_re = re[:, :LANES] + im[:, LANES:]
            grad_im = im[:, :LANES] - re[:, LANES:]
            grads.append(jnp.concatenate([grad_re, grad_im], 0).astype(BF16))
        low = left_side(backward, backs[...])
        back = back_side(jnp.minimum(g + 2, groups - 1))
        lows[...] = low
        backs[...] = back
        subs = [g * group + k for k in range(group)]
        for s, grad in zip(subs, grads):
            stage[s] = grad
        for s in subs:
            pltpu.make_async_copy(stage.at[s], out.at[slot[s]], out_sems.at[s]).start()
        hand_on(g).start()
        return carry

    count, ready = image.shape[0], groups // len(images)
    for p in range(len(images)):
        if p + 1 < len(images):
            images[p + 1].wait()
        lax.fori_loop(p * ready, (p + 1) * ready, step, 0)

    def finished(s, carry):
        pltpu.make_async_copy(stage.at[s], out.at[slot[s]], out_sems.at[s]).wait()
        return carry

    lax.fori_loop(0, count, finished, 0)
    for g in range(groups):
        hand_on(g).wait()


def patch_gradients(where, images, near, far, consts, slots, n_bt, n_freq):
    _, backward, right, spread_a, spread_b = consts
    count = 2 * images[0].shape[0]
    group = math.gcd(count // 4, 4)
    vmem, smem = pl.BlockSpec(memory_space=pltpu.VMEM), pl.BlockSpec(memory_space=pltpu.SMEM)
    half = near.shape[0]
    return pl.pallas_call(
        lambda *refs: patch_kernel(group, n_bt, n_freq, *refs),
        out_shape=(
            jax.ShapeDtypeStruct((slots, 2 * PIX, LANES), BF16),
            jax.ShapeDtypeStruct((count, 2 * PIX, LANES), BF16),
        ),
        in_specs=[smem] * 4 + [pl.BlockSpec(memory_space=pl.ANY)] * 4 + [vmem] * 4,
        out_specs=(pl.BlockSpec(memory_space=pl.ANY),) * 2,
        scratch_shapes=[
            pltpu.VMEM((2 * half,) + near.shape[1:], BF16),
            pltpu.SemaphoreType.DMA((2,)),
            pltpu.VMEM((count, 2 * PIX, LANES), F32),
            pltpu.SemaphoreType.DMA((4,)),
            pltpu.VMEM((count, 2 * PIX, LANES), BF16),
            pltpu.SemaphoreType.DMA((count,)),
            pltpu.VMEM((2 * PIX, group * LANES), BF16),
            pltpu.VMEM((group * 2 * PIX, LANES), BF16),
            pltpu.VMEM((count, 2 * PIX, LANES), BF16),
            pltpu.SemaphoreType.DMA((count // group,)),
        ],
        name="patch",
    )(*where, *images, near, far, backward, right, spread_a, spread_b)


def screen_kernel(
    group, n_bt, n_freq, me, slot, stations, slot_time, image_a, image_b, used,
    patches, forward, right, spread_a, spread_b, out_near, out_far,
    lines, line_sems, image, image_sems, window, window_sems, acc, mids, stage, out_sems,
):
    chunk = 32
    count = image.shape[0]
    line_copies = join_parts((used,), lines, line_sems, count // 4)
    image_copies = join_parts((image_a, image_b), image, image_sems, count // 4)

    def window_copy(s):
        return pltpu.make_async_copy(patches.at[slot[s]], window.at[s], window_sems.at[s])

    def ask(s, carry):
        window_copy(s).start()
        return carry

    lax.fori_loop(0, count, ask, 0)

    def ready(p):
        line_copies[p].wait()
        image_copies[p].wait()

        def have(s, carry):
            window_copy(s).wait()
            return carry

        lax.fori_loop(p * count // 4, (p + 1) * count // 4, have, 0)

    row = table_rows(n_bt, n_freq, me, stations, slot_time)
    groups = count // group

    def clear(i, carry):
        acc[pl.ds(i * chunk, chunk)] = jnp.zeros((chunk, PIX, LANES), F32)
        return carry

    lax.fori_loop(0, acc.shape[0] // chunk, clear, 0)
    ready(0)
    block = lax.broadcasted_iota(jnp.int32, (PIX, LANES), 1) // PIX

    def begin(g):
        return left_side(
            forward, jnp.concatenate([window[g * group + k] for k in range(group)], 1)
        )

    mids[...] = begin(0)

    def step(g, carry):
        terms = []
        subs = [g * group + k for k in range(group)]
        first_rows, second_rows = [[row(w, s) for s in subs] for w in (0, 1)]
        skies = right_side(mids[...], right)
        first_screens = screens_of([lines[s, 0:PIX] for s in subs], spread_a)
        second_screens = screens_of([lines[s, PIX:] for s in subs], spread_b)
        mid = begin(jnp.minimum(g + 1, groups - 1))
        for s, (a_re, a_im), (b_re, b_im), sky in zip(subs, first_screens, second_screens, skies):
            m_re, m_im = image[s, 0:PIX], image[s, PIX:]
            re, im = sky[:PIX], sky[PIX:]
            sky_re = re[:, :LANES] - im[:, LANES:]
            sky_im = re[:, LANES:] + im[:, :LANES]
            carry_re = b_re * m_re - b_im * m_im
            carry_im = b_re * m_im + b_im * m_re
            ga_re = sky_re * carry_re + sky_im * carry_im
            ga_im = sky_re * carry_im - sky_im * carry_re
            model_re = a_re * sky_re - a_im * sky_im
            model_im = a_re * sky_im + a_im * sky_re
            gb_re = m_re * model_re + m_im * model_im
            gb_im = m_re * model_im - m_im * model_re
            ta = jnp.where(
                block % 2 == 0,
                ga_re + pltpu.roll(ga_re, LANES - PIX, 1),
                ga_im + pltpu.roll(ga_im, PIX, 1),
            )
            ta = jnp.where(
                block == 1,
                pltpu.roll(ta, LANES - PIX, 1),
                jnp.where(block == 2, pltpu.roll(ta, PIX, 1), ta),
            )
            tb = jnp.where(
                block < 2,
                gb_re + pltpu.roll(gb_re, 2 * PIX, 1),
                gb_im + pltpu.roll(gb_im, 2 * PIX, 1),
            )
            terms.append((ta, tb))
        mids[...] = mid
        for (ta, tb), first, second in zip(terms, first_rows, second_rows):
            acc[first] = acc[first] + ta
            acc[second] = acc[second] + tb
        return carry

    for p in range(4):
        if p + 1 < 4:
            ready(p + 1)
        lax.fori_loop(p * groups // 4, (p + 1) * groups // 4, step, 0)
    copies = []
    half = out_far.shape[0]
    for start, out in ((half, out_far), (0, out_near)):
        for i in range(0, half, chunk):
            at = pl.ds(start + i, chunk)
            stage[at] = acc[at].astype(BF16)
            copy = pltpu.make_async_copy(
                stage.at[at], out.at[pl.ds(i, chunk)], out_sems.at[len(copies)]
            )
            copy.start()
            copies.append(copy)
    for copy in copies:
        copy.wait()


def screen_gradients(where, images, patches, used, rows, consts, n_bt, n_freq):
    forward, _, right, spread_a, spread_b = consts
    count = used.shape[0]
    group = math.gcd(count // 4, 4)
    vmem, smem = pl.BlockSpec(memory_space=pltpu.VMEM), pl.BlockSpec(memory_space=pltpu.SMEM)
    sums = jax.ShapeDtypeStruct((rows, PIX, LANES), BF16)
    return pl.pallas_call(
        lambda *refs: screen_kernel(group, n_bt, n_freq, *refs),
        out_shape=(sums, sums),
        in_specs=[smem] * 4 + [pl.BlockSpec(memory_space=pl.ANY)] * 4 + [vmem] * 4,
        out_specs=(pl.BlockSpec(memory_space=pl.ANY),) * 2,
        scratch_shapes=[
            pltpu.VMEM((count, 2 * PIX, LANES), BF16),
            pltpu.SemaphoreType.DMA((4,)),
            pltpu.VMEM((count, 2 * PIX, LANES), F32),
            pltpu.SemaphoreType.DMA((4,)),
            pltpu.VMEM((count, 2 * PIX, LANES), BF16),
            pltpu.SemaphoreType.DMA((count,)),
            pltpu.VMEM((2 * rows, PIX, LANES), F32),
            pltpu.VMEM((group * 2 * PIX, LANES), BF16),
            pltpu.VMEM((2 * rows, PIX, LANES), BF16),
            pltpu.SemaphoreType.DMA((2 * rows // 32,)),
        ],
        name="screen",
    )(*where, *images, used, patches, forward, right, spread_a, spread_b)


def exchange(x, axis):
    return lax.all_to_all(x, axis, split_axis=0, concat_axis=0, tiled=True)


def z_shift(n_z, step):
    return [(2 * z + c, 2 * ((z + step) % n_z) + c) for z in range(n_z) for c in range(2)]


def ring_gather(x, n_z):
    half = n_z // 2
    blocks = [None] * n_z
    blocks[0] = up = down = x
    for k in range(1, half):
        up = lax.ppermute(up, "freq", z_shift(n_z, 1))
        down = lax.ppermute(down, "freq", z_shift(n_z, -1))
        blocks[n_z - k], blocks[k] = up, down
    cut = x.shape[0] // 2
    up = lax.ppermute(up[:cut], "freq", z_shift(n_z, 1))
    down = lax.ppermute(down[cut:], "freq", z_shift(n_z, -1))
    blocks[half] = jnp.concatenate([up, down])
    return jnp.stack(blocks)


def ring_sum(mine, came, n_z):
    half, cut = n_z // 2, mine.shape[1] // 2

    def block(k, at=slice(None)):
        return mine[k, at].astype(F32) + came[k, at].astype(F32)

    up, down = block(half, slice(0, cut)).astype(BF16), block(half, slice(cut, None)).astype(BF16)
    up = lax.ppermute(up, "freq", z_shift(n_z, 1))
    down = lax.ppermute(down, "freq", z_shift(n_z, -1))
    for k in range(half - 1, 0, -1):
        next_up, next_down = block(k), block(n_z - k)
        if k == half - 1:
            zeros = jnp.zeros_like(up)
            up, down = jnp.concatenate([up, zeros]), jnp.concatenate([zeros, down])
        next_up = (next_up + up.astype(F32)).astype(BF16)
        next_down = (next_down + down.astype(F32)).astype(BF16)
        up = lax.ppermute(next_up, "freq", z_shift(n_z, 1))
        down = lax.ppermute(next_down, "freq", z_shift(n_z, -1))
    return (block(0) + up.astype(F32) + down.astype(F32)).astype(BF16)


def per_device(
    uv_grid, screens, residual, uv_coords, owner_tile, row_offset, column, stations, time_slot
):
    n_bt, n_freq = lax.axis_size("bt"), lax.axis_size("freq")
    n_z = n_freq // 2
    slots = n_bt * CAP
    consts = constant_tables()
    swap = [(f, f ^ 1) for f in range(n_freq)]
    row = TSLOTS * PIX
    mail, slot = make_mail(
        owner_tile[0, :, 0], row_offset[0], column[0], screens[:, 0], n_bt
    )
    me = lax.axis_index("freq").astype(jnp.int32).reshape(1)
    where = (me, slot, stations[0].T, time_slot[0])
    image_a = adjoint_images(residual[0], uv_coords[0], 0, 2)
    image_b = adjoint_images(residual[0], uv_coords[0], 1, 2)
    images = (image_a, image_b)
    mail = exchange(mail, "bt")
    asked = mail[:, row].astype(jnp.int32)
    near = ring_gather(mail[:, :row], n_z).reshape(n_z * n_bt * TSLOTS, PIX, LANES)
    far = lax.ppermute(near, "freq", swap)
    cut = cut_windows(asked, uv_grid[0])
    fetched = exchange(cut.reshape(n_bt, CAP, 2 * PIX, LANES), "bt")
    fetched = fetched.reshape(slots, 2 * PIX, LANES)
    grads, used = patch_gradients(where, images, near, far, consts, slots, n_bt, n_freq)
    returned = exchange(grads.reshape(n_bt, CAP, 2 * PIX, LANES), "bt")
    returned = returned.reshape(slots, 2 * PIX, LANES)
    terms, sent = screen_gradients(
        where, images, fetched, used, near.shape[0], consts, n_bt, n_freq
    )
    came = lax.ppermute(sent, "freq", swap)
    blocks = (n_z, n_bt, TSLOTS * PIX, LANES)
    part = ring_sum(terms.reshape(blocks), came.reshape(blocks), n_z)
    part = exchange(part, "bt")
    grid_grad = add_windows(asked, returned, *uv_grid.shape[1:])
    screen_grad = finish(part.reshape(n_bt, TSLOTS, PIX, LANES))
    return grid_grad[None], screen_grad[:, None]


def solution(mesh):
    in_specs = (
        P("freq", None, "bt", None),
        P(None, ("bt", "freq"), None, None),
        P("freq", "bt", None, None),
        P("freq", "bt", None, None),
        P("freq", "bt", None),
        P("freq", "bt"),
        P("freq", "bt"),
        P("freq", "bt", None),
        P("freq", "bt"),
    )
    out_specs = (P("freq", None, "bt", None), P(None, ("bt", "freq"), None, None))

    return jax.shard_map(
        per_device, mesh=mesh, in_specs=in_specs, out_specs=out_specs, check_vma=False
    )
```

```python
import math

import jax
import jax.numpy as jnp
import numpy as np
from jax import lax
from jax.experimental import pallas as pl
from jax.experimental.pallas import tpu as pltpu
from jax.sharding import PartitionSpec as P


PIX = 32
TSLOTS = 2
LANES = 128
CAP = 8
F32 = jnp.float32
BF16 = jnp.bfloat16


def constant_tables():
    ramp = np.arange(PIX)
    angle = (ramp[:, None] * ramp[None, :] % PIX) * (2.0 * math.pi / PIX)
    cos_part = (np.cos(angle) / math.sqrt(PIX)).astype(np.float32)
    sin_part = (np.sin(angle) / math.sqrt(PIX)).astype(np.float32)
    forward = np.block([[cos_part, -sin_part], [sin_part, cos_part]])
    backward = np.block([[cos_part, sin_part], [-sin_part, cos_part]])
    eye = np.eye(4, dtype=np.float32)
    right = np.concatenate([np.kron(eye, cos_part), np.kron(eye, sin_part)], 1)
    block = np.eye(PIX, dtype=np.float32)

    def spread(picks):
        out = np.zeros((LANES, len(picks) * PIX), np.float32)
        for j, i in enumerate(picks):
            out[i * PIX : (i + 1) * PIX, j * PIX : (j + 1) * PIX] = block
        return out

    spread_first = spread([0, 0, 1, 1, 2, 2, 3, 3])
    spread_second = spread([0, 1, 0, 1, 2, 3, 2, 3])
    as_bf16 = [
        jnp.asarray(v, BF16) for v in (forward, backward, right, spread_first, spread_second)
    ]
    return as_bf16


def dot(a, b):
    return jnp.dot(a, b, preferred_element_type=F32)


def swap_blocks(x):
    rolled = [x] + [pltpu.roll(x, d * PIX, 1) for d in (1, 2, 3)]
    line = lax.broadcasted_iota(jnp.int32, x.shape, 0)
    block = lax.broadcasted_iota(jnp.int32, x.shape, 1) // PIX
    rows = []
    for a in range(4):
        d = (block - a + 4) % 4
        moved = rolled[0]
        for k in (1, 2, 3):
            moved = jnp.where(d == k, rolled[k], moved)
        rows.append(jnp.sum(jnp.where(block == line, moved, 0.0), 0, keepdims=True))
    return rows


def mail_kernel(
    n_bt, owner, row_offset, column, screens, mail, slot, fill, request, own,
):
    count = owner.shape[0]
    for i in range(n_bt):
        fill[i] = 0

    def step(s, carry):
        o = owner[s]
        n = fill[o]
        fill[o] = n + 1
        place = o * CAP + n
        slot[s] = place
        request[place] = row_offset[s] * 1024 + column[s]
        return carry

    lax.fori_loop(0, count, step, 0, unroll=4)
    for t in range(TSLOTS):
        table = screens[t].astype(F32)
        for high in range(PIX // 4):
            for a, line in enumerate(swap_blocks(table[:, high * LANES : (high + 1) * LANES])):
                x = t * PIX + high * 4 + a
                own[x : x + 1] = line
    every = own[...].astype(BF16)
    lane = lax.broadcasted_iota(jnp.int32, (16, LANES), 1)

    def address(j, carry):
        n = fill[j]
        line = jnp.where(lane == 3 * CAP, n, 0)
        for k in range(CAP):
            code = jnp.where(k < n, request[j * CAP + k], 0)
            for part, value in enumerate((code >> 10, (code >> 5) & 31, code & 31)):
                line = jnp.where(lane == part * CAP + k, value, line)
        mail[j] = jnp.concatenate([every, line.astype(F32).astype(BF16)], 0)
        return carry

    lax.fori_loop(0, n_bt, address, 0)


def make_mail(owners, row_offset, column, screens, n_bt):
    count = owners.shape[0]
    smem, vmem = pl.BlockSpec(memory_space=pltpu.SMEM), pl.BlockSpec(memory_space=pltpu.VMEM)
    rows = TSLOTS * PIX
    return pl.pallas_call(
        lambda *refs: mail_kernel(n_bt, *refs),
        out_shape=(
            jax.ShapeDtypeStruct((n_bt, rows + 16, LANES), BF16),
            jax.ShapeDtypeStruct((count,), jnp.int32),
        ),
        in_specs=[smem] * 3 + [vmem],
        out_specs=(vmem, smem),
        scratch_shapes=[
            pltpu.SMEM((n_bt,), jnp.int32),
            pltpu.SMEM((n_bt * CAP,), jnp.int32),
            pltpu.VMEM((rows, LANES), F32),
        ],
        name="mail",
    )(owners, row_offset, column, screens)


def finish_kernel(parts, out):
    total = jnp.sum(parts[...].astype(F32), 0)
    line = lax.broadcasted_iota(jnp.int32, (4, LANES), 0)
    for t in range(TSLOTS):
        for high in range(PIX // 4):
            rows = swap_blocks(total[t, high * 4 : high * 4 + 4])
            tile = jnp.broadcast_to(rows[0], (4, LANES))
            for a in (1, 2, 3):
                tile = jnp.where(line == a, jnp.broadcast_to(rows[a], (4, LANES)), tile)
            out[t, :, high * LANES : (high + 1) * LANES] = tile


def finish(parts):
    vmem = pl.BlockSpec(memory_space=pltpu.VMEM)
    return pl.pallas_call(
        finish_kernel,
        out_shape=jax.ShapeDtypeStruct((TSLOTS, 4, PIX * PIX), F32),
        in_specs=[vmem],
        out_specs=vmem,
        name="finish",
        compiler_params=pltpu.CompilerParams(vmem_limit_bytes=4 << 20),
    )(parts)


def listed(asked, order):
    def step(j, n):
        for k in range(CAP):
            order[n + k] = j * CAP + k
        return n + asked[j, 3 * CAP]

    return lax.fori_loop(0, asked.shape[0], step, jnp.int32(0))


def corner(asked, i):
    j, k = i >> 3, i & 7
    return asked[j, k], asked[j, CAP + k] * PIX + asked[j, 2 * CAP + k]


def for_listed(n, body):
    done = 0
    for group in (8, 4, 1):

        def some(g, carry, group=group, done=done):
            body([done + g * group + k for k in range(group)])
            return carry

        count = (n - done) // group
        lax.fori_loop(0, count, some, 0)
        done = done + count * group


HALF = LANES // 2


def panel_of(c0, panels):
    p = jnp.minimum(c0 >> 6, panels - 1)
    return p, c0 - p * HALF


def cut_kernel(asked, tile, out, wide, order, stage, sems):
    comps, rows, columns = tile.shape
    panels = wide.shape[0]
    low = lax.broadcasted_iota(jnp.int32, (comps * rows, LANES), 1) < HALF
    before = None
    for j in range(columns // LANES):
        whole = tile[:, :, j * LANES : (j + 1) * LANES].astype(F32).reshape(comps * rows, LANES)
        wide[2 * j] = whole
        turned = pltpu.roll(whole, HALF, 1)
        if before is not None:
            wide[2 * j - 1] = jnp.where(low, before, turned)
        before = turned
    n = listed(asked, order)
    line = lax.broadcasted_iota(jnp.int32, (LANES, LANES), 0)
    lane = lax.broadcasted_iota(jnp.int32, (LANES, LANES), 1)
    ahead = line - lane % PIX
    block = lax.broadcasted_iota(jnp.int32, (PIX, LANES), 1) // PIX

    def body(places):
        done = []
        for place in places:
            i = order[place]
            r, c0 = corner(asked, i)
            p, shift = panel_of(c0, panels)
            lines = jnp.concatenate(
                [wide[p, pl.ds(c * rows + r, PIX), :] for c in range(comps)], 0
            ).astype(BF16)
            moved = dot(lines, jnp.where(ahead == shift, 1.0, 0.0).astype(BF16))
            parts = []
            for ri in range(2):
                part = moved[ri * 128 : ri * 128 + PIX]
                for m in range(1, 4):
                    start = (ri * 4 + m) * PIX
                    part = jnp.where(block == m, moved[start : start + PIX], part)
                parts.append(part)
            done.append((i, jnp.concatenate(parts, 0).astype(BF16)))
        for i, piece in done:
            stage[i] = piece
        for i, piece in done:
            pltpu.make_async_copy(stage.at[i], out.at[i], sems.at[i]).start()

    for_listed(n, body)

    def finished(g, carry):
        i = order[g]
        pltpu.make_async_copy(stage.at[i], out.at[i], sems.at[i]).wait()
        return carry

    lax.fori_loop(0, n, finished, 0)


def cut_windows(asked, tile):
    comps, rows, columns = tile.shape
    slots = asked.shape[0] * CAP
    return pl.pallas_call(
        cut_kernel,
        out_shape=jax.ShapeDtypeStruct((slots, 2 * PIX, LANES), BF16),
        in_specs=[pl.BlockSpec(memory_space=pltpu.SMEM), pl.BlockSpec(memory_space=pltpu.VMEM)],
        out_specs=pl.BlockSpec(memory_space=pl.ANY),
        scratch_shapes=[
            pltpu.VMEM((columns // HALF - 1, comps * rows, LANES), F32),
            pltpu.SMEM((slots + CAP,), jnp.int32),
            pltpu.VMEM((slots, 2 * PIX, LANES), BF16),
            pltpu.SemaphoreType.DMA((slots,)),
        ],
        name="cut",
    )(asked, tile)


def add_kernel(asked, pieces, out, wide, order):
    comps, rows, columns = out.shape
    panels = wide.shape[0]
    for p in range(panels):
        wide[p] = jnp.zeros((comps * rows, LANES), F32)
    n = listed(asked, order)
    line = lax.broadcasted_iota(jnp.int32, (LANES, LANES), 0)
    lane = lax.broadcasted_iota(jnp.int32, (LANES, LANES), 1)
    ahead = lane - line % PIX
    block = lax.broadcasted_iota(jnp.int32, (PIX, LANES), 1) // PIX

    def body(places):
        spread = []
        for place in places:
            i = order[place]
            r, c0 = corner(asked, i)
            p, shift = panel_of(c0, panels)
            piece = pieces[i].astype(F32)
            lines = []
            for ri in range(2):
                for m in range(4):
                    lines.append(jnp.where(block == m, piece[ri * PIX : (ri + 1) * PIX], 0.0))
            lines = jnp.concatenate(lines, 0).astype(BF16)
            spread.append((r, p, dot(lines, jnp.where(ahead == shift, 1.0, 0.0).astype(BF16))))
        for r, p, moved in spread:
            sums = []
            for c in range(comps):
                at = pl.ds(c * rows + r, PIX)
                sums.append((at, wide[p, at, :] + moved[c * PIX : (c + 1) * PIX]))
            for at, total in sums:
                wide[p, at, :] = total

    for_listed(n, body)
    low = lax.broadcasted_iota(jnp.int32, (comps * rows, LANES), 1) < HALF
    before = jnp.zeros((comps * rows, LANES), F32)
    for j in range(columns // LANES):
        if 2 * j + 1 < panels:
            turned = pltpu.roll(wide[2 * j + 1], HALF, 1)
        else:
            turned = jnp.zeros((comps * rows, LANES), F32)
        total = wide[2 * j] + jnp.where(low, before, turned)
        out[:, :, j * LANES : (j + 1) * LANES] = total.reshape(comps, rows, LANES)
        before = turned


def add_windows(asked, pieces, comps, rows, columns):
    slots = asked.shape[0] * CAP
    return pl.pallas_call(
        add_kernel,
        out_shape=jax.ShapeDtypeStruct((comps, rows, columns), F32),
        in_specs=[pl.BlockSpec(memory_space=pltpu.SMEM), pl.BlockSpec(memory_space=pltpu.VMEM)],
        out_specs=pl.BlockSpec(memory_space=pltpu.VMEM),
        scratch_shapes=[
            pltpu.VMEM((columns // HALF - 1, comps * rows, LANES), F32),
            pltpu.SMEM((slots + CAP,), jnp.int32),
        ],
        name="add",
        compiler_params=pltpu.CompilerParams(vmem_limit_bytes=14 << 20),
    )(asked, pieces)


def turn_waves(turns):
    part = turns - jnp.round(turns)
    z = part * part
    coef_sin = [(-1.0) ** k * math.pi ** (2 * k + 1) / math.factorial(2 * k + 1) for k in range(7)]
    coef_cos = [(-1.0) ** k * math.pi ** (2 * k) / math.factorial(2 * k) for k in range(8)]
    s = jnp.full_like(z, coef_sin[-1])
    for v in coef_sin[-2::-1]:
        s = s * z + v
    s = s * part
    c = jnp.full_like(z, coef_cos[-1])
    for v in coef_cos[-2::-1]:
        c = c * z + v
    return 1.0 - 2.0 * s * s, 2.0 * s * c


def image_kernel(group, vis, uv, out):
    samples = vis.shape[2]
    position = lax.broadcasted_iota(jnp.int32, (PIX, samples), 0).astype(F32) * (1.0 / PIX)

    def step(g, carry):
        done = []
        for k in range(group):
            s = g * group + k
            uv_rows = uv[s]
            x_cos, x_sin = turn_waves(position * uv_rows[0:1])
            y_cos, y_sin = turn_waves(position * uv_rows[1:2])
            wave_x = jnp.concatenate([x_cos, x_sin], 0).astype(BF16)
            y_cos, y_sin = y_cos.astype(BF16).astype(F32), y_sin.astype(BF16).astype(F32)
            rows = vis[s].astype(F32)
            weight_re, weight_im = [], []
            for m in range(4):
                re, im = rows[m : m + 1], rows[m + 4 : m + 5]
                weight_re.append(re * y_cos - im * y_sin)
                weight_im.append(re * y_sin + im * y_cos)
            weighted = jnp.concatenate(weight_re + weight_im, 0).astype(BF16)
            products = lax.dot_general(
                wave_x, weighted, (((1,), (1,)), ((), ())), preferred_element_type=F32
            )
            low, high = products[:PIX], products[PIX:]
            done.append((s, low[:, :LANES] - high[:, LANES:], low[:, LANES:] + high[:, :LANES]))
        for s, re, im in done:
            out[s, 0:PIX] = re
            out[s, PIX:] = im
        return carry

    lax.fori_loop(0, vis.shape[0] // group, step, 0)


def adjoint_images(vis, uv, first, count):
    group = math.gcd(count, 4)
    at = first // count
    blocks = [pl.BlockSpec((count,) + x.shape[1:], lambda i: (at, 0, 0)) for x in (vis, uv)]
    return pl.pallas_call(
        lambda *refs: image_kernel(group, *refs),
        out_shape=jax.ShapeDtypeStruct((count, 2 * PIX, LANES), F32),
        grid=(1,),
        in_specs=blocks,
        out_specs=pl.BlockSpec((count, 2 * PIX, LANES), lambda i: (0, 0, 0)),
        name="image",
    )(vis, uv)


def table_rows(n_bt, n_freq, me, stations, slot_time):
    n_z = n_freq // 2
    my_z, my_core = me[0] >> 1, me[0] & 1

    def row(which, s):
        station = stations[which, s]
        bt, freq = lax.div(station, n_freq), lax.rem(station, n_freq)
        half = jnp.where((freq & 1) == my_core, 0, n_bt * n_z)
        ahead = lax.rem((freq >> 1) - my_z + n_z, n_z)
        return (half + ahead * n_bt + bt) * TSLOTS + slot_time[s]

    return row


def join_parts(parts, whole, sems, chunk):
    copies = []
    for part in parts:
        for c in range(0, part.shape[0], chunk):
            k = len(copies)
            at = pl.ds(k * chunk, chunk)
            copy = pltpu.make_async_copy(part.at[pl.ds(c, chunk)], whole.at[at], sems.at[k])
            copy.start()
            copies.append(copy)
    return copies


def join_rings(halves, table, sems):
    copies, at = [], 0
    for early, late in halves:
        block = (early.shape[0] + late.shape[0]) // 8
        for part, start, count in ((early, 0, 3), (late, 0, 3), (early, 3, 2)):
            copy = pltpu.make_async_copy(
                part.at[pl.ds(start * block, count * block)],
                table.at[pl.ds(at, count * block)],
                sems.at[len(copies)],
            )
            copy.start()
            copies.append(copy)
            at += count * block
    return copies


def screens_of(lines, spread):
    wide = dot(jnp.concatenate(lines, 0), spread[...])
    at = [slice(k * PIX, (k + 1) * PIX) for k in range(len(lines))]
    return [(wide[k, :LANES], wide[k, LANES:]) for k in at]


def left_side(left, pieces):
    count = pieces.shape[1] // LANES
    inner = dot(left[...], pieces).astype(BF16)
    return jnp.concatenate([inner[:, k * LANES : (k + 1) * LANES] for k in range(count)], 0)


def right_side(lines, right):
    outer = dot(lines, right[...])
    return [outer[k : k + 2 * PIX] for k in range(0, lines.shape[0], 2 * PIX)]


def patch_kernel(
    group, n_bt, n_freq, me, slot, stations, slot_time, image_a, image_b, image_c,
    near_a, near_b, far_a, far_b, backward, right, spread_a, spread_b, out, used, table, sems, image, image_sems,
    stage, out_sems, backs, lows, lines, line_sems,
):
    copies = join_rings(((near_a, near_b), (far_a, far_b)), table, sems)
    images = join_parts((image_a, image_b, image_c), image, image_sems, image_c.shape[0])
    row = table_rows(n_bt, n_freq, me, stations, slot_time)
    for copy in copies + images[:1]:
        copy.wait()
    groups = image.shape[0] // group

    def back_side(g):
        subs = [g * group + k for k in range(group)]
        first_lines = [table[row(0, s)] for s in subs]
        second_lines = [table[row(1, s)] for s in subs]
        first_screens = screens_of(first_lines, spread_a)
        second_screens = screens_of(second_lines, spread_b)
        pieces = []
        for s, (a_re, a_im), (b_re, b_im) in zip(subs, first_screens, second_screens):
            m_re, m_im = image[s, 0:PIX], image[s, PIX:]
            both_re = a_re * b_re + a_im * b_im
            both_im = a_re * b_im - a_im * b_re
            back_re = both_re * m_re - both_im * m_im
            back_im = both_re * m_im + both_im * m_re
            pieces.append(jnp.concatenate([back_re, back_im], 0).astype(BF16))
        for s, a, b in zip(subs, first_lines, second_lines):
            lines[s] = jnp.concatenate([a, b], 0)
        return jnp.concatenate(pieces, 1)

    def hand_on(g):
        at = pl.ds(g * group, group)
        return pltpu.make_async_copy(lines.at[at], used.at[at], line_sems.at[g])

    lows[...] = left_side(backward, back_side(0))
    backs[...] = back_side(1)

    def step(g, carry):
        grads = []
        for grad in right_side(lows[...], right):
            re, im = grad[:PIX], grad[PIX:]
            grad_re = re[:, :LANES] + im[:, LANES:]
            grad_im = im[:, :LANES] - re[:, LANES:]
            grads.append(jnp.concatenate([grad_re, grad_im], 0).astype(BF16))
        low = left_side(backward, backs[...])
        back = back_side(jnp.minimum(g + 2, groups - 1))
        lows[...] = low
        backs[...] = back
        subs = [g * group + k for k in range(group)]
        for s, grad in zip(subs, grads):
            stage[s] = grad
        for s in subs:
            pltpu.make_async_copy(stage.at[s], out.at[slot[s]], out_sems.at[s]).start()
        hand_on(g).start()
        return carry

    count, ready = image.shape[0], groups // len(images)
    for p in range(len(images)):
        if p + 1 < len(images):
            images[p + 1].wait()
        lax.fori_loop(p * ready, (p + 1) * ready, step, 0)

    def finished(s, carry):
        pltpu.make_async_copy(stage.at[s], out.at[slot[s]], out_sems.at[s]).wait()
        return carry

    lax.fori_loop(0, count, finished, 0)
    for g in range(groups):
        hand_on(g).wait()


def patch_gradients(where, images, rings, consts, slots, n_bt, n_freq):
    _, backward, right, spread_a, spread_b = consts
    count = 4 * images[-1].shape[0]
    group = math.gcd(count // 4, 4)
    vmem, smem = pl.BlockSpec(memory_space=pltpu.VMEM), pl.BlockSpec(memory_space=pltpu.SMEM)
    half = rings[0].shape[0] + rings[1].shape[0]
    return pl.pallas_call(
        lambda *refs: patch_kernel(group, n_bt, n_freq, *refs),
        out_shape=(
            jax.ShapeDtypeStruct((slots, 2 * PIX, LANES), BF16),
            jax.ShapeDtypeStruct((count, 2 * PIX, LANES), BF16),
        ),
        in_specs=[smem] * 4 + [pl.BlockSpec(memory_space=pl.ANY)] * 7 + [vmem] * 4,
        out_specs=(pl.BlockSpec(memory_space=pl.ANY),) * 2,
        scratch_shapes=[
            pltpu.VMEM((2 * half, PIX, LANES), BF16),
            pltpu.SemaphoreType.DMA((6,)),
            pltpu.VMEM((count, 2 * PIX, LANES), F32),
            pltpu.SemaphoreType.DMA((4,)),
            pltpu.VMEM((count, 2 * PIX, LANES), BF16),
            pltpu.SemaphoreType.DMA((count,)),
            pltpu.VMEM((2 * PIX, group * LANES), BF16),
            pltpu.VMEM((group * 2 * PIX, LANES), BF16),
            pltpu.VMEM((count, 2 * PIX, LANES), BF16),
            pltpu.SemaphoreType.DMA((count // group,)),
        ],
        name="patch",
        compiler_params=pltpu.CompilerParams(vmem_limit_bytes=64 << 20),
    )(*where, *images, *rings, backward, right, spread_a, spread_b)


def screen_kernel(
    group, n_bt, n_freq, me, slot, stations, slot_time, image_a, image_b, image_c, used,
    patches, forward, right, spread_a, spread_b, out_near, out_far,
    lines, line_sems, image, image_sems, window, window_sems, acc, mids, stage, out_sems,
):
    chunk = 32
    count = image.shape[0]
    line_copies = join_parts((used,), lines, line_sems, count // 4)
    image_copies = join_parts((image_a, image_b, image_c), image, image_sems, count // 4)

    def window_copy(s):
        return pltpu.make_async_copy(patches.at[slot[s]], window.at[s], window_sems.at[s])

    def ask(s, carry):
        window_copy(s).start()
        return carry

    lax.fori_loop(0, count, ask, 0)

    def ready(p):
        line_copies[p].wait()
        image_copies[p].wait()

        def have(s, carry):
            window_copy(s).wait()
            return carry

        lax.fori_loop(p * count // 4, (p + 1) * count // 4, have, 0)

    row = table_rows(n_bt, n_freq, me, stations, slot_time)
    groups = count // group

    def clear(i, carry):
        acc[pl.ds(i * chunk, chunk)] = jnp.zeros((chunk, PIX, LANES), F32)
        return carry

    lax.fori_loop(0, acc.shape[0] // chunk, clear, 0)
    ready(0)
    block = lax.broadcasted_iota(jnp.int32, (PIX, LANES), 1) // PIX

    def begin(g):
        return left_side(
            forward, jnp.concatenate([window[g * group + k] for k in range(group)], 1)
        )

    mids[...] = begin(0)

    def step(g, carry):
        terms = []
        subs = [g * group + k for k in range(group)]
        first_rows, second_rows = [[row(w, s) for s in subs] for w in (0, 1)]
        skies = right_side(mids[...], right)
        first_screens = screens_of([lines[s, 0:PIX] for s in subs], spread_a)
        second_screens = screens_of([lines[s, PIX:] for s in subs], spread_b)
        mid = begin(jnp.minimum(g + 1, groups - 1))
        for s, (a_re, a_im), (b_re, b_im), sky in zip(subs, first_screens, second_screens, skies):
            m_re, m_im = image[s, 0:PIX], image[s, PIX:]
            re, im = sky[:PIX], sky[PIX:]
            sky_re = re[:, :LANES] - im[:, LANES:]
            sky_im = re[:, LANES:] + im[:, :LANES]
            carry_re = b_re * m_re - b_im * m_im
            carry_im = b_re * m_im + b_im * m_re
            ga_re = sky_re * carry_re + sky_im * carry_im
            ga_im = sky_re * carry_im - sky_im * carry_re
            model_re = a_re * sky_re - a_im * sky_im
            model_im = a_re * sky_im + a_im * sky_re
            gb_re = m_re * model_re + m_im * model_im
            gb_im = m_re * model_im - m_im * model_re
            ta = jnp.where(
                block % 2 == 0,
                ga_re + pltpu.roll(ga_re, LANES - PIX, 1),
                ga_im + pltpu.roll(ga_im, PIX, 1),
            )
            ta = jnp.where(
                block == 1,
                pltpu.roll(ta, LANES - PIX, 1),
                jnp.where(block == 2, pltpu.roll(ta, PIX, 1), ta),
            )
            tb = jnp.where(
                block < 2,
                gb_re + pltpu.roll(gb_re, 2 * PIX, 1),
                gb_im + pltpu.roll(gb_im, 2 * PIX, 1),
            )
            terms.append((ta, tb))
        mids[...] = mid
        for (ta, tb), first, second in zip(terms, first_rows, second_rows):
            acc[first] = acc[first] + ta
            acc[second] = acc[second] + tb
        return carry

    for p in range(4):
        if p + 1 < 4:
            ready(p + 1)
        lax.fori_loop(p * groups // 4, (p + 1) * groups // 4, step, 0)
    copies = []
    half = out_far.shape[0]
    for start, out in ((half, out_far), (0, out_near)):
        for i in range(0, half, chunk):
            at = pl.ds(start + i, chunk)
            stage[at] = acc[at].astype(BF16)
            copy = pltpu.make_async_copy(
                stage.at[at], out.at[pl.ds(i, chunk)], out_sems.at[len(copies)]
            )
            copy.start()
            copies.append(copy)
    for copy in copies:
        copy.wait()


def screen_gradients(where, images, patches, used, rows, consts, n_bt, n_freq):
    forward, _, right, spread_a, spread_b = consts
    count = used.shape[0]
    group = math.gcd(count // 4, 4)
    vmem, smem = pl.BlockSpec(memory_space=pltpu.VMEM), pl.BlockSpec(memory_space=pltpu.SMEM)
    sums = jax.ShapeDtypeStruct((rows, PIX, LANES), BF16)
    return pl.pallas_call(
        lambda *refs: screen_kernel(group, n_bt, n_freq, *refs),
        out_shape=(sums, sums),
        in_specs=[smem] * 4 + [pl.BlockSpec(memory_space=pl.ANY)] * 5 + [vmem] * 4,
        out_specs=(pl.BlockSpec(memory_space=pl.ANY),) * 2,
        scratch_shapes=[
            pltpu.VMEM((count, 2 * PIX, LANES), BF16),
            pltpu.SemaphoreType.DMA((4,)),
            pltpu.VMEM((count, 2 * PIX, LANES), F32),
            pltpu.SemaphoreType.DMA((4,)),
            pltpu.VMEM((count, 2 * PIX, LANES), BF16),
            pltpu.SemaphoreType.DMA((count,)),
            pltpu.VMEM((2 * rows, PIX, LANES), F32),
            pltpu.VMEM((group * 2 * PIX, LANES), BF16),
            pltpu.VMEM((2 * rows, PIX, LANES), BF16),
            pltpu.SemaphoreType.DMA((2 * rows // 32,)),
        ],
        name="screen",
    )(*where, *images, used, patches, forward, right, spread_a, spread_b)


def exchange(x, axis):
    return lax.all_to_all(x, axis, split_axis=0, concat_axis=0, tiled=True)


def z_shift(n_z, step):
    return [(2 * z + c, 2 * ((z + step) % n_z) + c) for z in range(n_z) for c in range(2)]


def ring_gather(x, n_z):
    half = n_z // 2
    blocks = [None] * n_z
    blocks[0] = up = down = x
    for k in range(1, half):
        up = lax.ppermute(up, "freq", z_shift(n_z, 1))
        down = lax.ppermute(down, "freq", z_shift(n_z, -1))
        blocks[n_z - k], blocks[k] = up, down
    cut = x.shape[0] // 2
    up = lax.ppermute(up[:cut], "freq", z_shift(n_z, 1))
    down = lax.ppermute(down[cut:], "freq", z_shift(n_z, -1))
    blocks[half] = jnp.concatenate([up, down])
    early = jnp.stack(blocks[:3] + blocks[6:])
    return early, jnp.stack(blocks[3:6])


def ring_sum(mine, came, n_z):
    half, cut = n_z // 2, mine.shape[1] // 2

    def block(k, at=slice(None)):
        return mine[k, at].astype(F32) + came[k, at].astype(F32)

    up, down = block(half, slice(0, cut)).astype(BF16), block(half, slice(cut, None)).astype(BF16)
    up = lax.ppermute(up, "freq", z_shift(n_z, 1))
    down = lax.ppermute(down, "freq", z_shift(n_z, -1))
    for k in range(half - 1, 0, -1):
        next_up, next_down = block(k), block(n_z - k)
        if k == half - 1:
            zeros = jnp.zeros_like(up)
            up, down = jnp.concatenate([up, zeros]), jnp.concatenate([zeros, down])
        next_up = (next_up + up.astype(F32)).astype(BF16)
        next_down = (next_down + down.astype(F32)).astype(BF16)
        up = lax.ppermute(next_up, "freq", z_shift(n_z, 1))
        down = lax.ppermute(next_down, "freq", z_shift(n_z, -1))
    return (block(0) + up.astype(F32) + down.astype(F32)).astype(BF16)


def per_device(
    uv_grid, screens, residual, uv_coords, owner_tile, row_offset, column, stations, time_slot
):
    n_bt, n_freq = lax.axis_size("bt"), lax.axis_size("freq")
    n_z = n_freq // 2
    slots = n_bt * CAP
    consts = constant_tables()
    swap = [(f, f ^ 1) for f in range(n_freq)]
    row = TSLOTS * PIX
    mail, slot = make_mail(
        owner_tile[0, :, 0], row_offset[0], column[0], screens[:, 0], n_bt
    )
    me = lax.axis_index("freq").astype(jnp.int32).reshape(1)
    where = (me, slot, stations[0].T, time_slot[0])
    quarter = residual.shape[1] // 4
    images = []
    for part, (begin, count) in enumerate(((0, 2), (2, 1), (3, 1))):
        images.append(adjoint_images(residual[0], uv_coords[0], begin * quarter, count * quarter))
    mail = exchange(mail, "bt")
    asked = mail[:, row].astype(jnp.int32)
    near = [x.reshape(-1, PIX, LANES) for x in ring_gather(mail[:, :row], n_z)]
    far_early = lax.ppermute(near[0], "freq", swap)
    far_late = lax.ppermute(near[1], "freq", swap)
    rings = (*near, far_early, far_late)
    cut = cut_windows(asked, uv_grid[0])
    fetched = exchange(cut.reshape(n_bt, CAP, 2 * PIX, LANES), "bt")
    fetched = fetched.reshape(slots, 2 * PIX, LANES)
    grads, used = patch_gradients(where, images, rings, consts, slots, n_bt, n_freq)
    returned = exchange(grads.reshape(n_bt, CAP, 2 * PIX, LANES), "bt")
    returned = returned.reshape(slots, 2 * PIX, LANES)
    terms, sent = screen_gradients(
        where, images, fetched, used, n_z * n_bt * TSLOTS, consts, n_bt, n_freq
    )
    came = lax.ppermute(sent, "freq", swap)
    blocks = (n_z, n_bt, TSLOTS * PIX, LANES)
    part = ring_sum(terms.reshape(blocks), came.reshape(blocks), n_z)
    part = exchange(part, "bt")
    grid_grad = add_windows(asked, returned, *uv_grid.shape[1:])
    screen_grad = finish(part.reshape(n_bt, TSLOTS, PIX, LANES))
    return grid_grad[None], screen_grad[:, None]


def solution(mesh):
    in_specs = (
        P("freq", None, "bt", None),
        P(None, ("bt", "freq"), None, None),
        P("freq", "bt", None, None),
        P("freq", "bt", None, None),
        P("freq", "bt", None),
        P("freq", "bt"),
        P("freq", "bt"),
        P("freq", "bt", None),
        P("freq", "bt"),
    )
    out_specs = (P("freq", None, "bt", None), P(None, ("bt", "freq"), None, None))

    return jax.shard_map(
        per_device, mesh=mesh, in_specs=in_specs, out_specs=out_specs, check_vma=False
    )
```

```python
import math

import jax
import jax.numpy as jnp
import numpy as np
from jax import lax
from jax.experimental import pallas as pl
from jax.experimental.pallas import tpu as pltpu
from jax.sharding import PartitionSpec as P


PIX = 32
TSLOTS = 2
LANES = 128
CAP = 8
F32 = jnp.float32
BF16 = jnp.bfloat16


def constant_tables():
    ramp = np.arange(PIX)
    angle = (ramp[:, None] * ramp[None, :] % PIX) * (2.0 * math.pi / PIX)
    cos_part = (np.cos(angle) / math.sqrt(PIX)).astype(np.float32)
    sin_part = (np.sin(angle) / math.sqrt(PIX)).astype(np.float32)
    forward = np.block([[cos_part, -sin_part], [sin_part, cos_part]])
    backward = np.block([[cos_part, sin_part], [-sin_part, cos_part]])
    eye = np.eye(4, dtype=np.float32)
    right = np.concatenate([np.kron(eye, cos_part), np.kron(eye, sin_part)], 1)
    block = np.eye(PIX, dtype=np.float32)

    def spread(picks):
        out = np.zeros((LANES, len(picks) * PIX), np.float32)
        for j, i in enumerate(picks):
            out[i * PIX : (i + 1) * PIX, j * PIX : (j + 1) * PIX] = block
        return out

    spread_first = spread([0, 0, 1, 1, 2, 2, 3, 3])
    spread_second = spread([0, 1, 0, 1, 2, 3, 2, 3])
    as_bf16 = [
        jnp.asarray(v, BF16) for v in (forward, backward, right, spread_first, spread_second)
    ]
    return as_bf16


def dot(a, b):
    return jnp.dot(a, b, preferred_element_type=F32)


def swap_blocks(x):
    rolled = [x] + [pltpu.roll(x, d * PIX, 1) for d in (1, 2, 3)]
    line = lax.broadcasted_iota(jnp.int32, x.shape, 0)
    block = lax.broadcasted_iota(jnp.int32, x.shape, 1) // PIX
    rows = []
    for a in range(4):
        d = (block - a + 4) % 4
        moved = rolled[0]
        for k in (1, 2, 3):
            moved = jnp.where(d == k, rolled[k], moved)
        rows.append(jnp.sum(jnp.where(block == line, moved, 0.0), 0, keepdims=True))
    return rows


def mail_kernel(
    n_bt, owner, row_offset, column, screens, mail, slot, fill, request, own,
):
    count = owner.shape[0]
    for i in range(n_bt):
        fill[i] = 0

    def step(s, carry):
        o = owner[s]
        n = fill[o]
        fill[o] = n + 1
        place = o * CAP + n
        slot[s] = place
        request[place] = row_offset[s] * 1024 + column[s]
        return carry

    lax.fori_loop(0, count, step, 0, unroll=4)
    for t in range(TSLOTS):
        table = screens[t].astype(F32)
        for high in range(PIX // 4):
            for a, line in enumerate(swap_blocks(table[:, high * LANES : (high + 1) * LANES])):
                x = t * PIX + high * 4 + a
                own[x : x + 1] = line
    every = own[...].astype(BF16)
    lane = lax.broadcasted_iota(jnp.int32, (16, LANES), 1)

    def address(j, carry):
        n = fill[j]
        line = jnp.where(lane == 3 * CAP, n, 0)
        for k in range(CAP):
            code = jnp.where(k < n, request[j * CAP + k], 0)
            for part, value in enumerate((code >> 10, (code >> 5) & 31, code & 31)):
                line = jnp.where(lane == part * CAP + k, value, line)
        mail[j] = jnp.concatenate([every, line.astype(F32).astype(BF16)], 0)
        return carry

    lax.fori_loop(0, n_bt, address, 0)


def make_mail(owners, row_offset, column, screens, n_bt):
    count = owners.shape[0]
    smem, vmem = pl.BlockSpec(memory_space=pltpu.SMEM), pl.BlockSpec(memory_space=pltpu.VMEM)
    rows = TSLOTS * PIX
    return pl.pallas_call(
        lambda *refs: mail_kernel(n_bt, *refs),
        out_shape=(
            jax.ShapeDtypeStruct((n_bt, rows + 16, LANES), BF16),
            jax.ShapeDtypeStruct((count,), jnp.int32),
        ),
        in_specs=[smem] * 3 + [vmem],
        out_specs=(vmem, smem),
        scratch_shapes=[
            pltpu.SMEM((n_bt,), jnp.int32),
            pltpu.SMEM((n_bt * CAP,), jnp.int32),
            pltpu.VMEM((rows, LANES), F32),
        ],
        name="mail",
    )(owners, row_offset, column, screens)


def finish_kernel(parts, out):
    total = jnp.sum(parts[...].astype(F32), 0)
    line = lax.broadcasted_iota(jnp.int32, (4, LANES), 0)
    for t in range(TSLOTS):
        for high in range(PIX // 4):
            rows = swap_blocks(total[t, high * 4 : high * 4 + 4])
            tile = jnp.broadcast_to(rows[0], (4, LANES))
            for a in (1, 2, 3):
                tile = jnp.where(line == a, jnp.broadcast_to(rows[a], (4, LANES)), tile)
            out[t, :, high * LANES : (high + 1) * LANES] = tile


def finish(parts):
    vmem = pl.BlockSpec(memory_space=pltpu.VMEM)
    return pl.pallas_call(
        finish_kernel,
        out_shape=jax.ShapeDtypeStruct((TSLOTS, 4, PIX * PIX), F32),
        in_specs=[vmem],
        out_specs=vmem,
        name="finish",
        compiler_params=pltpu.CompilerParams(vmem_limit_bytes=4 << 20),
    )(parts)


def listed(asked, order):
    def step(j, n):
        for k in range(CAP):
            order[n + k] = j * CAP + k
        return n + asked[j, 3 * CAP]

    return lax.fori_loop(0, asked.shape[0], step, jnp.int32(0))


def corner(asked, i):
    j, k = i >> 3, i & 7
    return asked[j, k], asked[j, CAP + k] * PIX + asked[j, 2 * CAP + k]


def for_listed(n, body):
    done = 0
    for group in (8, 4, 1):

        def some(g, carry, group=group, done=done):
            body([done + g * group + k for k in range(group)])
            return carry

        count = (n - done) // group
        lax.fori_loop(0, count, some, 0)
        done = done + count * group


HALF = LANES // 2


def panel_of(c0, panels):
    p = jnp.minimum(c0 >> 6, panels - 1)
    return p, c0 - p * HALF


def cut_kernel(asked, tile, out, wide, order, stage, sems):
    comps, rows, columns = tile.shape
    panels = wide.shape[0]
    low = lax.broadcasted_iota(jnp.int32, (comps * rows, LANES), 1) < HALF
    before = None
    for j in range(columns // LANES):
        whole = tile[:, :, j * LANES : (j + 1) * LANES].astype(F32).reshape(comps * rows, LANES)
        wide[2 * j] = whole
        turned = pltpu.roll(whole, HALF, 1)
        if before is not None:
            wide[2 * j - 1] = jnp.where(low, before, turned)
        before = turned
    n = listed(asked, order)
    line = lax.broadcasted_iota(jnp.int32, (LANES, LANES), 0)
    lane = lax.broadcasted_iota(jnp.int32, (LANES, LANES), 1)
    ahead = line - lane % PIX
    block = lax.broadcasted_iota(jnp.int32, (PIX, LANES), 1) // PIX

    def body(places):
        done = []
        for place in places:
            i = order[place]
            r, c0 = corner(asked, i)
            p, shift = panel_of(c0, panels)
            lines = jnp.concatenate(
                [wide[p, pl.ds(c * rows + r, PIX), :] for c in range(comps)], 0
            ).astype(BF16)
            moved = dot(lines, jnp.where(ahead == shift, 1.0, 0.0).astype(BF16))
            parts = []
            for ri in range(2):
                part = moved[ri * 128 : ri * 128 + PIX]
                for m in range(1, 4):
                    start = (ri * 4 + m) * PIX
                    part = jnp.where(block == m, moved[start : start + PIX], part)
                parts.append(part)
            done.append((i, jnp.concatenate(parts, 0).astype(BF16)))
        for i, piece in done:
            stage[i] = piece
        for i, piece in done:
            pltpu.make_async_copy(stage.at[i], out.at[i], sems.at[i]).start()

    for_listed(n, body)

    def finished(g, carry):
        i = order[g]
        pltpu.make_async_copy(stage.at[i], out.at[i], sems.at[i]).wait()
        return carry

    lax.fori_loop(0, n, finished, 0)


def cut_windows(asked, tile):
    comps, rows, columns = tile.shape
    slots = asked.shape[0] * CAP
    return pl.pallas_call(
        cut_kernel,
        out_shape=jax.ShapeDtypeStruct((slots, 2 * PIX, LANES), BF16),
        in_specs=[pl.BlockSpec(memory_space=pltpu.SMEM), pl.BlockSpec(memory_space=pltpu.VMEM)],
        out_specs=pl.BlockSpec(memory_space=pl.ANY),
        scratch_shapes=[
            pltpu.VMEM((columns // HALF - 1, comps * rows, LANES), F32),
            pltpu.SMEM((slots + CAP,), jnp.int32),
            pltpu.VMEM((slots, 2 * PIX, LANES), BF16),
            pltpu.SemaphoreType.DMA((slots,)),
        ],
        name="cut",
    )(asked, tile)


def add_kernel(asked, pieces, out, wide, order):
    comps, rows, columns = out.shape
    panels = wide.shape[0]
    for p in range(panels):
        wide[p] = jnp.zeros((comps * rows, LANES), F32)
    n = listed(asked, order)
    line = lax.broadcasted_iota(jnp.int32, (LANES, LANES), 0)
    lane = lax.broadcasted_iota(jnp.int32, (LANES, LANES), 1)
    ahead = lane - line % PIX
    block = lax.broadcasted_iota(jnp.int32, (PIX, LANES), 1) // PIX

    def body(places):
        spread = []
        for place in places:
            i = order[place]
            r, c0 = corner(asked, i)
            p, shift = panel_of(c0, panels)
            piece = pieces[i].astype(F32)
            lines = []
            for ri in range(2):
                for m in range(4):
                    lines.append(jnp.where(block == m, piece[ri * PIX : (ri + 1) * PIX], 0.0))
            lines = jnp.concatenate(lines, 0).astype(BF16)
            spread.append((r, p, dot(lines, jnp.where(ahead == shift, 1.0, 0.0).astype(BF16))))
        for r, p, moved in spread:
            sums = []
            for c in range(comps):
                at = pl.ds(c * rows + r, PIX)
                sums.append((at, wide[p, at, :] + moved[c * PIX : (c + 1) * PIX]))
            for at, total in sums:
                wide[p, at, :] = total

    for_listed(n, body)
    low = lax.broadcasted_iota(jnp.int32, (comps * rows, LANES), 1) < HALF
    before = jnp.zeros((comps * rows, LANES), F32)
    for j in range(columns // LANES):
        if 2 * j + 1 < panels:
            turned = pltpu.roll(wide[2 * j + 1], HALF, 1)
        else:
            turned = jnp.zeros((comps * rows, LANES), F32)
        total = wide[2 * j] + jnp.where(low, before, turned)
        out[:, :, j * LANES : (j + 1) * LANES] = total.reshape(comps, rows, LANES)
        before = turned


def add_windows(asked, pieces, comps, rows, columns):
    slots = asked.shape[0] * CAP
    return pl.pallas_call(
        add_kernel,
        out_shape=jax.ShapeDtypeStruct((comps, rows, columns), F32),
        in_specs=[pl.BlockSpec(memory_space=pltpu.SMEM), pl.BlockSpec(memory_space=pltpu.VMEM)],
        out_specs=pl.BlockSpec(memory_space=pltpu.VMEM),
        scratch_shapes=[
            pltpu.VMEM((columns // HALF - 1, comps * rows, LANES), F32),
            pltpu.SMEM((slots + CAP,), jnp.int32),
        ],
        name="add",
        compiler_params=pltpu.CompilerParams(vmem_limit_bytes=14 << 20),
    )(asked, pieces)


def turn_waves(turns):
    part = turns - jnp.round(turns)
    z = part * part
    coef_sin = [(-1.0) ** k * math.pi ** (2 * k + 1) / math.factorial(2 * k + 1) for k in range(7)]
    coef_cos = [(-1.0) ** k * math.pi ** (2 * k) / math.factorial(2 * k) for k in range(8)]
    s = jnp.full_like(z, coef_sin[-1])
    for v in coef_sin[-2::-1]:
        s = s * z + v
    s = s * part
    c = jnp.full_like(z, coef_cos[-1])
    for v in coef_cos[-2::-1]:
        c = c * z + v
    return 1.0 - 2.0 * s * s, 2.0 * s * c


def image_kernel(group, vis, uv, out):
    samples = vis.shape[2]
    position = lax.broadcasted_iota(jnp.int32, (PIX, samples), 0).astype(F32) * (1.0 / PIX)

    def step(g, carry):
        done = []
        for k in range(group):
            s = g * group + k
            uv_rows = uv[s]
            x_cos, x_sin = turn_waves(position * uv_rows[0:1])
            y_cos, y_sin = turn_waves(position * uv_rows[1:2])
            wave_x = jnp.concatenate([x_cos, x_sin], 0).astype(BF16)
            y_cos, y_sin = y_cos.astype(BF16).astype(F32), y_sin.astype(BF16).astype(F32)
            rows = vis[s].astype(F32)
            weight_re, weight_im = [], []
            for m in range(4):
                re, im = rows[m : m + 1], rows[m + 4 : m + 5]
                weight_re.append(re * y_cos - im * y_sin)
                weight_im.append(re * y_sin + im * y_cos)
            weighted = jnp.concatenate(weight_re + weight_im, 0).astype(BF16)
            products = lax.dot_general(
                wave_x, weighted, (((1,), (1,)), ((), ())), preferred_element_type=F32
            )
            low, high = products[:PIX], products[PIX:]
            done.append((s, low[:, :LANES] - high[:, LANES:], low[:, LANES:] + high[:, :LANES]))
        for s, re, im in done:
            out[s, 0:PIX] = re
            out[s, PIX:] = im
        return carry

    lax.fori_loop(0, vis.shape[0] // group, step, 0)


def adjoint_images(vis, uv, first, count):
    group = math.gcd(count, 4)
    at = first // count
    blocks = [pl.BlockSpec((count,) + x.shape[1:], lambda i: (at, 0, 0)) for x in (vis, uv)]
    return pl.pallas_call(
        lambda *refs: image_kernel(group, *refs),
        out_shape=jax.ShapeDtypeStruct((count, 2 * PIX, LANES), F32),
        grid=(1,),
        in_specs=blocks,
        out_specs=pl.BlockSpec((count, 2 * PIX, LANES), lambda i: (0, 0, 0)),
        name="image",
    )(vis, uv)


def table_rows(n_bt, n_freq, me, stations, slot_time):
    n_z = n_freq // 2
    my_z, my_core = me[0] >> 1, me[0] & 1

    def row(which, s):
        station = stations[which, s]
        bt, freq = lax.div(station, n_freq), lax.rem(station, n_freq)
        half = jnp.where((freq & 1) == my_core, 0, n_bt * n_z)
        ahead = lax.rem((freq >> 1) - my_z + n_z, n_z)
        return (half + ahead * n_bt + bt) * TSLOTS + slot_time[s]

    return row


def join_parts(parts, whole, sems, chunk):
    copies = []
    for part in parts:
        for c in range(0, part.shape[0], chunk):
            k = len(copies)
            at = pl.ds(k * chunk, chunk)
            copy = pltpu.make_async_copy(part.at[pl.ds(c, chunk)], whole.at[at], sems.at[k])
            copy.start()
            copies.append(copy)
    return copies


def join_rings(halves, table, sems):
    copies, at = [], 0
    for early, late in halves:
        block = (early.shape[0] + late.shape[0]) // 8
        for part, start, count in ((early, 0, 3), (late, 0, 3), (early, 3, 2)):
            copy = pltpu.make_async_copy(
                part.at[pl.ds(start * block, count * block)],
                table.at[pl.ds(at, count * block)],
                sems.at[len(copies)],
            )
            copy.start()
            copies.append(copy)
            at += count * block
    return copies


def screens_of(lines, spread):
    wide = dot(jnp.concatenate(lines, 0), spread[...])
    at = [slice(k * PIX, (k + 1) * PIX) for k in range(len(lines))]
    return [(wide[k, :LANES], wide[k, LANES:]) for k in at]


def left_side(left, pieces):
    count = pieces.shape[1] // LANES
    inner = dot(left[...], pieces).astype(BF16)
    return jnp.concatenate([inner[:, k * LANES : (k + 1) * LANES] for k in range(count)], 0)


def right_side(lines, right):
    outer = dot(lines, right[...])
    return [outer[k : k + 2 * PIX] for k in range(0, lines.shape[0], 2 * PIX)]


def solve_kernel(
    group, n_bt, n_freq, me, slot, stations, slot_time, image_a, image_b, image_c,
    near_a, near_b, far_a, far_b, patches, forward, backward, right, spread_a, spread_b,
    out, out_near, out_far,
    table, sems, image, image_sems, window, window_sems, stage, stage_sems,
    acc, sums, sum_sems, mids, backs,
):
    chunk = 32
    count = image.shape[0]
    groups = count // group
    copies = join_rings(((near_a, near_b), (far_a, far_b)), table, sems)
    images = join_parts((image_a, image_b, image_c), image, image_sems, count // 4)
    row = table_rows(n_bt, n_freq, me, stations, slot_time)
    block = lax.broadcasted_iota(jnp.int32, (PIX, LANES), 1) // PIX

    def window_copy(s):
        return pltpu.make_async_copy(patches.at[slot[s]], window.at[s], window_sems.at[s])

    def grad_copy(s):
        return pltpu.make_async_copy(stage.at[s], out.at[slot[s]], stage_sems.at[s])

    def each(step, first, last):
        def run(s, carry):
            step(s)
            return carry

        lax.fori_loop(first, last, run, 0)

    def clear(i):
        acc[pl.ds(i * chunk, chunk)] = jnp.zeros((chunk, PIX, LANES), F32)

    def ready(p):
        images[p].wait()
        each(lambda s: window_copy(s).wait(), p * count // 4, (p + 1) * count // 4)

    each(lambda s: window_copy(s).start(), 0, count)
    each(clear, 0, acc.shape[0] // chunk)
    for copy in copies:
        copy.wait()
    ready(0)

    def begin(g):
        pieces = [window[g * group + k] for k in range(group)]
        return left_side(forward, jnp.concatenate(pieces, 1))

    def both(g):
        subs = [g * group + k for k in range(group)]
        first_rows, second_rows = [[row(w, s) for s in subs] for w in (0, 1)]
        skies = right_side(mids[...], right)
        first_screens = screens_of([table[r] for r in first_rows], spread_a)
        second_screens = screens_of([table[r] for r in second_rows], spread_b)
        mid = begin(jnp.minimum(g + 1, groups - 1))
        pieces, terms = [], []
        for s, (a_re, a_im), (b_re, b_im), sky in zip(subs, first_screens, second_screens, skies):
            m_re, m_im = image[s, 0:PIX], image[s, PIX:]
            both_re = a_re * b_re + a_im * b_im
            both_im = a_re * b_im - a_im * b_re
            back_re = both_re * m_re - both_im * m_im
            back_im = both_re * m_im + both_im * m_re
            pieces.append(jnp.concatenate([back_re, back_im], 0).astype(BF16))
            re, im = sky[:PIX], sky[PIX:]
            sky_re = re[:, :LANES] - im[:, LANES:]
            sky_im = re[:, LANES:] + im[:, :LANES]
            carry_re = b_re * m_re - b_im * m_im
            carry_im = b_re * m_im + b_im * m_re
            ga_re = sky_re * carry_re + sky_im * carry_im
            ga_im = sky_re * carry_im - sky_im * carry_re
            model_re = a_re * sky_re - a_im * sky_im
            model_im = a_re * sky_im + a_im * sky_re
            gb_re = m_re * model_re + m_im * model_im
            gb_im = m_re * model_im - m_im * model_re
            ta = jnp.where(
                block % 2 == 0,
                ga_re + pltpu.roll(ga_re, LANES - PIX, 1),
                ga_im + pltpu.roll(ga_im, PIX, 1),
            )
            ta = jnp.where(
                block == 1,
                pltpu.roll(ta, LANES - PIX, 1),
                jnp.where(block == 2, pltpu.roll(ta, PIX, 1), ta),
            )
            tb = jnp.where(
                block < 2,
                gb_re + pltpu.roll(gb_re, 2 * PIX, 1),
                gb_im + pltpu.roll(gb_im, 2 * PIX, 1),
            )
            terms.append((ta, tb))
        mids[...] = mid
        for (ta, tb), first, second in zip(terms, first_rows, second_rows):
            acc[first] = acc[first] + ta
            acc[second] = acc[second] + tb
        return jnp.concatenate(pieces, 1)

    def gradients():
        grads = []
        for grad in right_side(left_side(backward, backs[...]), right):
            re, im = grad[:PIX], grad[PIX:]
            grad_re = re[:, :LANES] + im[:, LANES:]
            grad_im = im[:, :LANES] - re[:, LANES:]
            grads.append(jnp.concatenate([grad_re, grad_im], 0).astype(BF16))
        return grads

    def give(g, grads):
        for k, grad in enumerate(grads):
            stage[g * group + k] = grad
        for k in range(group):
            grad_copy(g * group + k).start()

    mids[...] = begin(0)
    backs[...] = both(0)

    def step(g):
        grads = gradients()
        back = both(g + 1)
        backs[...] = back
        give(g, grads)

    for p in range(4):
        if p + 1 < 4:
            ready(p + 1)
        each(step, p * groups // 4, min((p + 1) * groups // 4, groups - 1))
    give(groups - 1, gradients())
    sent = []
    half = out_far.shape[0]
    for start, to in ((half, out_far), (0, out_near)):
        for i in range(0, half, chunk):
            at = pl.ds(start + i, chunk)
            sums[at] = acc[at].astype(BF16)
            copy = pltpu.make_async_copy(sums.at[at], to.at[pl.ds(i, chunk)], sum_sems.at[len(sent)])
            copy.start()
            sent.append(copy)
    for copy in sent:
        copy.wait()
    each(lambda s: grad_copy(s).wait(), 0, count)


def solve(where, images, rings, patches, consts, n_bt, n_freq):
    count = 4 * images[-1].shape[0]
    group = math.gcd(count // 4, 4)
    half = rings[0].shape[0] + rings[1].shape[0]
    vmem, smem = pl.BlockSpec(memory_space=pltpu.VMEM), pl.BlockSpec(memory_space=pltpu.SMEM)
    anywhere = pl.BlockSpec(memory_space=pl.ANY)
    sums = jax.ShapeDtypeStruct((half, PIX, LANES), BF16)
    return pl.pallas_call(
        lambda *refs: solve_kernel(group, n_bt, n_freq, *refs),
        out_shape=(jax.ShapeDtypeStruct(patches.shape, BF16), sums, sums),
        in_specs=[smem] * 4 + [anywhere] * 8 + [vmem] * 5,
        out_specs=(anywhere,) * 3,
        scratch_shapes=[
            pltpu.VMEM((2 * half, PIX, LANES), BF16),
            pltpu.SemaphoreType.DMA((6,)),
            pltpu.VMEM((count, 2 * PIX, LANES), F32),
            pltpu.SemaphoreType.DMA((4,)),
            pltpu.VMEM((count, 2 * PIX, LANES), BF16),
            pltpu.SemaphoreType.DMA((count,)),
            pltpu.VMEM((count, 2 * PIX, LANES), BF16),
            pltpu.SemaphoreType.DMA((count,)),
            pltpu.VMEM((2 * half, PIX, LANES), F32),
            pltpu.VMEM((2 * half, PIX, LANES), BF16),
            pltpu.SemaphoreType.DMA((2 * half // 32,)),
            pltpu.VMEM((group * 2 * PIX, LANES), BF16),
            pltpu.VMEM((2 * PIX, group * LANES), BF16),
        ],
        name="solve",
        compiler_params=pltpu.CompilerParams(vmem_limit_bytes=44 << 20),
    )(*where, *images, *rings, patches, *consts)


def exchange(x, axis):
    return lax.all_to_all(x, axis, split_axis=0, concat_axis=0, tiled=True)


def z_shift(n_z, step):
    return [(2 * z + c, 2 * ((z + step) % n_z) + c) for z in range(n_z) for c in range(2)]


def ring_gather(x, n_z):
    half = n_z // 2
    blocks = [None] * n_z
    blocks[0] = up = down = x
    for k in range(1, half):
        up = lax.ppermute(up, "freq", z_shift(n_z, 1))
        down = lax.ppermute(down, "freq", z_shift(n_z, -1))
        blocks[n_z - k], blocks[k] = up, down
    cut = x.shape[0] // 2
    up = lax.ppermute(up[:cut], "freq", z_shift(n_z, 1))
    down = lax.ppermute(down[cut:], "freq", z_shift(n_z, -1))
    blocks[half] = jnp.concatenate([up, down])
    early = jnp.stack(blocks[:3] + blocks[6:])
    return early, jnp.stack(blocks[3:6])


def ring_sum(mine, came, n_z):
    half, cut = n_z // 2, mine.shape[1] // 2

    def block(k, at=slice(None)):
        return mine[k, at].astype(F32) + came[k, at].astype(F32)

    up, down = block(half, slice(0, cut)).astype(BF16), block(half, slice(cut, None)).astype(BF16)
    up = lax.ppermute(up, "freq", z_shift(n_z, 1))
    down = lax.ppermute(down, "freq", z_shift(n_z, -1))
    for k in range(half - 1, 0, -1):
        next_up, next_down = block(k), block(n_z - k)
        if k == half - 1:
            zeros = jnp.zeros_like(up)
            up, down = jnp.concatenate([up, zeros]), jnp.concatenate([zeros, down])
        next_up = (next_up + up.astype(F32)).astype(BF16)
        next_down = (next_down + down.astype(F32)).astype(BF16)
        up = lax.ppermute(next_up, "freq", z_shift(n_z, 1))
        down = lax.ppermute(next_down, "freq", z_shift(n_z, -1))
    return (block(0) + up.astype(F32) + down.astype(F32)).astype(BF16)


def per_device(
    uv_grid, screens, residual, uv_coords, owner_tile, row_offset, column, stations, time_slot
):
    n_bt, n_freq = lax.axis_size("bt"), lax.axis_size("freq")
    n_z = n_freq // 2
    slots = n_bt * CAP
    consts = constant_tables()
    swap = [(f, f ^ 1) for f in range(n_freq)]
    row = TSLOTS * PIX
    mail, slot = make_mail(
        owner_tile[0, :, 0], row_offset[0], column[0], screens[:, 0], n_bt
    )
    me = lax.axis_index("freq").astype(jnp.int32).reshape(1)
    where = (me, slot, stations[0].T, time_slot[0])
    quarter = residual.shape[1] // 4
    images = []
    for part, (begin, count) in enumerate(((0, 2), (2, 1), (3, 1))):
        images.append(adjoint_images(residual[0], uv_coords[0], begin * quarter, count * quarter))
    mail = exchange(mail, "bt")
    asked = mail[:, row].astype(jnp.int32)
    near = [x.reshape(-1, PIX, LANES) for x in ring_gather(mail[:, :row], n_z)]
    far_early = lax.ppermute(near[0], "freq", swap)
    far_late = lax.ppermute(near[1], "freq", swap)
    rings = (*near, far_early, far_late)
    cut = cut_windows(asked, uv_grid[0])
    fetched = exchange(cut.reshape(n_bt, CAP, 2 * PIX, LANES), "bt")
    fetched = fetched.reshape(slots, 2 * PIX, LANES)
    grads, terms, sent = solve(where, images, rings, fetched, consts, n_bt, n_freq)
    returned = exchange(grads.reshape(n_bt, CAP, 2 * PIX, LANES), "bt")
    returned = returned.reshape(slots, 2 * PIX, LANES)
    came = lax.ppermute(sent, "freq", swap)
    blocks = (n_z, n_bt, TSLOTS * PIX, LANES)
    part = ring_sum(terms.reshape(blocks), came.reshape(blocks), n_z)
    part = exchange(part, "bt")
    grid_grad = add_windows(asked, returned, *uv_grid.shape[1:])
    screen_grad = finish(part.reshape(n_bt, TSLOTS, PIX, LANES))
    return grid_grad[None], screen_grad[:, None]


def solution(mesh):
    in_specs = (
        P("freq", None, "bt", None),
        P(None, ("bt", "freq"), None, None),
        P("freq", "bt", None, None),
        P("freq", "bt", None, None),
        P("freq", "bt", None),
        P("freq", "bt"),
        P("freq", "bt"),
        P("freq", "bt", None),
        P("freq", "bt"),
    )
    out_specs = (P("freq", None, "bt", None), P(None, ("bt", "freq"), None, None))

    return jax.shard_map(
        per_device, mesh=mesh, in_specs=in_specs, out_specs=out_specs, check_vma=False
    )
```
